512 devices in a mesh: cfg: 2 (over y_hi), seq: 32 (over z, core), tp: 8 (over x, y_lo).
Axes of the slice: x: 4, y: 4 (y_hi: 2, y_lo: 2; y = y_hi * 2 + y_lo), z: 16, core: 2. Of those that a mesh axis runs over, the one named last changes fastest.
Arguments:
- stream: bfloat16 [2, 12288, 3072], P('cfg', 'seq', 'tp'), may hold values from -1.5 to 1.5
- qkv: bfloat16 [2, 12288, 3, 3072], P('cfg', 'seq', None, 'tp'), may hold values from -400 to 400
- q_gain: float32 [128], replicated, may hold values from 0.5 to 6
- k_gain: float32 [128], replicated, may hold values from 0.5 to 6
- w_out: bfloat16 [3072, 3072], P('tp'), may hold values from -0.109375 to 0.109375
- mod: float32 [2, 8, 3, 3072], P('cfg'), may hold values from -4 to 4
- w_proj: bfloat16 [64, 3072], replicated, may hold values from -0.109375 to 0.109375
- latent: float32 [6144, 128], P('seq'), may hold values from -6 to 6
- guidance: float32 [8], replicated, may hold values from 2 to 6
- img_counts: int32 [8], replicated, may hold values from 1 to 2816, 11264 in all
- img_widths: int32 [8], replicated, may hold values from 16 to 64
- step_index: int32 [8], replicated, may hold values from 0 to 7
Outputs:
- velocity: float32 [6144, 128], P('seq', 'cfg')
- next_latent: float32 [6144, 128], P('seq', 'cfg')
- top_logit: float32 [2, 24], P('cfg', 'tp')
The draws below stay inside these ranges and needn't reach their ends.
Inputs may be any that keep to these rules, and one draw needn't show every extreme that they name: Request r holds 128 text rows followed by img_counts[r] image rows; requests lie end to end in order and fill all 12288 rows; the counts sum to 11264 and the largest is exactly 2816.
All inputs are finite; a program needn't handle non-finite values.
Results may differ from the reference program's by a relative error of at most 0.017.
The reference program's roundings to bfloat16 on the way count: a program that leaves them out, or rounds other values in their place, can miss the bound.
Values may be sent and summed in bfloat16 or wider, within the bound.
A program may use at most 64 MiB of HBM per device.

```python
import math
import jax
import jax.numpy as jnp
import numpy as np
from jax import lax

HEADS = 24
HDIM = 128
CH = 64
NREQ = 8
TXT = 128
STEPS = 8
D = 3072
TOKENS = 12288
IMG_TOTAL = 11264
IMG_MOST = 2816
N_TP = 8


def draw_gain(key, salt):
    local_key = jax.random.fold_in(key, salt)
    gains = jax.random.uniform(local_key, (HDIM,), jnp.float32, 0.5, 1.5)
    return gains


def draw_q_gain(key, part):
    return draw_gain(key, 11)


def draw_k_gain(key, part):
    return draw_gain(key, 12)


def draw_qkv(key, part):
    key_base, key_row, key_wide, key_narrow = jax.random.split(jax.random.fold_in(key, 21), 4)
    shape_full = (2, TOKENS, 3, D)
    which_part = jnp.arange(3)[None, None, :, None]
    row_scale = jnp.exp(jax.random.uniform(key_row, (2, TOKENS, 3, 1), jnp.float32, 0.0, math.log(10.0)))
    row_scale = jnp.where(which_part == 2, 1.0, row_scale)
    col_wide = jnp.exp(jax.random.uniform(key_wide, (1, 1, 3, D), jnp.float32, 0.0, math.log(10.0)))
    col_narrow = jnp.exp(jax.random.uniform(key_narrow, (1, 1, 3, D), jnp.float32, math.log(0.5), math.log(2.0)))
    col_scale = jnp.where(which_part == 2, col_narrow, col_wide)
    base_values = jnp.clip(jax.random.normal(key_base, shape_full, jnp.float32), -4.0, 4.0)
    values = base_values * row_scale * col_scale
    return values.astype(jnp.bfloat16)


def plant(result, own_key, low, largest):
    longest = result.shape.index(max(result.shape))
    spots = []
    for shift in (0, 1):
        where = [jax.random.randint(jax.random.fold_in(own_key, axis), (), 0, length) for axis, length in enumerate(result.shape)]
        where[longest] = (where[longest] + shift) % result.shape[longest]
        spots.append(tuple(where))
    return result.at[spots[0]].set(low).at[spots[1]].set(largest)


def block_scale(rng, dims, cuts, smallest, high):
    level = 1.0
    for dim, blocks in cuts:
        heights = jax.random.uniform(jax.random.fold_in(jax.random.fold_in(rng, 6), dim), (blocks,), jnp.float32, smallest / len(cuts), high / len(cuts))
        level = level * jnp.repeat(jnp.exp(heights), dims[dim] // blocks).reshape((-1,) + (1,) * (len(dims) - 1 - dim))
    return level


def length_profile(count, total, reach, skew):
    loads = [(1 << 20) // math.isqrt(rank ** skew) + 1 for rank in range(2, count + 1)]
    spare, holding = total - reach - (count - 1), [1] * (count - 1)
    while spare > 0:
        free = [i for i in range(count - 1) if holding[i] < reach]
        mass, budget = sum([loads[i] for i in free]), spare
        for i in free:
            addition = min(reach - holding[i], max(1, budget * loads[i] // mass), spare)
            holding[i] = holding[i] + addition
            spare = spare - addition
    return np.array([reach] + holding)


def ragged(key, count, total, bound, slope):
    if count == 2:
        one = jax.random.randint(key, (), max(1, total - bound), min(bound, total - 1) + 1)
        return jnp.stack([one, total - one])
    sizes = jnp.asarray(length_profile(count, total, bound, slope), jnp.int32)
    couples = (count - 1) // 2
    giver, taker = sizes[1:1 + 2 * couples:2], sizes[2:2 + 2 * couples:2]
    slack = jnp.minimum(giver - 1, bound - taker)
    passed = jax.random.randint(jax.random.fold_in(key, 1), (couples,), 0, 1 << 20) % (slack + 1)
    sizes = sizes.at[1:1 + 2 * couples:2].set(giver - passed).at[2:2 + 2 * couples:2].set(taker + passed)
    return sizes[jax.random.permutation(jax.random.fold_in(key, 2), count)]


def normal_values(own_key, shape, width, bound, pieces=(), kind=jnp.bfloat16):
    values = width * jax.random.normal(own_key, shape, jnp.float32)
    if pieces:
        values = values * block_scale(own_key, shape, pieces, -0.22, 0.18)
    return jnp.clip(values, -bound, bound).astype(kind)


def setup_inputs(seed: int = 0) -> dict:
    keys = jax.random.split(jax.random.key(seed), 13)
    stream = normal_values(keys[0], (2, TOKENS, D), 0.25, 1.5, ((0, 2), (1, 32), (2, 8)))
    qkv = draw_qkv(jax.random.fold_in(keys[12], 71), 0)
    q_gain = draw_q_gain(jax.random.fold_in(keys[12], 71), 0)
    k_gain = draw_k_gain(jax.random.fold_in(keys[12], 71), 0)
    w_out = normal_values(keys[4], (D, D), D ** -0.5, 0.109375, ((0, 8),))
    mod = normal_values(keys[5], (2, NREQ, 3, D), 1.0, 4.0, ((0, 2),), jnp.float32)
    w_proj = normal_values(keys[6], (CH, D), D ** -0.5, 0.109375)
    latent = normal_values(keys[7], (TOKENS // 2, 2 * CH), 1.0, 6.0, ((0, 32),), jnp.float32)
    guidance = jnp.clip(jax.random.uniform(keys[8], (NREQ,), jnp.float32, 2.0, 6.0), 2.0, 6.0)
    img_counts = ragged(keys[9], NREQ, IMG_TOTAL, IMG_MOST, 2).astype(jnp.int32)
    img_widths = plant(jax.random.randint(keys[10], (NREQ,), 16, 65), jax.random.fold_in(keys[10], 1), 16, 64).astype(jnp.int32)
    step_index = plant(jax.random.randint(keys[11], (NREQ,), 0, STEPS), jax.random.fold_in(keys[11], 1), 0, STEPS - 1).astype(jnp.int32)
    return {"stream": stream, "qkv": qkv, "q_gain": q_gain, "k_gain": k_gain, "w_out": w_out, "mod": mod, "w_proj": w_proj, "latent": latent, "guidance": guidance, "img_counts": img_counts, "img_widths": img_widths, "step_index": step_index}


PHI_MIX = 0.7

def rope_tables():
    pair_index = np.arange(64)
    axis_of = np.where(pair_index < 8, 0, np.where(pair_index < 36, 1, 2))
    axis_start = np.array([0, 8, 36])[axis_of]
    axis_width = np.array([16.0, 56.0, 56.0])[axis_of]
    frequency = 10000.0 ** (-2.0 * (pair_index - axis_start) / axis_width)
    return (np.repeat(axis_of, 2), np.repeat(frequency, 2))

def row_layout(first_row, row_count, img_counts):
    lengths = TXT + img_counts
    row_ends = jnp.cumsum(lengths).astype(jnp.int32)
    starts = row_ends - lengths
    row_ids = first_row + jnp.arange(row_count, dtype=jnp.int32)
    request = lax.optimization_barrier(jnp.sum((row_ids[:, None] >= row_ends[None, :]).astype(jnp.int32), axis=1))
    request_hot = request[:, None] == jnp.arange(img_counts.shape[0], dtype=jnp.int32)[None, :]
    start_row = lax.optimization_barrier(jnp.sum(jnp.where(request_hot, starts[None, :], 0), axis=1))
    local_row = row_ids - start_row
    is_image = local_row >= TXT
    image_pos = jnp.maximum(local_row - TXT, 0)
    return (request, request_hot, is_image, image_pos)

def rope_angles(is_image, image_pos, request_hot, img_widths):
    axis_of, frequency = rope_tables()
    width_row = lax.optimization_barrier(jnp.sum(jnp.where(request_hot, img_widths[None, :], 0), axis=1))
    width_row = jnp.maximum(width_row, 1)
    id_height = jnp.where(is_image, image_pos // width_row, 0)
    id_width = jnp.where(is_image, image_pos % width_row, 0)
    on_height = jnp.asarray(axis_of == 1)[None, :]
    on_width = jnp.asarray(axis_of == 2)[None, :]
    position = jnp.where(on_height, id_height[:, None], jnp.where(on_width, id_width[:, None], 0))
    angles = position.astype(jnp.float32) * jnp.asarray(frequency, jnp.float32)[None, :]
    return (jnp.cos(angles)[:, None, :], jnp.sin(angles)[:, None, :])

def head_norm(values, gain):
    mean_square = lax.optimization_barrier(jnp.mean(values * values, axis=-1, keepdims=True))
    return values * lax.rsqrt(mean_square + 1e-06) * gain

def rotary(values, angle_cos, angle_sin):
    channel = jnp.arange(values.shape[-1], dtype=jnp.int32)
    is_even = channel % 2 == 0
    partner = jnp.where(is_even, -jnp.roll(values, -1, axis=-1), jnp.roll(values, 1, axis=-1))
    return values * angle_cos + partner * angle_sin

def pick_rows(hot_float, table):
    return jnp.dot(hot_float, table, precision=lax.Precision.HIGHEST, preferred_element_type=jnp.float32)

def spread_rows(token_values, row_count):
    return jnp.broadcast_to(token_values[:, None], (row_count, CH)).reshape(row_count // 2, 2 * CH)

def sigma_at(step_value):
    remaining = 1.0 - step_value / STEPS
    return 3.0 * remaining / (1.0 + 2.0 * remaining)

def reference(stream, qkv, q_gain, k_gain, w_out, mod, w_proj, latent, guidance, img_counts, img_widths, step_index):
    request, request_hot, is_image, image_pos = row_layout(0, TOKENS, img_counts)
    angle_cos, angle_sin = rope_angles(is_image, image_pos, request_hot, img_widths)
    hot_float = request_hot.astype(jnp.float32)
    block_rows = math.gcd(TOKENS, 256)
    scale_root = math.sqrt(float(HDIM))
    group_cols = D // N_TP
    flows = []
    group_tops = []
    for group_index in range(2):
        query = head_norm(qkv[group_index, :, 0].astype(jnp.float32).reshape(TOKENS, HEADS, HDIM), q_gain)
        query = rotary(query, angle_cos, angle_sin).astype(jnp.bfloat16)
        key_rows = head_norm(qkv[group_index, :, 1].astype(jnp.float32).reshape(TOKENS, HEADS, HDIM), k_gain)
        key_rows = rotary(key_rows, angle_cos, angle_sin).astype(jnp.bfloat16)
        value_rows = qkv[group_index, :, 2].reshape(TOKENS, HEADS, HDIM)

        def one_block(block_index):
            row_start = (block_index * block_rows).astype(jnp.int32)
            query_block = lax.dynamic_slice_in_dim(query, row_start, block_rows, 0)
            request_block = lax.dynamic_slice_in_dim(request, row_start, block_rows, 0)
            scores = jnp.einsum('qhd,khd->hqk', query_block.astype(jnp.float32), key_rows.astype(jnp.float32), precision=lax.Precision.HIGHEST) / scale_root
            same_request = request_block[:, None] == request[None, :]
            scores = jnp.where(same_request[None], scores, -jnp.inf)
            row_max = lax.optimization_barrier(jnp.max(scores, axis=-1, keepdims=True))
            weights = jnp.exp(scores - row_max)
            row_total = lax.optimization_barrier(jnp.sum(weights, axis=-1))
            rounded = lax.optimization_barrier(weights.astype(jnp.bfloat16))
            summed = jnp.einsum('hqk,khd->qhd', rounded.astype(jnp.float32), value_rows.astype(jnp.float32), precision=lax.Precision.HIGHEST)
            attended_block = (summed / row_total.T[:, :, None]).astype(jnp.bfloat16)
            return (attended_block, lax.optimization_barrier(jnp.max(scores, axis=(1, 2))))
        block_ids = jnp.arange(TOKENS // block_rows, dtype=jnp.int32)
        attended, block_tops = lax.map(one_block, block_ids)
        attended = attended.reshape(TOKENS, D)
        group_tops.append(lax.optimization_barrier(jnp.max(block_tops, axis=0)))
        projected = jnp.zeros((TOKENS, D), jnp.float32)
        for tp_slot in range(N_TP):
            piece = jnp.dot(attended[:, tp_slot * group_cols:(tp_slot + 1) * group_cols], w_out[tp_slot * group_cols:(tp_slot + 1) * group_cols], preferred_element_type=jnp.float32)
            piece = lax.optimization_barrier(piece.astype(jnp.bfloat16))
            projected = projected + piece.astype(jnp.float32)
        gate = pick_rows(hot_float, mod[group_index, :, 0])
        scale_row = pick_rows(hot_float, mod[group_index, :, 1])
        shift_row = pick_rows(hot_float, mod[group_index, :, 2])
        mixed = stream[group_index].astype(jnp.float32) + gate * projected
        centred = mixed - lax.optimization_barrier(jnp.mean(mixed, axis=1, keepdims=True))
        variance = lax.optimization_barrier(jnp.mean(centred * centred, axis=1, keepdims=True))
        normed = (centred * lax.rsqrt(variance + 1e-06) * (1.0 + scale_row) + shift_row).astype(jnp.bfloat16)
        flow = jnp.dot(normed, w_proj.T, preferred_element_type=jnp.float32)
        flows.append(flow.reshape(TOKENS // 2, 2 * CH))
    cond_vel = flows[0]
    uncond_vel = flows[1]
    guide_row = lax.optimization_barrier(jnp.sum(hot_float * guidance[None, :], axis=1))
    guided = uncond_vel + spread_rows(guide_row, TOKENS) * (cond_vel - uncond_vel)
    image_mask = is_image.astype(jnp.float32)
    cond_square = lax.optimization_barrier(jnp.sum((cond_vel * cond_vel).reshape(TOKENS, CH), axis=1)) * image_mask
    guided_square = lax.optimization_barrier(jnp.sum((guided * guided).reshape(TOKENS, CH), axis=1)) * image_mask
    cond_total = lax.optimization_barrier(jnp.sum(hot_float * cond_square[:, None], axis=0))
    guided_total = lax.optimization_barrier(jnp.sum(hot_float * guided_square[:, None], axis=0))
    entries = img_counts.astype(jnp.float32) * CH
    factor = (PHI_MIX * jnp.sqrt(cond_total / entries + 1e-06) + (1.0 - PHI_MIX)) / jnp.sqrt(guided_total / entries + 1e-06)
    factor_row = lax.optimization_barrier(jnp.sum(hot_float * factor[None, :], axis=1)) * image_mask
    velocity = guided * spread_rows(factor_row, TOKENS)
    step_float = step_index.astype(jnp.float32)
    delta = sigma_at(step_float + 1.0) - sigma_at(step_float)
    delta_row = lax.optimization_barrier(jnp.sum(hot_float * delta[None, :], axis=1))
    next_latent = latent + spread_rows(delta_row, TOKENS) * velocity
    return (velocity, next_latent, jnp.stack(group_tops))
```

```python
import functools
import math

import jax
import jax.numpy as jnp
import numpy as np
from jax import lax
from jax.experimental import pallas as pl
from jax.experimental.pallas import tpu as pltpu
from jax.sharding import PartitionSpec as P

MESH = pl.DeviceIdType.MESH
HDIM = 128
CH = 64
TXT = 128
STEPS = 8
NREQ = 8
PHI_MIX = 0.7
NEG = -1e30
SCALE = 1.0 / math.sqrt(float(HDIM))
EXP2_SCALE = SCALE * math.log2(math.e)
F32 = jnp.float32
BF16 = jnp.bfloat16


def frequency_row():
    pair_index = np.arange(64)
    axis_of = np.where(pair_index < 8, 0, np.where(pair_index < 36, 1, 2))
    axis_start = np.array([0, 8, 36])[axis_of]
    axis_width = np.array([16.0, 56.0, 56.0])[axis_of]
    frequency = 10000.0 ** (-2.0 * (pair_index - axis_start) / axis_width)
    return np.repeat(frequency, 2).astype(np.float32)[None, :]


def request_ends(counts):
    ends = []
    end = jnp.int32(0)
    for r in range(NREQ):
        end = end + (TXT + counts[r])
        ends.append(end)
    return ends


def pick(rows, ends, values):
    out = jnp.full(rows.shape, values[0])
    for r in range(NREQ - 1):
        out = jnp.where(rows >= ends[r], values[r + 1], out)
    return out


def prep_kernel(counts, widths, qkv_ref, freq_ref, qg_ref, kg_ref, q_ref, kv_ref, reqq_ref, reqk_ref):
    rows, heads = qkv_ref.shape[1], q_ref.shape[0]
    ends = request_ends(counts)
    starts = [jnp.int32(0)] + ends[:-1]
    row = lax.axis_index("seq") * rows + lax.broadcasted_iota(jnp.int32, (rows, HDIM), 0)
    ids = [jnp.int32(r) for r in range(NREQ)]
    reqq_ref[...] = pick(row, ends, ids)
    blocks = reqk_ref.shape[0]
    every = lax.broadcasted_iota(jnp.int32, (blocks, rows), 0) * rows + lax.broadcasted_iota(jnp.int32, (blocks, rows), 1)
    reqk_ref[...] = pick(every, ends, ids)
    start = pick(row, ends, starts)
    width = pick(row, ends, [widths[r].astype(F32) for r in range(NREQ)])
    pos = jnp.maximum(row - start - TXT, 0).astype(F32)
    height_id = jnp.floor((pos + 0.5) / width)
    width_id = pos - height_id * width
    lane = lax.broadcasted_iota(jnp.int32, (rows, HDIM), 1)
    position = jnp.where(lane < 16, 0.0, jnp.where(lane < 72, height_id, width_id))
    angle = position * freq_ref[...]
    cos = jnp.cos(angle)
    even = lane % 2 == 0
    sin = jnp.sin(angle)
    sin = jnp.where(even, -sin, sin)

    def rotated(part, h, gain):
        x = qkv_ref[part, :, h * HDIM : (h + 1) * HDIM].astype(F32)
        x = x * lax.rsqrt(jnp.mean(x * x, axis=-1, keepdims=True) + 1e-06) * gain
        partner = jnp.where(even, pltpu.roll(x, HDIM - 1, 1), pltpu.roll(x, 1, 1))
        return x * cos + partner * sin

    for h in range(heads):
        key = rotated(1, h, kg_ref[...])
        for b in range(rows // HDIM):
            span = slice(b * HDIM, (b + 1) * HDIM)
            kv_ref[h, 0, span, :] = key[span].T.astype(BF16)
        kv_ref[h, 1] = qkv_ref[2, :, h * HDIM : (h + 1) * HDIM]
        q_ref[h] = rotated(0, h, qg_ref[...]).astype(BF16)


def attend_kernel(
    q_ref, kv_ref, reqq_ref, reqk_ref, att_ref, top_ref,
    win, m_s, l_s, acc_s, right_sem, left_sem, share_sem, recv_sem,
):
    heads, rows = q_ref.shape[0], q_ref.shape[1]
    reach = win.shape[0] // 2
    me = lax.axis_index("seq")
    count = lax.axis_size("seq")
    chips = count // 2
    chip, core = me // 2, me % 2
    other = 1 - core
    right = ((chip + 1) % chips) * 2 + core
    left = ((chip + chips - 1) % chips) * 2 + core
    partner = chip * 2 + other

    barrier = pltpu.get_barrier_semaphore()
    for peer in (left, right, partner):
        pl.semaphore_signal(barrier, inc=1, device_id={"seq": peer}, device_id_type=MESH)
    pl.semaphore_wait(barrier, 3)

    def remote(src, dst, send, recv, peer):
        return pltpu.make_async_remote_copy(
            src_ref=src, dst_ref=dst, send_sem=send, recv_sem=recv,
            device_id={"seq": peer}, device_id_type=MESH,
        )

    def slot(dz, p, h):
        return win.at[dz + reach, p, h]

    def go_right(d, h, src):
        return remote(src, slot(-d, core, h), right_sem.at[d - 1, h], recv_sem.at[reach - d, core, h], right)

    def go_left(d, h, src):
        return remote(src, slot(d, core, h), left_sem.at[d - 1, h], recv_sem.at[reach + d, core, h], left)

    def share(dz, h, src):
        return remote(src, slot(dz, core, h), share_sem.at[dz + reach, h], recv_sem.at[dz + reach, core, h], partner)

    def landed(dz, p, h):
        remote(slot(dz, p, h), slot(dz, p, h), share_sem.at[0, 0], recv_sem.at[dz + reach, p, h], partner).wait_recv()

    for h in range(heads):
        go_right(1, h, kv_ref.at[h]).start()
        go_left(1, h, kv_ref.at[h]).start()
        share(0, h, kv_ref.at[h]).start()

    tiles = rows // HDIM

    def wide(x):
        return jnp.concatenate([x] * tiles, axis=1)

    def update(h, pieces):
        q = q_ref[h]
        asked = wide(reqq_ref[...])
        scores = []
        for ref, source in pieces:
            keys = jnp.concatenate([ref[0, b * HDIM : (b + 1) * HDIM, :] for b in range(tiles)], axis=1)
            s = jnp.dot(q, keys, preferred_element_type=F32)
            scores.append(jnp.where(asked == reqk_ref[pl.ds(source, 1), :], s, NEG))
        best = functools.reduce(jnp.maximum, scores)
        m_old = m_s[h]
        m_new = jnp.maximum(m_old, jnp.max(best, axis=1, keepdims=True))
        shrink = jnp.exp2((m_old - m_new) * EXP2_SCALE)
        m_wide = wide(m_new)
        total = None
        acc = acc_s[h] * shrink
        for (ref, source), s in zip(pieces, scores):
            p = jnp.exp2((s - m_wide) * EXP2_SCALE)
            total = p if total is None else total + p
            acc = acc + jnp.dot(p.astype(BF16), ref[1], preferred_element_type=F32)
        l_s[h] = l_s[h] * shrink + jnp.sum(total, axis=1, keepdims=True)
        acc_s[h] = acc
        m_s[h] = m_new

    def block_of(dz, p):
        return ((chip + dz + chips) % chips) * 2 + p

    def own(h, carry):
        m_s[h] = jnp.full((rows, HDIM), NEG, F32)
        l_s[h] = jnp.zeros((rows, HDIM), F32)
        acc_s[h] = jnp.zeros((rows, HDIM), F32)
        update(h, [(kv_ref.at[h], me)])
        return carry

    lax.fori_loop(0, heads, own, 0)

    def pair(d, p, h):
        return [(slot(-d, p, h), block_of(-d, p)), (slot(d, p, h), block_of(d, p))]

    def receive(d, h, last):
        landed(-d, core, h)
        if not last:
            go_right(d + 1, h, slot(-d, core, h)).start()
        landed(d, core, h)
        if not last:
            go_left(d + 1, h, slot(d, core, h)).start()
            share(-d, h, slot(-d, core, h)).start()
            share(d, h, slot(d, core, h)).start()

    def first(h, carry):
        receive(1, h, False)
        update(h, pair(1, core, h))
        landed(0, other, h)
        update(h, [(slot(0, other, h), partner)])
        return carry

    lax.fori_loop(0, heads, first, 0)

    def middle(t, carry):
        d = 2 + t // heads
        h = t % heads
        receive(d, h, False)
        update(h, pair(d, core, h))
        landed(1 - d, other, h)
        landed(d - 1, other, h)
        update(h, pair(d - 1, other, h))
        return carry

    lax.fori_loop(0, heads * (reach - 2), middle, 0)

    give = reach - 2 * reach * core
    take = -give

    def last(h, carry):
        landed(1 - reach, other, h)
        landed(reach - 1, other, h)
        update(h, pair(reach - 1, other, h))
        receive(reach, h, True)
        share(give, h, slot(give, core, h)).start()
        update(h, pair(reach, core, h))
        return carry

    lax.fori_loop(0, heads, last, 0)

    def ending(h, carry):
        landed(take, other, h)
        update(h, [(slot(take, other, h), block_of(take, other))])
        return carry

    lax.fori_loop(0, heads, ending, 0)

    lane = lax.broadcasted_iota(jnp.int32, (8, HDIM), 1)
    tops = jnp.zeros((8, HDIM), F32)
    for h in range(heads):
        att_ref[:, h * HDIM : (h + 1) * HDIM] = (acc_s[h] / l_s[h]).astype(BF16)
        top = jnp.max(jnp.max(m_s[h], axis=0, keepdims=True), axis=1, keepdims=True) * SCALE
        tops = jnp.where(lane == 2 * NREQ + h, top, tops)
    top_ref[...] = tops

    def drain(h, carry):
        for d in range(1, reach + 1):
            go_right(d, h, kv_ref.at[h]).wait_send()
            go_left(d, h, kv_ref.at[h]).wait_send()
        for dz in range(1 - reach, reach):
            share(dz, h, kv_ref.at[h]).wait_send()
        share(give, h, kv_ref.at[h]).wait_send()
        return carry

    lax.fori_loop(0, heads, drain, 0)


def finish_kernel(
    counts, steps, guidance, att_ref, w_ref, stream_ref, mod_ref, proj_ref, latent_ref, top_ref,
    vel_ref, next_ref, tops_ref,
    part, got, res, mixed, gate, scale, shift, flow_s, mine, flows, row_s, sums,
    part_send, part_recv, res_send, res_recv, flow_send, flow_recv, sum_send, sum_recv,
):
    n_tp, n_seq, n_cfg = lax.axis_size("tp"), lax.axis_size("seq"), lax.axis_size("cfg")
    group, me, col = lax.axis_index("cfg"), lax.axis_index("seq"), lax.axis_index("tp")
    rows, width = stream_ref.shape
    feats = w_ref.shape[1]
    piece = rows // n_tp
    barrier = pltpu.get_barrier_semaphore()

    def tp_peer(k):
        return (col + k) % n_tp

    def plane_peer(k):
        return (group + k // n_tp) % n_cfg, (col + k) % n_tp

    def seq_peer(k):
        return (me + k) % n_seq

    def hail_plane(k, carry):
        g, c = plane_peer(k)
        pl.semaphore_signal(barrier, inc=1, device_id={"cfg": g, "tp": c}, device_id_type=MESH)
        return carry

    lax.fori_loop(1, n_tp * n_cfg, hail_plane, 0)

    def hail_seq(k, carry):
        pl.semaphore_signal(barrier, inc=1, device_id={"seq": seq_peer(k)}, device_id_type=MESH)
        return carry

    lax.fori_loop(1, n_seq, hail_seq, 0)

    att = att_ref[...]
    chunk = 512

    def project(j, carry):
        at = pl.ds(pl.multiple_of(j * chunk, chunk), chunk)
        out = jnp.dot(att, w_ref[:, at], preferred_element_type=F32).astype(BF16)
        for k in range(n_tp):
            part[k, :, at] = out[k * piece : (k + 1) * piece]
        return carry

    lax.fori_loop(0, feats // chunk, project, 0)

    ends = request_ends(counts)
    token = me * rows + col * piece + lax.broadcasted_iota(jnp.int32, (piece, chunk), 0)

    def pick_rows(j, carry):
        at = pl.ds(pl.multiple_of(j * chunk, chunk), chunk)
        for which, out in ((0, gate), (1, scale), (2, shift)):
            value = jnp.broadcast_to(mod_ref[which, 0:1, at], (piece, chunk))
            for r in range(NREQ - 1):
                value = jnp.where(token >= ends[r], mod_ref[which, r + 1 : r + 2, at], value)
            out[:, at] = value
        return carry

    lax.fori_loop(0, feats // chunk, pick_rows, 0)

    pl.semaphore_wait(barrier, n_tp * n_cfg - 1 + n_seq - 1)

    def res_copy(k, dest_slot):
        c = tp_peer(k)
        return pltpu.make_async_remote_copy(
            src_ref=stream_ref.at[pl.ds(c * piece, piece)], dst_ref=res.at[dest_slot],
            send_sem=res_send.at[k], recv_sem=res_recv.at[dest_slot],
            device_id={"tp": c}, device_id_type=MESH,
        )

    def part_copy(k, dest_slot):
        c = tp_peer(k)
        return pltpu.make_async_remote_copy(
            src_ref=part.at[c], dst_ref=got.at[dest_slot],
            send_sem=part_send.at[k], recv_sem=part_recv.at[dest_slot],
            device_id={"tp": c}, device_id_type=MESH,
        )

    def give_tp(k, carry):
        res_copy(k, col).start()
        part_copy(k, col).start()
        return carry

    lax.fori_loop(1, n_tp, give_tp, 0)
    got[col] = part[col]
    res[col] = stream_ref[pl.ds(pl.multiple_of(col * piece, piece), piece), :]

    def take_tp(k, carry):
        res_copy(k, tp_peer(k)).wait_recv()
        part_copy(k, tp_peer(k)).wait_recv()
        return carry

    lax.fori_loop(1, n_tp, take_tp, 0)

    mean = jnp.zeros((piece, 1), F32)
    for j in range(n_tp):
        at = slice(j * width, (j + 1) * width)
        total = got[0, :, at].astype(F32)
        for k in range(1, n_tp):
            total = total + got[k, :, at].astype(F32)
        value = res[j].astype(F32) + gate[:, at] * total
        mixed[:, at] = value
        mean = mean + jnp.sum(value, axis=1, keepdims=True)
    mean = mean * (1.0 / feats)
    variance = jnp.zeros((piece, 1), F32)
    for j in range(n_tp):
        at = slice(j * width, (j + 1) * width)
        centred = mixed[:, at] - mean
        mixed[:, at] = centred
        variance = variance + jnp.sum(centred * centred, axis=1, keepdims=True)
    inverse = lax.rsqrt(variance * (1.0 / feats) + 1e-06)
    flow = jnp.zeros((piece, HDIM), F32)
    for j in range(n_tp):
        at = slice(j * width, (j + 1) * width)
        normed = (mixed[:, at] * inverse * (1.0 + scale[:, at]) + shift[:, at]).astype(BF16)
        flow = flow + lax.dot_general(
            normed, proj_ref[:, at], (((1,), (1,)), ((), ())), preferred_element_type=F32
        )
    flow_s[...] = flow
    even = flow_s[pl.ds(0, piece // 2, stride=2), :]
    odd = flow_s[pl.ds(1, piece // 2, stride=2), :]
    own_flow = even + pltpu.roll(odd, CH, 1)
    mine[...] = own_flow
    flows[group, col] = own_flow

    def flow_copy(k, g_slot, c_slot):
        g, c = plane_peer(k)
        return pltpu.make_async_remote_copy(
            src_ref=mine, dst_ref=flows.at[g_slot, c_slot],
            send_sem=flow_send.at[k], recv_sem=flow_recv.at[g_slot, c_slot],
            device_id={"cfg": g, "tp": c}, device_id_type=MESH,
        )

    def give_flow(k, carry):
        flow_copy(k, group, col).start()
        return carry

    lax.fori_loop(1, n_tp * n_cfg, give_flow, 0)

    pairs = rows // 2
    lane2 = lax.broadcasted_iota(jnp.int32, (pairs, HDIM), 1)
    row2 = me * rows + 2 * lax.broadcasted_iota(jnp.int32, (pairs, HDIM), 0) + (lane2 >= CH).astype(jnp.int32)
    request = pick(row2, ends, [jnp.int32(r) for r in range(NREQ)])
    image = (row2 - pick(row2, ends, [jnp.int32(0)] + ends[:-1])) >= TXT
    guide = pick(row2, ends, [guidance[r] for r in range(NREQ)])
    step = pick(row2, ends, [steps[r].astype(F32) for r in range(NREQ)])

    def sigma(u):
        remaining = 1.0 - u / STEPS
        return 3.0 * remaining / (1.0 + 2.0 * remaining)

    delta = sigma(step + 1.0) - sigma(step)

    def take_flow(k, carry):
        g, c = plane_peer(k)
        flow_copy(k, g, c).wait_recv()
        return carry

    lax.fori_loop(1, n_tp * n_cfg, take_flow, 0)

    cond = flows[0].reshape(pairs, HDIM)
    uncond = flows[1].reshape(pairs, HDIM)
    guided = uncond + guide * (cond - uncond)
    cond_square = jnp.where(image, cond * cond, 0.0)
    guided_square = jnp.where(image, guided * guided, 0.0)
    parts = []
    for square in (cond_square, guided_square):
        for r in range(NREQ):
            parts.append(jnp.sum(jnp.where(request == r, square, 0.0), axis=0, keepdims=True))
    stacked = jnp.sum(jnp.concatenate(parts, axis=0), axis=1, keepdims=True)
    diagonal = lax.broadcasted_iota(jnp.int32, (2 * NREQ, HDIM), 0) == lax.broadcasted_iota(jnp.int32, (2 * NREQ, HDIM), 1)
    own_sums = jnp.sum(jnp.where(diagonal, stacked, 0.0), axis=0, keepdims=True) + top_ref[0:1, :]
    row_s[...] = own_sums
    sums[me] = own_sums

    def sum_copy(k, dest_slot):
        return pltpu.make_async_remote_copy(
            src_ref=row_s, dst_ref=sums.at[dest_slot],
            send_sem=sum_send.at[k], recv_sem=sum_recv.at[dest_slot],
            device_id={"seq": seq_peer(k)}, device_id_type=MESH,
        )

    def give_sum(k, carry):
        sum_copy(k, me).start()
        return carry

    lax.fori_loop(1, n_seq, give_sum, 0)

    def take_sum(k, carry):
        sum_copy(k, seq_peer(k)).wait_recv()
        return carry

    lax.fori_loop(1, n_seq, take_sum, 0)

    total = sums[0]
    top = sums[0]
    for k in range(1, n_seq):
        total = total + sums[k]
        top = jnp.maximum(top, sums[k])
    tops_ref[...] = top
    lane1 = lax.broadcasted_iota(jnp.int32, (1, HDIM), 1)
    entries = jnp.ones((1, HDIM), F32)
    for r in range(NREQ):
        entries = jnp.where(lane1 == r, counts[r].astype(F32) * CH, entries)
    guided_total = pltpu.roll(total, HDIM - NREQ, 1)
    factor = (PHI_MIX * jnp.sqrt(total / entries + 1e-06) + (1.0 - PHI_MIX)) / jnp.sqrt(guided_total / entries + 1e-06)
    factor_row = jnp.zeros((pairs, HDIM), F32)
    for r in range(NREQ):
        one = jnp.sum(jnp.where(lane1 == r, factor, 0.0), axis=1, keepdims=True)
        factor_row = jnp.where(request == r, one, factor_row)
    velocity = guided * jnp.where(image, factor_row, 0.0)
    stepped = latent_ref[...] + delta * velocity
    vel_ref[...] = jnp.where(group == 0, velocity, pltpu.roll(velocity, CH, 1))
    next_ref[...] = jnp.where(group == 0, stepped, pltpu.roll(stepped, CH, 1))

    def drain_tp(k, carry):
        res_copy(k, col).wait_send()
        part_copy(k, col).wait_send()
        return carry

    lax.fori_loop(1, n_tp, drain_tp, 0)

    def drain_flow(k, carry):
        flow_copy(k, group, col).wait_send()
        return carry

    lax.fori_loop(1, n_tp * n_cfg, drain_flow, 0)

    def drain_sum(k, carry):
        sum_copy(k, me).wait_send()
        return carry

    lax.fori_loop(1, n_seq, drain_sum, 0)


def local(stream, qkv, q_gain, k_gain, w_out, mod, w_proj, latent, guidance, img_counts, img_widths, step_index):
    rows, width = stream.shape[1], stream.shape[2]
    feats = w_out.shape[1]
    heads = width // HDIM
    n_seq, n_tp, n_cfg = lax.axis_size("seq"), lax.axis_size("tp"), lax.axis_size("cfg")
    piece = rows // n_tp
    img_most = (rows * n_seq - NREQ * TXT) // 4
    reach = ((TXT + img_most + rows - 2) // rows + 1) // 2
    smem = pl.BlockSpec(memory_space=pltpu.SMEM)
    vmem = pl.BlockSpec(memory_space=pltpu.VMEM)
    dma = pltpu.SemaphoreType.DMA

    q, kv, reqq, reqk = pl.pallas_call(
        prep_kernel,
        out_shape=(
            jax.ShapeDtypeStruct((heads, rows, HDIM), BF16),
            jax.ShapeDtypeStruct((heads, 2, rows, HDIM), BF16),
            jax.ShapeDtypeStruct((rows, HDIM), jnp.int32),
            jax.ShapeDtypeStruct((n_seq, rows), jnp.int32),
        ),
        in_specs=[smem] * 2 + [vmem] * 4,
        out_specs=(vmem,) * 4,
        name="prep",
    )(
        img_counts, img_widths, jnp.transpose(qkv[0], (1, 0, 2)), jnp.asarray(frequency_row()),
        q_gain.reshape(1, HDIM), k_gain.reshape(1, HDIM),
    )

    att, top = pl.pallas_call(
        attend_kernel,
        out_shape=(
            jax.ShapeDtypeStruct((rows, width), BF16),
            jax.ShapeDtypeStruct((8, HDIM), F32),
        ),
        in_specs=[vmem] * 4,
        out_specs=(vmem,) * 2,
        scratch_shapes=[
            pltpu.VMEM((2 * reach + 1, 2, heads, 2, rows, HDIM), BF16),
            pltpu.VMEM((heads, rows, HDIM), F32),
            pltpu.VMEM((heads, rows, HDIM), F32),
            pltpu.VMEM((heads, rows, HDIM), F32),
            dma((reach, heads)),
            dma((reach, heads)),
            dma((2 * reach + 1, heads)),
            dma((2 * reach + 1, 2, heads)),
        ],
        compiler_params=pltpu.CompilerParams(collective_id=0, has_side_effects=True, vmem_limit_bytes=40 << 20),
        name="attend",
    )(q, kv, reqq, reqk)

    proj = jnp.pad(w_proj, ((0, HDIM - CH), (0, 0)))
    pairs = rows // 2
    vel, nxt, tops = pl.pallas_call(
        finish_kernel,
        out_shape=(
            jax.ShapeDtypeStruct((pairs, HDIM), F32),
            jax.ShapeDtypeStruct((pairs, HDIM), F32),
            jax.ShapeDtypeStruct((1, HDIM), F32),
        ),
        in_specs=[smem] * 3 + [vmem] * 7,
        out_specs=(vmem,) * 3,
        scratch_shapes=[
            pltpu.VMEM((n_tp, piece, feats), BF16),
            pltpu.VMEM((n_tp, piece, feats), BF16),
            pltpu.VMEM((n_tp, piece, width), BF16),
            pltpu.VMEM((piece, feats), F32),
            pltpu.VMEM((piece, feats), F32),
            pltpu.VMEM((piece, feats), F32),
            pltpu.VMEM((piece, feats), F32),
            pltpu.VMEM((piece, HDIM), F32),
            pltpu.VMEM((piece // 2, HDIM), F32),
            pltpu.VMEM((n_cfg, n_tp, piece // 2, HDIM), F32),
            pltpu.VMEM((1, HDIM), F32),
            pltpu.VMEM((n_seq, 1, HDIM), F32),
            dma((n_tp,)),
            dma((n_tp,)),
            dma((n_tp,)),
            dma((n_tp,)),
            dma((n_tp * n_cfg,)),
            dma((n_cfg, n_tp)),
            dma((n_seq,)),
            dma((n_seq,)),
        ],
        compiler_params=pltpu.CompilerParams(collective_id=1, has_side_effects=True, vmem_limit_bytes=40 << 20),
        name="finish",
    )(
        img_counts, step_index, guidance, att, w_out, stream[0], jnp.transpose(mod[0], (1, 0, 2)), proj, latent, top,
    )
    return (vel[:, :CH], nxt[:, :CH], tops[:, 2 * NREQ : 2 * NREQ + heads])


def solution(mesh):
    placed = (
        P("cfg", "seq", "tp"),
        P("cfg", "seq", None, "tp"),
        P(),
        P(),
        P("tp", None),
        P("cfg", None, None, None),
        P(),
        P("seq", None),
        P(),
        P(),
        P(),
        P(),
    )
    return jax.shard_map(
        local,
        mesh=mesh,
        in_specs=placed,
        out_specs=(P("seq", "cfg"), P("seq", "cfg"), P("cfg", "tp")),
        check_vma=False,
    )
```

```python
import functools
import math

import jax
import jax.numpy as jnp
import numpy as np
from jax import lax
from jax.experimental import pallas as pl
from jax.experimental.pallas import tpu as pltpu
from jax.sharding import PartitionSpec as P

MESH = pl.DeviceIdType.MESH
HDIM = 128
CH = 64
TXT = 128
STEPS = 8
NREQ = 8
PHI_MIX = 0.7
NEG = -1e30
SCALE = 1.0 / math.sqrt(float(HDIM))
EXP2_SCALE = SCALE * math.log2(math.e)
F32 = jnp.float32
BF16 = jnp.bfloat16


def frequency_row():
    pair_index = np.arange(64)
    axis_of = np.where(pair_index < 8, 0, np.where(pair_index < 36, 1, 2))
    axis_start = np.array([0, 8, 36])[axis_of]
    axis_width = np.array([16.0, 56.0, 56.0])[axis_of]
    frequency = 10000.0 ** (-2.0 * (pair_index - axis_start) / axis_width)
    return np.repeat(frequency, 2).astype(np.float32)[None, :]


def request_ends(counts):
    ends = []
    end = jnp.int32(0)
    for r in range(NREQ):
        end = end + (TXT + counts[r])
        ends.append(end)
    return ends


def pick(rows, ends, values):
    out = jnp.full(rows.shape, values[0])
    for r in range(NREQ - 1):
        out = jnp.where(rows >= ends[r], values[r + 1], out)
    return out


ORDER = ((1, 0), (1, 1), (2, 0), (2, 1), (3, 0), (1, 2), (3, 1), (4, 0), (2, 2), (4, 1), (3, 2), (4, 2))
D_CODE = sum(d * 5**i for i, (d, h) in enumerate(ORDER))
H_CODE = sum(h * 3**i for i, (d, h) in enumerate(ORDER))


def kernel(
    counts, widths, steps, guidance, qkv_ref, w_ref, stream_ref, mod_ref, proj_ref, latent_ref, freq_ref, qg_ref, kg_ref,
    vel_ref, next_ref, tops_ref,
    qkv, q_s, kv, reqq, reqk, win, m_s, l_s, acc_s,
    wall, att_s, attx, made, yout, ygot,
    res, mod_s, proj_s, mixed, gate, scale, shift, flow_s, mine, flows, row_s, sums,
    load_sem, right_sem, left_sem, share_sem, recv_sem, wsend, wrecv, wshare, wpartner,
    att_send, att_recv, y_send, y_recv, res_send, res_recv, flow_send, flow_recv, sum_send, sum_recv,
):
    n_tp, n_seq, n_cfg = lax.axis_size("tp"), lax.axis_size("seq"), lax.axis_size("cfg")
    group, me, col = lax.axis_index("cfg"), lax.axis_index("seq"), lax.axis_index("tp")
    heads, rows = q_s.shape[0], q_s.shape[1]
    width = heads * HDIM
    feats = w_ref.shape[1]
    half = feats // 2
    piece = rows // n_tp
    quarter = 2 * piece
    reach = win.shape[0] // 2
    chips = n_seq // 2
    chip, core = me // 2, me % 2
    other = 1 - core
    right = ((chip + 1) % chips) * 2 + core
    left = ((chip + chips - 1) % chips) * 2 + core
    partner = chip * 2 + other
    n_x = n_tp // 2
    tx, ty = col // 2, col % 2
    tiles = rows // HDIM
    barrier = pltpu.get_barrier_semaphore()

    def tp_peer(k):
        return (col + k) % n_tp

    def plane_peer(k):
        return (group + k // n_tp) % n_cfg, (col + k) % n_tp

    def seq_peer(k):
        return (me + k) % n_seq

    def hail_plane(k, carry):
        g, c = plane_peer(k)
        pl.semaphore_signal(barrier, inc=1, device_id={"cfg": g, "tp": c}, device_id_type=MESH)
        return carry

    lax.fori_loop(1, n_tp * n_cfg, hail_plane, 0)

    def hail_seq(k, carry):
        pl.semaphore_signal(barrier, inc=1, device_id={"seq": seq_peer(k)}, device_id_type=MESH)
        return carry

    lax.fori_loop(1, n_seq, hail_seq, 0)

    def remote(src, dst, send, recv, axis, peer):
        return pltpu.make_async_remote_copy(
            src_ref=src, dst_ref=dst, send_sem=send, recv_sem=recv,
            device_id={axis: peer}, device_id_type=MESH,
        )

    loads = [
        pltpu.make_async_copy(qkv_ref.at[1], qkv.at[1], load_sem.at[0]),
        pltpu.make_async_copy(qkv_ref.at[0], qkv.at[0], load_sem.at[1]),
        pltpu.make_async_copy(mod_ref, mod_s, load_sem.at[2]),
        pltpu.make_async_copy(proj_ref, proj_s.at[pl.ds(0, CH)], load_sem.at[3]),
        pltpu.make_async_copy(stream_ref.at[pl.ds(pl.multiple_of(col * piece, piece), piece)], res.at[col], load_sem.at[4]),
    ]
    for copy in loads:
        copy.start()
    values = [
        pltpu.make_async_copy(qkv_ref.at[2, :, pl.ds(h * HDIM, HDIM)], kv.at[h, 1], load_sem.at[5 + h]) for h in range(heads)
    ]
    for copy in values:
        copy.start()
    my_cols = pl.ds(pl.multiple_of(ty * half, half), half)
    near_cols = pl.ds(pl.multiple_of((1 - ty) * half, half), half)
    own_w = pltpu.make_async_copy(w_ref.at[:, my_cols], wall.at[col], load_sem.at[5 + heads])
    own_w.start()

    ends = request_ends(counts)
    starts = [jnp.int32(0)] + ends[:-1]
    ids = [jnp.int32(r) for r in range(NREQ)]
    row = me * rows + lax.broadcasted_iota(jnp.int32, (rows, HDIM), 0)
    start = pick(row, ends, starts)
    span = pick(row, ends, [widths[r].astype(F32) for r in range(NREQ)])
    pos = jnp.maximum(row - start - TXT, 0).astype(F32)
    height_id = jnp.floor((pos + 0.5) / span)
    width_id = pos - height_id * span
    lane = lax.broadcasted_iota(jnp.int32, (rows, HDIM), 1)
    angle = jnp.where(lane < 16, 0.0, jnp.where(lane < 72, height_id, width_id)) * freq_ref[...]
    even = lane % 2 == 0
    cos = jnp.cos(angle)
    sin = jnp.sin(angle)
    sin = jnp.where(even, -sin, sin)

    def rotated(part, h, gain):
        x = qkv[part, :, h * HDIM : (h + 1) * HDIM].astype(F32)
        x = x * lax.rsqrt(jnp.mean(x * x, axis=-1, keepdims=True) + 1e-06) * gain
        mate = jnp.where(even, pltpu.roll(x, HDIM - 1, 1), pltpu.roll(x, 1, 1))
        return x * cos + mate * sin

    loads[0].wait()
    for h in range(heads):
        key = rotated(1, h, kg_ref[...])
        for b in range(tiles):
            at = slice(b * HDIM, (b + 1) * HDIM)
            kv[h, 0, at, :] = key[at].T.astype(BF16)
    for copy in values:
        copy.wait()

    pl.semaphore_wait(barrier, n_tp * n_cfg - 1 + n_seq - 1)

    def slot(dz, p, h):
        return win.at[dz + reach, p, h]

    def go_right(d, h, src):
        return remote(src, slot(-d, core, h), right_sem.at[d - 1, h], recv_sem.at[reach - d, core, h], "seq", right)

    def go_left(d, h, src):
        return remote(src, slot(d, core, h), left_sem.at[d - 1, h], recv_sem.at[reach + d, core, h], "seq", left)

    def share(dz, h, src):
        return remote(src, slot(dz, core, h), share_sem.at[dz + reach, h], recv_sem.at[dz + reach, core, h], "seq", partner)

    def landed(dz, p, h):
        remote(slot(dz, p, h), slot(dz, p, h), share_sem.at[0, 0], recv_sem.at[dz + reach, p, h], "seq", partner).wait_recv()

    def set_out(h):
        go_right(1, h, kv.at[h]).start()
        go_left(1, h, kv.at[h]).start()
        share(0, h, kv.at[h]).start()

    set_out(0)
    set_out(1)

    x_next = ((tx + 1) % n_x) * 2 + ty
    x_prev = ((tx + n_x - 1) % n_x) * 2 + ty
    y_peer = tx * 2 + 1 - ty
    far_x = ((tx + 2) % n_x) * 2
    core_rows = pl.ds(pl.multiple_of(core * 2 * quarter, 2 * quarter), 2 * quarter)
    low_rows = pl.ds(pl.multiple_of(core * 2 * quarter, quarter), quarter)
    high_rows = pl.ds(pl.multiple_of(core * 2 * quarter + quarter, quarter), quarter)
    mate_rows = pl.ds(pl.multiple_of(other * 2 * quarter, 2 * quarter), 2 * quarter)
    mate_low = pl.ds(pl.multiple_of(other * 2 * quarter, quarter), quarter)
    mate_high = pl.ds(pl.multiple_of(other * 2 * quarter + quarter, quarter), quarter)

    def w_at(source, part):
        return wall.at[source, part]

    prev_own, prev_near = x_prev, (x_prev // 2) * 2 + 1 - ty
    next_own, next_near = x_next, (x_next // 2) * 2 + 1 - ty
    far_own, far_near = far_x + ty, far_x + 1 - ty
    pieces = [
        (y_peer, core_rows, mate_rows),
        (prev_own, core_rows, mate_rows),
        (prev_near, core_rows, mate_rows),
        (next_own, core_rows, mate_rows),
        (next_near, core_rows, mate_rows),
        (far_own, low_rows, mate_low),
        (far_near, low_rows, mate_low),
        (far_own, high_rows, mate_high),
        (far_near, high_rows, mate_high),
    ]

    def w_sends():
        own = w_ref.at[core_rows, my_cols]
        near = w_at(y_peer, core_rows)
        return [
            remote(w_ref.at[core_rows, near_cols], w_at(col, core_rows), wsend.at[0], wrecv.at[0], "tp", y_peer),
            remote(own, w_at(col, core_rows), wsend.at[1], wrecv.at[1], "tp", x_next),
            remote(own, w_at(col, core_rows), wsend.at[3], wrecv.at[3], "tp", x_prev),
            remote(near, near, wsend.at[2], wrecv.at[2], "tp", x_next),
            remote(near, near, wsend.at[4], wrecv.at[4], "tp", x_prev),
            remote(w_at(prev_own, low_rows), w_at(prev_own, low_rows), wsend.at[5], wrecv.at[5], "tp", x_next),
            remote(w_at(next_own, high_rows), w_at(next_own, high_rows), wsend.at[7], wrecv.at[7], "tp", x_prev),
            remote(w_at(prev_near, low_rows), w_at(prev_near, low_rows), wsend.at[6], wrecv.at[6], "tp", x_next),
            remote(w_at(next_near, high_rows), w_at(next_near, high_rows), wsend.at[8], wrecv.at[8], "tp", x_prev),
        ]

    w_out = w_sends()

    def w_share(n):
        source, part, _ = pieces[n]
        return remote(w_at(source, part), w_at(source, part), wshare.at[n], wpartner.at[n], "seq", partner)

    def w_landed(n):
        source, part, _ = pieces[n]
        remote(w_at(source, part), w_at(source, part), wshare.at[n], wrecv.at[n], "tp", y_peer).wait_recv()

    def w_shared(n):
        source, _, part = pieces[n]
        remote(w_at(source, part), w_at(source, part), wshare.at[n], wpartner.at[n], "seq", partner).wait_recv()

    for n in (0, 1, 2):
        w_out[n].start()

    def res_copy(k, dest_slot):
        c = tp_peer(k)
        return remote(
            stream_ref.at[pl.ds(pl.multiple_of(c * piece, piece), piece)], res.at[dest_slot],
            res_send.at[k], res_recv.at[dest_slot], "tp", c,
        )

    def give_res(k, carry):
        res_copy(k, col).start()
        return carry

    lax.fori_loop(1, n_tp, give_res, 0)

    loads[1].wait()
    for h in range(heads):
        q_s[h] = rotated(0, h, qg_ref[...]).astype(BF16)
    reqq[...] = pick(row, ends, ids)
    every = lax.broadcasted_iota(jnp.int32, (n_seq, rows), 0) * rows + lax.broadcasted_iota(jnp.int32, (n_seq, rows), 1)
    reqk[...] = pick(every, ends, ids)

    def wide(x):
        return jnp.concatenate([x] * tiles, axis=1)

    def update(h, blocks):
        q = q_s[h]
        asked = wide(reqq[...])
        scores = []
        for ref, source in blocks:
            keys = jnp.concatenate([ref[0, b * HDIM : (b + 1) * HDIM, :] for b in range(tiles)], axis=1)
            s = jnp.dot(q, keys, preferred_element_type=F32)
            scores.append(jnp.where(asked == reqk[pl.ds(source, 1), :], s, NEG))
        best = functools.reduce(jnp.maximum, scores)
        m_old = m_s[h]
        m_new = jnp.maximum(m_old, jnp.max(best, axis=1, keepdims=True))
        shrink = jnp.exp2((m_old - m_new) * EXP2_SCALE)
        m_wide = wide(m_new)
        total = None
        acc = acc_s[h] * shrink
        for (ref, source), s in zip(blocks, scores):
            p = jnp.exp2((s - m_wide) * EXP2_SCALE)
            total = p if total is None else total + p
            acc = acc + jnp.dot(p.astype(BF16), ref[1], preferred_element_type=F32)
        l_s[h] = l_s[h] * shrink + jnp.sum(total, axis=1, keepdims=True)
        acc_s[h] = acc
        m_s[h] = m_new

    def block_of(dz, p):
        return ((chip + dz + chips) % chips) * 2 + p

    def own(h, carry):
        m_s[h] = jnp.full((rows, HDIM), NEG, F32)
        l_s[h] = jnp.zeros((rows, HDIM), F32)
        acc_s[h] = jnp.zeros((rows, HDIM), F32)
        update(h, [(kv.at[h], me)])
        return carry

    lax.fori_loop(0, heads, own, 0)

    loads[2].wait()
    chunk = 512
    token = me * rows + col * piece + lax.broadcasted_iota(jnp.int32, (piece, chunk), 0)

    def pick_rows(j, carry):
        at = pl.ds(pl.multiple_of(j * chunk, chunk), chunk)
        for which, out in ((0, gate), (1, scale), (2, shift)):
            value = jnp.broadcast_to(mod_s[which, 0:1, at], (piece, chunk))
            for r in range(NREQ - 1):
                value = jnp.where(token >= ends[r], mod_s[which, r + 1 : r + 2, at], value)
            out[:, at] = value
        return carry

    lax.fori_loop(0, feats // chunk, pick_rows, 0)

    give = reach - 2 * reach * core
    take = -give

    def pair(d, p, h):
        return [(slot(-d, p, h), block_of(-d, p)), (slot(d, p, h), block_of(d, p))]

    def att_copy(h, k, dest_slot):
        c = tp_peer(k)
        return remote(
            att_s.at[h, pl.ds(pl.multiple_of((c // 2) * quarter, quarter), quarter)], attx.at[h, dest_slot],
            att_send.at[h, k], att_recv.at[h, dest_slot], "tp", c,
        )

    def give_att(h):
        att_s[h] = (acc_s[h] / l_s[h]).astype(BF16)

        def one(k, carry):
            att_copy(h, k, col).start()
            return carry

        lax.fori_loop(1, n_tp, one, 0)
        attx[h, col] = att_s[h, pl.ds(pl.multiple_of(tx * quarter, quarter), quarter), :]

    def take_att(h):
        def one(k, carry):
            att_copy(h, k, tp_peer(k)).wait_recv()
            return carry

        lax.fori_loop(1, n_tp, one, 0)

    def product(h, at):
        left_side = jnp.concatenate([attx[h, k] for k in range(n_tp)], axis=1)
        weights = wall[:, h * HDIM : (h + 1) * HDIM, at].reshape(n_tp * HDIM, chunk)
        return jnp.dot(left_side, weights, preferred_element_type=F32)

    def step(i, carry):
        d_code, h_code, d_last, h_last = carry
        d, h = d_code % 5, h_code % 3

        @pl.when(i == 3)
        def _():
            w_landed(0)
            w_out[3].start()
            w_out[4].start()
            w_landed(1)
            w_out[5].start()
            w_landed(3)
            w_out[6].start()
            for n in (0, 1, 3):
                w_share(n).start()

        @pl.when(i == 7)
        def _():
            w_landed(2)
            w_out[7].start()
            w_landed(4)
            w_out[8].start()
            for n in (2, 4):
                w_share(n).start()

        @pl.when(i == 9)
        def _():
            for n in (5, 7):
                w_landed(n)
                w_share(n).start()

        @pl.when(i == 11)
        def _():
            take_att(1)

            def one(j, c):
                at = pl.ds(pl.multiple_of(j * chunk, chunk), chunk)
                made[:, at] = made[:, at] + product(1, at)
                return c

            lax.fori_loop(0, half // chunk, one, 0)

        landed(-d, core, h)

        @pl.when(d < reach)
        def _():
            go_right(d + 1, h, slot(-d, core, h)).start()

        landed(d, core, h)

        @pl.when(d < reach)
        def _():
            go_left(d + 1, h, slot(d, core, h)).start()
            share(-d, h, slot(-d, core, h)).start()
            share(d, h, slot(d, core, h)).start()

        @pl.when(d == reach)
        def _():
            share(give, h, slot(give, core, h)).start()

        @pl.when(i == 2)
        def _():
            set_out(2)

        update(h, pair(d, core, h))

        @pl.when((i > 0) & (d_last < reach))
        def _():
            landed(-d_last, other, h_last)
            landed(d_last, other, h_last)
            update(h_last, pair(d_last, other, h_last))

        @pl.when(((i > 0) & (i < 4)) | (d_last == reach))
        def _():
            near = (d_last != reach).astype(jnp.int32)
            dz = (1 - near) * take
            hh = near * (i - 1) + (1 - near) * h_last
            landed(dz, other, hh)
            update(hh, [(slot(dz, other, hh), block_of(dz, other))])

        @pl.when(i == 8)
        def _():
            give_att(0)

        @pl.when(i == 10)
        def _():
            give_att(1)
            for n in (6, 8):
                w_landed(n)
                w_share(n).start()
            own_w.wait()
            for n in range(9):
                w_shared(n)
            take_att(0)

            def one(j, c):
                at = pl.ds(pl.multiple_of(j * chunk, chunk), chunk)
                made[:, at] = product(0, at)
                return c

            lax.fori_loop(0, half // chunk, one, 0)

        return d_code // 5, h_code // 3, d, h

    lax.fori_loop(0, len(ORDER), step, (jnp.int32(D_CODE), jnp.int32(H_CODE), jnp.int32(0), jnp.int32(0)))

    landed(take, other, 2)
    update(2, [(slot(take, other, 2), block_of(take, other))])
    give_att(2)

    lane8 = lax.broadcasted_iota(jnp.int32, (1, HDIM), 1)
    top_row = jnp.zeros((1, HDIM), F32)
    for h in range(heads):
        top = jnp.max(jnp.max(m_s[h], axis=0, keepdims=True), axis=1, keepdims=True) * SCALE
        top_row = jnp.where(lane8 == 2 * NREQ + h, top, top_row)

    loads[3].wait()
    proj_s[pl.ds(CH, HDIM - CH), :] = jnp.zeros((HDIM - CH, feats), BF16)
    loads[4].wait()

    def take_res(k, carry):
        res_copy(k, tp_peer(k)).wait_recv()
        return carry

    lax.fori_loop(1, n_tp, take_res, 0)
    take_att(2)

    def y_copy(j):
        return remote(yout.at[j], ygot.at[j], y_send.at[j], y_recv.at[j], "tp", y_peer)

    keep = pl.ds(pl.multiple_of(ty * piece, piece), piece)
    pass_on = pl.ds(pl.multiple_of((1 - ty) * piece, piece), piece)

    def last_product(j, carry):
        at = pl.ds(pl.multiple_of(j * chunk, chunk), chunk)
        made[:, at] = made[:, at] + product(2, at)
        yout[j] = made[pass_on, at].astype(BF16)
        y_copy(j).start()
        return carry

    lax.fori_loop(0, half // chunk, last_product, 0)

    total1 = jnp.zeros((piece, 1), F32)
    for j in range(half // width):
        at = pl.ds(pl.multiple_of(ty * half + j * width, width), width)
        value = res[ty * (n_tp // 2) + j].astype(F32) + gate[:, at] * made[keep, j * width : (j + 1) * width]
        mixed[:, at] = value
        total1 = total1 + jnp.sum(value, axis=1, keepdims=True)
    for j in range(half // chunk):
        y_copy(j).wait_recv()
        at = pl.ds(pl.multiple_of((1 - ty) * half + j * chunk, chunk), chunk)
        mixed[:, at] = gate[:, at] * ygot[j].astype(F32)
    for j in range(half // width):
        at = pl.ds(pl.multiple_of((1 - ty) * half + j * width, width), width)
        value = res[(1 - ty) * (n_tp // 2) + j].astype(F32) + mixed[:, at]
        mixed[:, at] = value
        total1 = total1 + jnp.sum(value, axis=1, keepdims=True)
    mean = total1 * (1.0 / feats)
    variance = jnp.zeros((piece, 1), F32)
    for j in range(n_tp):
        at = slice(j * width, (j + 1) * width)
        centred = mixed[:, at] - mean
        mixed[:, at] = centred
        variance = variance + jnp.sum(centred * centred, axis=1, keepdims=True)
    inverse = lax.rsqrt(variance * (1.0 / feats) + 1e-06)
    flow = jnp.zeros((piece, HDIM), F32)
    for j in range(n_tp):
        at = slice(j * width, (j + 1) * width)
        normed = (mixed[:, at] * inverse * (1.0 + scale[:, at]) + shift[:, at]).astype(BF16)
        flow = flow + lax.dot_general(
            normed, proj_s[:, at], (((1,), (1,)), ((), ())), preferred_element_type=F32
        )
    flow_s[...] = flow
    even_rows = flow_s[pl.ds(0, piece // 2, stride=2), :]
    odd_rows = flow_s[pl.ds(1, piece // 2, stride=2), :]
    own_flow = even_rows + pltpu.roll(odd_rows, CH, 1)
    mine[...] = own_flow
    flows[group, col] = own_flow
    def flow_copy(k, g_slot, c_slot):
        g, c = plane_peer(k)
        return pltpu.make_async_remote_copy(
            src_ref=mine, dst_ref=flows.at[g_slot, c_slot],
            send_sem=flow_send.at[k], recv_sem=flow_recv.at[g_slot, c_slot],
            device_id={"cfg": g, "tp": c}, device_id_type=MESH,
        )

    def give_flow(k, carry):
        flow_copy(k, group, col).start()
        return carry

    lax.fori_loop(1, n_tp * n_cfg, give_flow, 0)

    pairs = rows // 2
    lane2 = lax.broadcasted_iota(jnp.int32, (pairs, HDIM), 1)
    row2 = me * rows + 2 * lax.broadcasted_iota(jnp.int32, (pairs, HDIM), 0) + (lane2 >= CH).astype(jnp.int32)
    request = pick(row2, ends, [jnp.int32(r) for r in range(NREQ)])
    image = (row2 - pick(row2, ends, [jnp.int32(0)] + ends[:-1])) >= TXT
    guide = pick(row2, ends, [guidance[r] for r in range(NREQ)])
    at_step = pick(row2, ends, [steps[r].astype(F32) for r in range(NREQ)])

    def sigma(u):
        remaining = 1.0 - u / STEPS
        return 3.0 * remaining / (1.0 + 2.0 * remaining)

    delta = sigma(at_step + 1.0) - sigma(at_step)

    def take_flow(k, carry):
        g, c = plane_peer(k)
        flow_copy(k, g, c).wait_recv()
        return carry

    lax.fori_loop(1, n_tp * n_cfg, take_flow, 0)

    cond = flows[0].reshape(pairs, HDIM)
    uncond = flows[1].reshape(pairs, HDIM)
    guided = uncond + guide * (cond - uncond)
    cond_square = jnp.where(image, cond * cond, 0.0)
    guided_square = jnp.where(image, guided * guided, 0.0)
    parts = []
    for square in (cond_square, guided_square):
        for r in range(NREQ):
            parts.append(jnp.sum(jnp.where(request == r, square, 0.0), axis=0, keepdims=True))
    stacked = jnp.sum(jnp.concatenate(parts, axis=0), axis=1, keepdims=True)
    diagonal = lax.broadcasted_iota(jnp.int32, (2 * NREQ, HDIM), 0) == lax.broadcasted_iota(jnp.int32, (2 * NREQ, HDIM), 1)
    own_sums = jnp.sum(jnp.where(diagonal, stacked, 0.0), axis=0, keepdims=True) + top_row
    row_s[...] = own_sums
    sums[me] = own_sums

    def sum_copy(k, dest_slot):
        return pltpu.make_async_remote_copy(
            src_ref=row_s, dst_ref=sums.at[dest_slot],
            send_sem=sum_send.at[k], recv_sem=sum_recv.at[dest_slot],
            device_id={"seq": seq_peer(k)}, device_id_type=MESH,
        )

    def give_sum(k, carry):
        sum_copy(k, me).start()
        return carry

    lax.fori_loop(1, n_seq, give_sum, 0)

    def take_sum(k, carry):
        sum_copy(k, seq_peer(k)).wait_recv()
        return carry

    lax.fori_loop(1, n_seq, take_sum, 0)

    total = sums[0]
    top = sums[0]
    for k in range(1, n_seq):
        total = total + sums[k]
        top = jnp.maximum(top, sums[k])
    tops_ref[...] = top
    lane1 = lax.broadcasted_iota(jnp.int32, (1, HDIM), 1)
    entries = jnp.ones((1, HDIM), F32)
    for r in range(NREQ):
        entries = jnp.where(lane1 == r, counts[r].astype(F32) * CH, entries)
    guided_total = pltpu.roll(total, HDIM - NREQ, 1)
    factor = (PHI_MIX * jnp.sqrt(total / entries + 1e-06) + (1.0 - PHI_MIX)) / jnp.sqrt(guided_total / entries + 1e-06)
    factor_row = jnp.zeros((pairs, HDIM), F32)
    for r in range(NREQ):
        one = jnp.sum(jnp.where(lane1 == r, factor, 0.0), axis=1, keepdims=True)
        factor_row = jnp.where(request == r, one, factor_row)
    velocity = guided * jnp.where(image, factor_row, 0.0)
    stepped = latent_ref[...] + delta * velocity
    vel_ref[...] = jnp.where(group == 0, velocity, pltpu.roll(velocity, CH, 1))
    next_ref[...] = jnp.where(group == 0, stepped, pltpu.roll(stepped, CH, 1))

    def drain_tp(k, carry):
        res_copy(k, col).wait_send()
        for h in range(heads):
            att_copy(h, k, col).wait_send()
        return carry

    lax.fori_loop(1, n_tp, drain_tp, 0)

    def drain_flow(k, carry):
        flow_copy(k, group, col).wait_send()
        return carry

    lax.fori_loop(1, n_tp * n_cfg, drain_flow, 0)

    def drain_sum(k, carry):
        sum_copy(k, me).wait_send()
        return carry

    lax.fori_loop(1, n_seq, drain_sum, 0)

    def drain(h, carry):
        for d in range(1, reach + 1):
            go_right(d, h, kv.at[h]).wait_send()
            go_left(d, h, kv.at[h]).wait_send()
        for dz in range(1 - reach, reach):
            share(dz, h, kv.at[h]).wait_send()
        share(give, h, kv.at[h]).wait_send()
        return carry

    lax.fori_loop(0, heads, drain, 0)
    for copy in w_out:
        copy.wait_send()
    for n in range(9):
        w_share(n).wait_send()
    for j in range(half // chunk):
        y_copy(j).wait_send()


def local(stream, qkv, q_gain, k_gain, w_out, mod, w_proj, latent, guidance, img_counts, img_widths, step_index):
    rows, width = stream.shape[1], stream.shape[2]
    feats = w_out.shape[1]
    heads = width // HDIM
    n_seq, n_tp, n_cfg = lax.axis_size("seq"), lax.axis_size("tp"), lax.axis_size("cfg")
    piece = rows // n_tp
    img_most = (rows * n_seq - NREQ * TXT) // 4
    reach = ((TXT + img_most + rows - 2) // rows + 1) // 2
    smem = pl.BlockSpec(memory_space=pltpu.SMEM)
    vmem = pl.BlockSpec(memory_space=pltpu.VMEM)
    hbm = pl.BlockSpec(memory_space=pl.ANY)
    dma = pltpu.SemaphoreType.DMA
    pairs = rows // 2
    half = feats // 2
    chunk = 512
    vel, nxt, tops = pl.pallas_call(
        kernel,
        out_shape=(
            jax.ShapeDtypeStruct((pairs, HDIM), F32),
            jax.ShapeDtypeStruct((pairs, HDIM), F32),
            jax.ShapeDtypeStruct((1, HDIM), F32),
        ),
        in_specs=[smem] * 4 + [hbm] * 5 + [vmem] * 4,
        out_specs=(vmem,) * 3,
        scratch_shapes=[
            pltpu.VMEM((2, rows, width), BF16),
            pltpu.VMEM((heads, rows, HDIM), BF16),
            pltpu.VMEM((heads, 2, rows, HDIM), BF16),
            pltpu.VMEM((rows, HDIM), jnp.int32),
            pltpu.VMEM((n_seq, rows), jnp.int32),
            pltpu.VMEM((2 * reach + 1, 2, heads, 2, rows, HDIM), BF16),
            pltpu.VMEM((heads, rows, HDIM), F32),
            pltpu.VMEM((heads, rows, HDIM), F32),
            pltpu.VMEM((heads, rows, HDIM), F32),
            pltpu.VMEM((n_tp, rows, half), BF16),
            pltpu.VMEM((heads, rows, HDIM), BF16),
            pltpu.VMEM((heads, n_tp, 2 * piece, HDIM), BF16),
            pltpu.VMEM((2 * piece, half), F32),
            pltpu.VMEM((half // chunk, piece, chunk), BF16),
            pltpu.VMEM((half // chunk, piece, chunk), BF16),
            pltpu.VMEM((n_tp, piece, width), BF16),
            pltpu.VMEM((3, NREQ, feats), F32),
            pltpu.VMEM((HDIM, feats), BF16),
            pltpu.VMEM((piece, feats), F32),
            pltpu.VMEM((piece, feats), F32),
            pltpu.VMEM((piece, feats), F32),
            pltpu.VMEM((piece, feats), F32),
            pltpu.VMEM((piece, HDIM), F32),
            pltpu.VMEM((piece // 2, HDIM), F32),
            pltpu.VMEM((n_cfg, n_tp, piece // 2, HDIM), F32),
            pltpu.VMEM((1, HDIM), F32),
            pltpu.VMEM((n_seq, 1, HDIM), F32),
            dma((6 + heads,)),
            dma((reach, heads)),
            dma((reach, heads)),
            dma((2 * reach + 1, heads)),
            dma((2 * reach + 1, 2, heads)),
            dma((9,)),
            dma((9,)),
            dma((9,)),
            dma((9,)),
            dma((heads, n_tp)),
            dma((heads, n_tp)),
            dma((half // chunk,)),
            dma((half // chunk,)),
            dma((n_tp,)),
            dma((n_tp,)),
            dma((n_tp * n_cfg,)),
            dma((n_cfg, n_tp)),
            dma((n_seq,)),
            dma((n_seq,)),
        ],
        compiler_params=pltpu.CompilerParams(collective_id=0, has_side_effects=True, vmem_limit_bytes=56 << 20),
        name="flow_step",
    )(
        img_counts, img_widths, step_index, guidance, jnp.transpose(qkv[0], (1, 0, 2)), w_out, stream[0],
        jnp.transpose(mod[0], (1, 0, 2)), w_proj, latent, jnp.asarray(frequency_row()),
        q_gain.reshape(1, HDIM), k_gain.reshape(1, HDIM),
    )
    return (vel[:, :CH], nxt[:, :CH], tops[:, 2 * NREQ : 2 * NREQ + heads])


def solution(mesh):
    placed = (
        P("cfg", "seq", "tp"),
        P("cfg", "seq", None, "tp"),
        P(),
        P(),
        P("tp", None),
        P("cfg", None, None, None),
        P(),
        P("seq", None),
        P(),
        P(),
        P(),
        P(),
    )
    return jax.shard_map(
        local,
        mesh=mesh,
        in_specs=placed,
        out_specs=(P("seq", "cfg"), P("seq", "cfg"), P("cfg", "tp")),
        check_vma=False,
    )
```

```python
import functools
import math

import jax
import jax.numpy as jnp
import numpy as np
from jax import lax
from jax.experimental import pallas as pl
from jax.experimental.pallas import tpu as pltpu
from jax.sharding import PartitionSpec as P

MESH = pl.DeviceIdType.MESH
HDIM = 128
CH = 64
TXT = 128
STEPS = 8
NREQ = 8
PHI_MIX = 0.7
NEG = -1e30
SCALE = 1.0 / math.sqrt(float(HDIM))
EXP2_SCALE = SCALE * math.log2(math.e)
F32 = jnp.float32
BF16 = jnp.bfloat16


def frequency_row():
    pair_index = np.arange(64)
    axis_of = np.where(pair_index < 8, 0, np.where(pair_index < 36, 1, 2))
    axis_start = np.array([0, 8, 36])[axis_of]
    axis_width = np.array([16.0, 56.0, 56.0])[axis_of]
    frequency = 10000.0 ** (-2.0 * (pair_index - axis_start) / axis_width)
    return np.repeat(frequency, 2).astype(np.float32)[None, :]


def request_ends(counts):
    ends = []
    end = jnp.int32(0)
    for r in range(NREQ):
        end = end + (TXT + counts[r])
        ends.append(end)
    return ends


def pick(rows, ends, values):
    out = jnp.full(rows.shape, values[0])
    for r in range(NREQ - 1):
        out = jnp.where(rows >= ends[r], values[r + 1], out)
    return out


ORDER = ((1, 0), (1, 1), (2, 0), (2, 1), (3, 0), (1, 2), (3, 1), (4, 0), (2, 2), (4, 1), (3, 2), (4, 2))
D_CODE = sum(d * 5**i for i, (d, h) in enumerate(ORDER))
H_CODE = sum(h * 3**i for i, (d, h) in enumerate(ORDER))


def kernel(
    rim,
    counts_ref, widths_ref, steps_ref, guidance_ref, qkv_ref, w_ref, stream_ref, mod_ref, proj_ref, latent_ref,
    freq_ref, qg_ref, kg_ref,
    vel_ref, next_ref, tops_ref,
    counts, widths, steps, guidance, latent_s, freq_s, qg_s, kg_s, qkv, q_s, kv, reqq, reqk, win, m_s, l_s, acc_s,
    wall, att_s, attx, made, yout, ygot,
    res, mod_s, proj_s, mixed, gate, scale, shift, flow_s, mine, flows, row_s, sums,
    first_sem, load_sem, right_sem, left_sem, share_sem, recv_sem, wsend, wrecv, wshare, wpartner,
    att_send, att_recv, y_send, y_recv, res_send, res_recv, flow_send, flow_recv, sum_send, sum_recv,
):
    n_tp, n_seq, n_cfg = lax.axis_size("tp"), lax.axis_size("seq"), lax.axis_size("cfg")
    group, me, col = lax.axis_index("cfg"), lax.axis_index("seq"), lax.axis_index("tp")
    heads, rows = q_s.shape[0], q_s.shape[1]
    width = heads * HDIM
    feats = w_ref.shape[1]
    half = feats // 2
    piece = rows // n_tp
    quarter = 2 * piece
    reach = win.shape[0] // 2
    chips = n_seq // 2
    chip, core = me // 2, me % 2
    other = 1 - core
    right = ((chip + 1) % chips) * 2 + core
    left = ((chip + chips - 1) % chips) * 2 + core
    partner = chip * 2 + other
    n_x = n_tp // 2
    tx, ty = col // 2, col % 2
    tiles = rows // HDIM
    barrier = pltpu.get_barrier_semaphore()

    def tp_peer(k):
        return (col + k) % n_tp

    def plane_peer(k):
        return (group + k // n_tp) % n_cfg, (col + k) % n_tp

    def seq_peer(k):
        return (me + k) % n_seq

    def hail_plane(k, carry):
        g, c = plane_peer(k)
        pl.semaphore_signal(barrier, inc=1, device_id={"cfg": g, "tp": c}, device_id_type=MESH)
        return carry

    lax.fori_loop(1, n_tp * n_cfg, hail_plane, 0)

    near_count = 4 * reach + 1

    def hail_seq(k, carry):
        peer = (2 * chip + 2 * n_seq - 2 * reach + k) % n_seq

        @pl.when(peer != me)
        def _():
            pl.semaphore_signal(barrier, inc=1, device_id={"seq": peer}, device_id_type=MESH)

        return carry

    lax.fori_loop(0, near_count + 1, hail_seq, 0)

    def remote(src, dst, send, recv, axis, peer):
        return pltpu.make_async_remote_copy(
            src_ref=src, dst_ref=dst, send_sem=send, recv_sem=recv,
            device_id={axis: peer}, device_id_type=MESH,
        )

    firsts = [
        pltpu.make_async_copy(source, target, first_sem.at[n])
        for n, (source, target) in enumerate(
            (
                (counts_ref, counts), (widths_ref, widths), (steps_ref, steps), (guidance_ref, guidance),
                (freq_ref, freq_s), (qg_ref, qg_s), (kg_ref, kg_s), (latent_ref, latent_s),
            )
        )
    ]
    for copy in firsts:
        copy.start()
    loads = [
        pltpu.make_async_copy(qkv_ref.at[1], qkv.at[1], load_sem.at[0]),
        pltpu.make_async_copy(qkv_ref.at[0], qkv.at[0], load_sem.at[1]),
        pltpu.make_async_copy(mod_ref, mod_s, load_sem.at[2]),
        pltpu.make_async_copy(proj_ref, proj_s.at[pl.ds(0, CH)], load_sem.at[3]),
        pltpu.make_async_copy(stream_ref.at[pl.ds(pl.multiple_of(col * piece, piece), piece)], res.at[col], load_sem.at[4]),
    ]
    for copy in loads:
        copy.start()
    values = [
        pltpu.make_async_copy(qkv_ref.at[2, :, pl.ds(h * HDIM, HDIM)], kv.at[h, 1], load_sem.at[5 + h]) for h in range(heads)
    ]
    for copy in values:
        copy.start()
    my_cols = pl.ds(pl.multiple_of(ty * half, half), half)
    near_cols = pl.ds(pl.multiple_of((1 - ty) * half, half), half)
    own_w = pltpu.make_async_copy(w_ref.at[:, my_cols], wall.at[col], load_sem.at[5 + heads])
    own_w.start()

    for copy in firsts:
        copy.wait()
    ends = request_ends(counts)
    starts = [jnp.int32(0)] + ends[:-1]
    ids = [jnp.int32(r) for r in range(NREQ)]
    row = me * rows + lax.broadcasted_iota(jnp.int32, (rows, HDIM), 0)
    start = pick(row, ends, starts)
    span = pick(row, ends, [widths[r].astype(F32) for r in range(NREQ)])
    pos = jnp.maximum(row - start - TXT, 0).astype(F32)
    height_id = jnp.floor((pos + 0.5) / span)
    width_id = pos - height_id * span
    lane = lax.broadcasted_iota(jnp.int32, (rows, HDIM), 1)
    angle = jnp.where(lane < 16, 0.0, jnp.where(lane < 72, height_id, width_id)) * freq_s[...]
    even = lane % 2 == 0
    cos = jnp.cos(angle)
    sin = jnp.sin(angle)
    sin = jnp.where(even, -sin, sin)

    def rotated(part, h, gain):
        x = qkv[part, :, h * HDIM : (h + 1) * HDIM].astype(F32)
        x = x * lax.rsqrt(jnp.mean(x * x, axis=-1, keepdims=True) + 1e-06) * gain
        mate = jnp.where(even, pltpu.roll(x, HDIM - 1, 1), pltpu.roll(x, 1, 1))
        return x * cos + mate * sin

    def make_key(h):
        key = rotated(1, h, kg_s[...])
        for b in range(tiles):
            at = slice(b * HDIM, (b + 1) * HDIM)
            kv[h, 0, at, :] = key[at].T.astype(BF16)

    loads[0].wait()
    make_key(0)
    for copy in values:
        copy.wait()

    def slot(dz, p, h):
        return win.at[dz + reach, p, h]

    def go_right(d, h, src):
        return remote(src, slot(-d, core, h), right_sem.at[d - 1, h], recv_sem.at[reach - d, core, h], "seq", right)

    def go_left(d, h, src):
        return remote(src, slot(d, core, h), left_sem.at[d - 1, h], recv_sem.at[reach + d, core, h], "seq", left)

    def share(dz, h, src):
        return remote(src, slot(dz, core, h), share_sem.at[dz + reach, h], recv_sem.at[dz + reach, core, h], "seq", partner)

    def landed(dz, p, h):
        remote(slot(dz, p, h), slot(dz, p, h), share_sem.at[0, 0], recv_sem.at[dz + reach, p, h], "seq", partner).wait_recv()

    cut = rows - rim
    whole, early, late = pl.ds(0, rows), pl.ds(0, rim), pl.ds(cut, rim)

    def rim_right(h, at):
        return remote(
            slot(1 - reach, core, h).at[:, at], slot(-reach, core, h).at[:, at],
            right_sem.at[reach - 1, h], recv_sem.at[0, core, h], "seq", right,
        )

    def rim_left(h, at):
        return remote(
            slot(reach - 1, core, h).at[:, at], slot(reach, core, h).at[:, at],
            left_sem.at[reach - 1, h], recv_sem.at[2 * reach, core, h], "seq", left,
        )

    def at_rim(right_op, left_op):
        @pl.when(core == 0)
        def _():
            right_op(late)
            left_op(whole)

        @pl.when(core == 1)
        def _():
            right_op(whole)
            left_op(early)

    def set_out(h):
        go_right(1, h, kv.at[h]).start()
        go_left(1, h, kv.at[h]).start()
        share(0, h, kv.at[h]).start()

    pl.semaphore_wait(barrier, n_tp * n_cfg - 1 + near_count)
    set_out(0)
    make_key(1)
    set_out(1)

    x_next = ((tx + 1) % n_x) * 2 + ty
    x_prev = ((tx + n_x - 1) % n_x) * 2 + ty
    y_peer = tx * 2 + 1 - ty
    far_x = ((tx + 2) % n_x) * 2
    core_rows = pl.ds(pl.multiple_of(core * 2 * quarter, 2 * quarter), 2 * quarter)
    low_rows = pl.ds(pl.multiple_of(core * 2 * quarter, quarter), quarter)
    high_rows = pl.ds(pl.multiple_of(core * 2 * quarter + quarter, quarter), quarter)
    mate_rows = pl.ds(pl.multiple_of(other * 2 * quarter, 2 * quarter), 2 * quarter)
    mate_low = pl.ds(pl.multiple_of(other * 2 * quarter, quarter), quarter)
    mate_high = pl.ds(pl.multiple_of(other * 2 * quarter + quarter, quarter), quarter)

    def w_at(source, part):
        return wall.at[source, part]

    prev_own, prev_near = x_prev, (x_prev // 2) * 2 + 1 - ty
    next_own, next_near = x_next, (x_next // 2) * 2 + 1 - ty
    far_own, far_near = far_x + ty, far_x + 1 - ty
    pieces = [
        (y_peer, core_rows, mate_rows),
        (prev_own, core_rows, mate_rows),
        (prev_near, core_rows, mate_rows),
        (next_own, core_rows, mate_rows),
        (next_near, core_rows, mate_rows),
        (far_own, low_rows, mate_low),
        (far_near, low_rows, mate_low),
        (far_own, high_rows, mate_high),
        (far_near, high_rows, mate_high),
    ]

    def w_sends():
        own = w_ref.at[core_rows, my_cols]
        near = w_at(y_peer, core_rows)
        return [
            remote(w_ref.at[core_rows, near_cols], w_at(col, core_rows), wsend.at[0], wrecv.at[0], "tp", y_peer),
            remote(own, w_at(col, core_rows), wsend.at[1], wrecv.at[1], "tp", x_next),
            remote(own, w_at(col, core_rows), wsend.at[3], wrecv.at[3], "tp", x_prev),
            remote(near, near, wsend.at[2], wrecv.at[2], "tp", x_next),
            remote(near, near, wsend.at[4], wrecv.at[4], "tp", x_prev),
            remote(w_at(prev_own, low_rows), w_at(prev_own, low_rows), wsend.at[5], wrecv.at[5], "tp", x_next),
            remote(w_at(next_own, high_rows), w_at(next_own, high_rows), wsend.at[7], wrecv.at[7], "tp", x_prev),
            remote(w_at(prev_near, low_rows), w_at(prev_near, low_rows), wsend.at[6], wrecv.at[6], "tp", x_next),
            remote(w_at(next_near, high_rows), w_at(next_near, high_rows), wsend.at[8], wrecv.at[8], "tp", x_prev),
        ]

    w_out = w_sends()

    def w_share(n):
        source, part, _ = pieces[n]
        return remote(w_at(source, part), w_at(source, part), wshare.at[n], wpartner.at[n], "seq", partner)

    def w_landed(n):
        source, part, _ = pieces[n]
        remote(w_at(source, part), w_at(source, part), wshare.at[n], wrecv.at[n], "tp", y_peer).wait_recv()

    def w_shared(n):
        source, _, part = pieces[n]
        remote(w_at(source, part), w_at(source, part), wshare.at[n], wpartner.at[n], "seq", partner).wait_recv()

    for n in (0, 1, 2):
        w_out[n].start()

    def res_copy(k, dest_slot):
        c = tp_peer(k)
        return remote(
            stream_ref.at[pl.ds(pl.multiple_of(c * piece, piece), piece)], res.at[dest_slot],
            res_send.at[k], res_recv.at[dest_slot], "tp", c,
        )

    def give_res(k, carry):
        res_copy(k, col).start()
        return carry

    lax.fori_loop(1, n_tp, give_res, 0)

    make_key(2)
    loads[1].wait()
    for h in range(heads):
        q_s[h] = rotated(0, h, qg_s[...]).astype(BF16)
    reqq[...] = pick(row, ends, ids)
    every = lax.broadcasted_iota(jnp.int32, (n_seq, rows), 0) * rows + lax.broadcasted_iota(jnp.int32, (n_seq, rows), 1)
    reqk[...] = pick(every, ends, ids)

    def wide(x):
        return jnp.concatenate([x] * tiles, axis=1)

    def update(h, blocks):
        q = q_s[h]
        asked = wide(reqq[...])
        scores = []
        for ref, source in blocks:
            keys = jnp.concatenate([ref[0, b * HDIM : (b + 1) * HDIM, :] for b in range(tiles)], axis=1)
            s = jnp.dot(q, keys, preferred_element_type=F32)
            scores.append(jnp.where(asked == reqk[pl.ds(source, 1), :], s, NEG))
        best = functools.reduce(jnp.maximum, scores)
        m_old = m_s[h]
        m_new = jnp.maximum(m_old, jnp.max(best, axis=1, keepdims=True))
        shrink = jnp.exp2((m_old - m_new) * EXP2_SCALE)
        m_wide = wide(m_new)
        total = None
        acc = acc_s[h] * shrink
        for (ref, source), s in zip(blocks, scores):
            p = jnp.exp2((s - m_wide) * EXP2_SCALE)
            total = p if total is None else total + p
            acc = acc + jnp.dot(p.astype(BF16), ref[1], preferred_element_type=F32)
        l_s[h] = l_s[h] * shrink + jnp.sum(total, axis=1, keepdims=True)
        acc_s[h] = acc
        m_s[h] = m_new

    def block_of(dz, p):
        return ((chip + dz + chips) % chips) * 2 + p

    def own(h, carry):
        blank = jnp.zeros((2, cut, HDIM), BF16)

        @pl.when(core == 0)
        def _():
            win[0, 0, h, :, pl.ds(0, cut), :] = blank

        @pl.when(core == 1)
        def _():
            win[2 * reach, 1, h, :, pl.ds(rim, cut), :] = blank

        m_s[h] = jnp.full((rows, HDIM), NEG, F32)
        l_s[h] = jnp.zeros((rows, HDIM), F32)
        acc_s[h] = jnp.zeros((rows, HDIM), F32)
        update(h, [(kv.at[h], me)])
        return carry

    lax.fori_loop(0, heads, own, 0)

    loads[2].wait()
    chunk = 512
    token = me * rows + col * piece + lax.broadcasted_iota(jnp.int32, (piece, chunk), 0)

    def pick_rows(j, carry):
        at = pl.ds(pl.multiple_of(j * chunk, chunk), chunk)
        for which, out in ((0, gate), (1, scale), (2, shift)):
            value = jnp.broadcast_to(mod_s[which, 0:1, at], (piece, chunk))
            for r in range(NREQ - 1):
                value = jnp.where(token >= ends[r], mod_s[which, r + 1 : r + 2, at], value)
            out[:, at] = value
        return carry

    lax.fori_loop(0, feats // chunk, pick_rows, 0)

    give = reach - 2 * reach * core
    take = -give

    def pair(d, p, h):
        return [(slot(-d, p, h), block_of(-d, p)), (slot(d, p, h), block_of(d, p))]

    def att_copy(h, k, dest_slot):
        c = tp_peer(k)
        return remote(
            att_s.at[h, pl.ds(pl.multiple_of((c // 2) * quarter, quarter), quarter)], attx.at[h, dest_slot],
            att_send.at[h, k], att_recv.at[h, dest_slot], "tp", c,
        )

    def give_att(h):
        att_s[h] = (acc_s[h] / l_s[h]).astype(BF16)

        def one(k, carry):
            att_copy(h, k, col).start()
            return carry

        lax.fori_loop(1, n_tp, one, 0)
        attx[h, col] = att_s[h, pl.ds(pl.multiple_of(tx * quarter, quarter), quarter), :]

    def take_att(h):
        def one(k, carry):
            att_copy(h, k, tp_peer(k)).wait_recv()
            return carry

        lax.fori_loop(1, n_tp, one, 0)

    def product(h, at):
        left_side = jnp.concatenate([attx[h, k] for k in range(n_tp)], axis=1)
        weights = wall[:, h * HDIM : (h + 1) * HDIM, at].reshape(n_tp * HDIM, chunk)
        return jnp.dot(left_side, weights, preferred_element_type=F32)

    def step(i, carry):
        d_code, h_code, d_last, h_last = carry
        d, h = d_code % 5, h_code % 3

        @pl.when(i == 3)
        def _():
            w_landed(0)
            w_out[3].start()
            w_out[4].start()
            w_landed(1)
            w_out[5].start()
            w_landed(3)
            w_out[6].start()
            for n in (0, 1, 3):
                w_share(n).start()

        @pl.when(i == 7)
        def _():
            w_landed(2)
            w_out[7].start()
            w_landed(4)
            w_out[8].start()
            for n in (2, 4):
                w_share(n).start()

        @pl.when(i == 9)
        def _():
            for n in (5, 7):
                w_landed(n)
                w_share(n).start()

        @pl.when(i == 11)
        def _():
            take_att(1)

            def one(j, c):
                at = pl.ds(pl.multiple_of(j * chunk, chunk), chunk)
                made[:, at] = made[:, at] + product(1, at)
                return c

            lax.fori_loop(0, half // chunk, one, 0)

        @pl.when(d < reach - 1)
        def _():
            landed(-d, core, h)
            go_right(d + 1, h, slot(-d, core, h)).start()
            landed(d, core, h)
            go_left(d + 1, h, slot(d, core, h)).start()

        @pl.when(d == reach - 1)
        def _():
            landed(-d, core, h)
            landed(d, core, h)
            at_rim(lambda at: rim_right(h, at).start(), lambda at: rim_left(h, at).start())

        @pl.when(d < reach)
        def _():
            share(-d, h, slot(-d, core, h)).start()
            share(d, h, slot(d, core, h)).start()

        @pl.when(d == reach)
        def _():
            at_rim(lambda at: rim_right(h, at).wait_recv(), lambda at: rim_left(h, at).wait_recv())
            share(give, h, slot(give, core, h)).start()

        @pl.when(i == 2)
        def _():
            set_out(2)

        update(h, pair(d, core, h))

        @pl.when((i > 0) & (d_last < reach))
        def _():
            landed(-d_last, other, h_last)
            landed(d_last, other, h_last)
            update(h_last, pair(d_last, other, h_last))

        @pl.when(((i > 0) & (i < 4)) | (d_last == reach))
        def _():
            near = (d_last != reach).astype(jnp.int32)
            dz = (1 - near) * take
            hh = near * (i - 1) + (1 - near) * h_last
            landed(dz, other, hh)
            update(hh, [(slot(dz, other, hh), block_of(dz, other))])

        @pl.when(i == 8)
        def _():
            give_att(0)

        @pl.when(i == 10)
        def _():
            give_att(1)
            for n in (6, 8):
                w_landed(n)
                w_share(n).start()
            own_w.wait()
            for n in range(9):
                w_shared(n)
            take_att(0)

            def one(j, c):
                at = pl.ds(pl.multiple_of(j * chunk, chunk), chunk)
                made[:, at] = product(0, at)
                return c

            lax.fori_loop(0, half // chunk, one, 0)

        return d_code // 5, h_code // 3, d, h

    lax.fori_loop(0, len(ORDER), step, (jnp.int32(D_CODE), jnp.int32(H_CODE), jnp.int32(0), jnp.int32(0)))

    landed(take, other, 2)
    update(2, [(slot(take, other, 2), block_of(take, other))])
    give_att(2)

    lane8 = lax.broadcasted_iota(jnp.int32, (1, HDIM), 1)
    top_row = jnp.zeros((1, HDIM), F32)
    for h in range(heads):
        top = jnp.max(jnp.max(m_s[h], axis=0, keepdims=True), axis=1, keepdims=True) * SCALE
        top_row = jnp.where(lane8 == 2 * NREQ + h, top, top_row)

    loads[3].wait()
    proj_s[pl.ds(CH, HDIM - CH), :] = jnp.zeros((HDIM - CH, feats), BF16)
    loads[4].wait()

    def take_res(k, carry):
        res_copy(k, tp_peer(k)).wait_recv()
        return carry

    lax.fori_loop(1, n_tp, take_res, 0)
    take_att(2)

    def y_copy(j):
        return remote(yout.at[j], ygot.at[j], y_send.at[j], y_recv.at[j], "tp", y_peer)

    keep = pl.ds(pl.multiple_of(ty * piece, piece), piece)
    pass_on = pl.ds(pl.multiple_of((1 - ty) * piece, piece), piece)

    def last_product(j, carry):
        at = pl.ds(pl.multiple_of(j * chunk, chunk), chunk)
        made[:, at] = made[:, at] + product(2, at)
        yout[j] = made[pass_on, at].astype(BF16)
        y_copy(j).start()
        return carry

    lax.fori_loop(0, half // chunk, last_product, 0)

    total1 = jnp.zeros((piece, 1), F32)
    for j in range(half // width):
        at = pl.ds(pl.multiple_of(ty * half + j * width, width), width)
        value = res[ty * (n_tp // 2) + j].astype(F32) + gate[:, at] * made[keep, j * width : (j + 1) * width]
        mixed[:, at] = value
        total1 = total1 + jnp.sum(value, axis=1, keepdims=True)
    for j in range(half // chunk):
        y_copy(j).wait_recv()
        at = pl.ds(pl.multiple_of((1 - ty) * half + j * chunk, chunk), chunk)
        mixed[:, at] = gate[:, at] * ygot[j].astype(F32)
    for j in range(half // width):
        at = pl.ds(pl.multiple_of((1 - ty) * half + j * width, width), width)
        value = res[(1 - ty) * (n_tp // 2) + j].astype(F32) + mixed[:, at]
        mixed[:, at] = value
        total1 = total1 + jnp.sum(value, axis=1, keepdims=True)
    mean = total1 * (1.0 / feats)
    variance = jnp.zeros((piece, 1), F32)
    for j in range(n_tp):
        at = slice(j * width, (j + 1) * width)
        centred = mixed[:, at] - mean
        mixed[:, at] = centred
        variance = variance + jnp.sum(centred * centred, axis=1, keepdims=True)
    inverse = lax.rsqrt(variance * (1.0 / feats) + 1e-06)
    flow = jnp.zeros((piece, HDIM), F32)
    for j in range(n_tp):
        at = slice(j * width, (j + 1) * width)
        normed = (mixed[:, at] * inverse * (1.0 + scale[:, at]) + shift[:, at]).astype(BF16)
        flow = flow + lax.dot_general(
            normed, proj_s[:, at], (((1,), (1,)), ((), ())), preferred_element_type=F32
        )
    flow_s[...] = flow
    even_rows = flow_s[pl.ds(0, piece // 2, stride=2), :]
    odd_rows = flow_s[pl.ds(1, piece // 2, stride=2), :]
    own_flow = even_rows + pltpu.roll(odd_rows, CH, 1)
    mine[...] = own_flow
    flows[group, col] = own_flow
    def flow_copy(k, g_slot, c_slot):
        g, c = plane_peer(k)
        return pltpu.make_async_remote_copy(
            src_ref=mine, dst_ref=flows.at[g_slot, c_slot],
            send_sem=flow_send.at[k], recv_sem=flow_recv.at[g_slot, c_slot],
            device_id={"cfg": g, "tp": c}, device_id_type=MESH,
        )

    def give_flow(k, carry):
        flow_copy(k, group, col).start()
        return carry

    lax.fori_loop(1, n_tp * n_cfg, give_flow, 0)

    pairs = rows // 2
    lane2 = lax.broadcasted_iota(jnp.int32, (pairs, HDIM), 1)
    row2 = me * rows + 2 * lax.broadcasted_iota(jnp.int32, (pairs, HDIM), 0) + (lane2 >= CH).astype(jnp.int32)
    request = pick(row2, ends, [jnp.int32(r) for r in range(NREQ)])
    image = (row2 - pick(row2, ends, [jnp.int32(0)] + ends[:-1])) >= TXT
    guide = pick(row2, ends, [guidance[r] for r in range(NREQ)])
    at_step = pick(row2, ends, [steps[r].astype(F32) for r in range(NREQ)])

    def sigma(u):
        remaining = 1.0 - u / STEPS
        return 3.0 * remaining / (1.0 + 2.0 * remaining)

    delta = sigma(at_step + 1.0) - sigma(at_step)

    def take_flow(k, carry):
        g, c = plane_peer(k)
        flow_copy(k, g, c).wait_recv()
        return carry

    lax.fori_loop(1, n_tp * n_cfg, take_flow, 0)

    cond = flows[0].reshape(pairs, HDIM)
    uncond = flows[1].reshape(pairs, HDIM)
    guided = uncond + guide * (cond - uncond)
    cond_square = jnp.where(image, cond * cond, 0.0)
    guided_square = jnp.where(image, guided * guided, 0.0)
    parts = []
    for square in (cond_square, guided_square):
        for r in range(NREQ):
            parts.append(jnp.sum(jnp.where(request == r, square, 0.0), axis=0, keepdims=True))
    stacked = jnp.sum(jnp.concatenate(parts, axis=0), axis=1, keepdims=True)
    diagonal = lax.broadcasted_iota(jnp.int32, (2 * NREQ, HDIM), 0) == lax.broadcasted_iota(jnp.int32, (2 * NREQ, HDIM), 1)
    own_sums = jnp.sum(jnp.where(diagonal, stacked, 0.0), axis=0, keepdims=True) + top_row
    row_s[...] = own_sums
    sums[me] = own_sums

    def sum_copy(k, dest_slot):
        return pltpu.make_async_remote_copy(
            src_ref=row_s, dst_ref=sums.at[dest_slot],
            send_sem=sum_send.at[k], recv_sem=sum_recv.at[dest_slot],
            device_id={"seq": seq_peer(k)}, device_id_type=MESH,
        )

    def give_sum(k, carry):
        sum_copy(k, me).start()
        return carry

    lax.fori_loop(1, n_seq, give_sum, 0)

    def take_sum(k, carry):
        sum_copy(k, seq_peer(k)).wait_recv()
        return carry

    lax.fori_loop(1, n_seq, take_sum, 0)

    total = sums[0]
    top = sums[0]
    for k in range(1, n_seq):
        total = total + sums[k]
        top = jnp.maximum(top, sums[k])
    tops_ref[...] = pltpu.roll(top, HDIM - 2 * NREQ, 1)[:, :heads]
    lane1 = lax.broadcasted_iota(jnp.int32, (1, HDIM), 1)
    entries = jnp.ones((1, HDIM), F32)
    for r in range(NREQ):
        entries = jnp.where(lane1 == r, counts[r].astype(F32) * CH, entries)
    guided_total = pltpu.roll(total, HDIM - NREQ, 1)
    factor = (PHI_MIX * jnp.sqrt(total / entries + 1e-06) + (1.0 - PHI_MIX)) / jnp.sqrt(guided_total / entries + 1e-06)
    factor_row = jnp.zeros((pairs, HDIM), F32)
    for r in range(NREQ):
        one = jnp.sum(jnp.where(lane1 == r, factor, 0.0), axis=1, keepdims=True)
        factor_row = jnp.where(request == r, one, factor_row)
    velocity = guided * jnp.where(image, factor_row, 0.0)
    stepped = latent_s[...] + delta * velocity
    for value, out in ((velocity, vel_ref), (stepped, next_ref)):
        value = jnp.where(group == 0, value, pltpu.roll(value, CH, 1))
        out[:, :HDIM] = value[:HDIM].T[:CH]
        out[:, HDIM:] = jnp.concatenate([value[HDIM:], value[HDIM:]], axis=0).T[:CH, : pairs - HDIM]

    def drain_tp(k, carry):
        res_copy(k, col).wait_send()
        for h in range(heads):
            att_copy(h, k, col).wait_send()
        return carry

    lax.fori_loop(1, n_tp, drain_tp, 0)

    def drain_flow(k, carry):
        flow_copy(k, group, col).wait_send()
        return carry

    lax.fori_loop(1, n_tp * n_cfg, drain_flow, 0)

    def drain_sum(k, carry):
        sum_copy(k, me).wait_send()
        return carry

    lax.fori_loop(1, n_seq, drain_sum, 0)

    def drain(h, carry):
        for d in range(1, reach):
            go_right(d, h, kv.at[h]).wait_send()
            go_left(d, h, kv.at[h]).wait_send()
        at_rim(lambda at: rim_right(h, at).wait_send(), lambda at: rim_left(h, at).wait_send())
        for dz in range(1 - reach, reach):
            share(dz, h, kv.at[h]).wait_send()
        share(give, h, kv.at[h]).wait_send()
        return carry

    lax.fori_loop(0, heads, drain, 0)
    for copy in w_out:
        copy.wait_send()
    for n in range(9):
        w_share(n).wait_send()
    for j in range(half // chunk):
        y_copy(j).wait_send()


def local(stream, qkv, q_gain, k_gain, w_out, mod, w_proj, latent, guidance, img_counts, img_widths, step_index):
    rows, width = stream.shape[1], stream.shape[2]
    feats = w_out.shape[1]
    heads = width // HDIM
    n_seq, n_tp, n_cfg = lax.axis_size("seq"), lax.axis_size("tp"), lax.axis_size("cfg")
    piece = rows // n_tp
    img_most = (rows * n_seq - NREQ * TXT) // 4
    longest = TXT + img_most
    reach = ((longest + rows - 2) // rows + 1) // 2
    rim = min(rows, -(-(longest - (2 * reach - 1) * rows - 1) // HDIM) * HDIM)
    vmem = pl.BlockSpec(memory_space=pltpu.VMEM)
    hbm = pl.BlockSpec(memory_space=pl.ANY)
    dma = pltpu.SemaphoreType.DMA
    pairs = rows // 2
    half = feats // 2
    chunk = 512
    vel, nxt, tops = pl.pallas_call(
        functools.partial(kernel, rim),
        out_shape=(
            jax.ShapeDtypeStruct((CH, pairs), F32),
            jax.ShapeDtypeStruct((CH, pairs), F32),
            jax.ShapeDtypeStruct((1, heads), F32),
        ),
        in_specs=[hbm] * 13,
        out_specs=(vmem,) * 3,
        scratch_shapes=[
            pltpu.SMEM((NREQ,), jnp.int32),
            pltpu.SMEM((NREQ,), jnp.int32),
            pltpu.SMEM((NREQ,), jnp.int32),
            pltpu.SMEM((NREQ,), F32),
            pltpu.VMEM((pairs, HDIM), F32),
            pltpu.VMEM((1, HDIM), F32),
            pltpu.VMEM((1, HDIM), F32),
            pltpu.VMEM((1, HDIM), F32),
            pltpu.VMEM((2, rows, width), BF16),
            pltpu.VMEM((heads, rows, HDIM), BF16),
            pltpu.VMEM((heads, 2, rows, HDIM), BF16),
            pltpu.VMEM((rows, HDIM), jnp.int32),
            pltpu.VMEM((n_seq, rows), jnp.int32),
            pltpu.VMEM((2 * reach + 1, 2, heads, 2, rows, HDIM), BF16),
            pltpu.VMEM((heads, rows, HDIM), F32),
            pltpu.VMEM((heads, rows, HDIM), F32),
            pltpu.VMEM((heads, rows, HDIM), F32),
            pltpu.VMEM((n_tp, rows, half), BF16),
            pltpu.VMEM((heads, rows, HDIM), BF16),
            pltpu.VMEM((heads, n_tp, 2 * piece, HDIM), BF16),
            pltpu.VMEM((2 * piece, half), F32),
            pltpu.VMEM((half // chunk, piece, chunk), BF16),
            pltpu.VMEM((half // chunk, piece, chunk), BF16),
            pltpu.VMEM((n_tp, piece, width), BF16),
            pltpu.VMEM((3, NREQ, feats), F32),
            pltpu.VMEM((HDIM, feats), BF16),
            pltpu.VMEM((piece, feats), F32),
            pltpu.VMEM((piece, feats), F32),
            pltpu.VMEM((piece, feats), F32),
            pltpu.VMEM((piece, feats), F32),
            pltpu.VMEM((piece, HDIM), F32),
            pltpu.VMEM((piece // 2, HDIM), F32),
            pltpu.VMEM((n_cfg, n_tp, piece // 2, HDIM), F32),
            pltpu.VMEM((1, HDIM), F32),
            pltpu.VMEM((n_seq, 1, HDIM), F32),
            dma((8,)),
            dma((6 + heads,)),
            dma((reach, heads)),
            dma((reach, heads)),
            dma((2 * reach + 1, heads)),
            dma((2 * reach + 1, 2, heads)),
            dma((9,)),
            dma((9,)),
            dma((9,)),
            dma((9,)),
            dma((heads, n_tp)),
            dma((heads, n_tp)),
            dma((half // chunk,)),
            dma((half // chunk,)),
            dma((n_tp,)),
            dma((n_tp,)),
            dma((n_tp * n_cfg,)),
            dma((n_cfg, n_tp)),
            dma((n_seq,)),
            dma((n_seq,)),
        ],
        compiler_params=pltpu.CompilerParams(collective_id=0, has_side_effects=True, vmem_limit_bytes=56 << 20),
        name="flow_step",
    )(
        img_counts, img_widths, step_index, guidance, jnp.transpose(qkv[0], (1, 0, 2)), w_out, stream[0],
        jnp.transpose(mod[0], (1, 0, 2)), w_proj, latent, jnp.asarray(frequency_row()),
        q_gain.reshape(1, HDIM), k_gain.reshape(1, HDIM),
    )
    return (vel.T, nxt.T, tops)


def solution(mesh):
    placed = (
        P("cfg", "seq", "tp"),
        P("cfg", "seq", None, "tp"),
        P(),
        P(),
        P("tp", None),
        P("cfg", None, None, None),
        P(),
        P("seq", None),
        P(),
        P(),
        P(),
        P(),
    )
    return jax.shard_map(
        local,
        mesh=mesh,
        in_specs=placed,
        out_specs=(P("seq", "cfg"), P("seq", "cfg"), P("cfg", "tp")),
        check_vma=False,
    )
```

```python
import functools
import math

import jax
import jax.numpy as jnp
import numpy as np
from jax import lax
from jax.experimental import pallas as pl
from jax.experimental.pallas import tpu as pltpu
from jax.sharding import PartitionSpec as P

MESH = pl.DeviceIdType.MESH
HDIM = 128
CH = 64
TXT = 128
STEPS = 8
NREQ = 8
PHI_MIX = 0.7
NEG = -1e30
SCALE = 1.0 / math.sqrt(float(HDIM))
EXP2_SCALE = SCALE * math.log2(math.e)
F32 = jnp.float32
BF16 = jnp.bfloat16


def frequency_row():
    pair_index = np.arange(64)
    axis_of = np.where(pair_index < 8, 0, np.where(pair_index < 36, 1, 2))
    axis_start = np.array([0, 8, 36])[axis_of]
    axis_width = np.array([16.0, 56.0, 56.0])[axis_of]
    frequency = 10000.0 ** (-2.0 * (pair_index - axis_start) / axis_width)
    return np.repeat(frequency, 2).astype(np.float32)[None, :]


def request_ends(counts):
    ends = []
    end = jnp.int32(0)
    for r in range(NREQ):
        end = end + (TXT + counts[r])
        ends.append(end)
    return ends


def pick(rows, ends, values):
    out = jnp.full(rows.shape, values[0])
    for r in range(NREQ - 1):
        out = jnp.where(rows >= ends[r], values[r + 1], out)
    return out


def kernel(
    rim,
    counts_ref, widths_ref, steps_ref, guidance_ref, qkv_ref, w_ref, stream_ref, mod_ref, proj_ref, latent_ref,
    freq_ref, qg_ref, kg_ref,
    vel_ref, next_ref, tops_ref,
    counts, widths, steps, guidance, latent_s, freq_s, qg_s, kg_s, qkv, q_s, kv, reqq, reqk, win, m_s, l_s, acc_s,
    wall, att_s, attx, made, yout, ygot,
    res, mod_s, proj_s, mixed, gate, scale, shift, flow_s, mine, flows, row_s, sums,
    first_sem, load_sem, right_sem, left_sem, share_sem, recv_sem, wsend, wrecv, wshare, wpartner,
    att_send, att_recv, y_send, y_recv, res_send, res_recv, flow_send, flow_recv, sum_send, sum_recv,
):
    n_tp, n_seq, n_cfg = lax.axis_size("tp"), lax.axis_size("seq"), lax.axis_size("cfg")
    group, me, col = lax.axis_index("cfg"), lax.axis_index("seq"), lax.axis_index("tp")
    heads, rows = q_s.shape[0], q_s.shape[1]
    width = heads * HDIM
    feats = w_ref.shape[1]
    half = feats // 2
    piece = rows // n_tp
    quarter = 2 * piece
    reach = win.shape[0] // 2
    chips = n_seq // 2
    chip, core = me // 2, me % 2
    other = 1 - core
    right = ((chip + 1) % chips) * 2 + core
    left = ((chip + chips - 1) % chips) * 2 + core
    partner = chip * 2 + other
    n_x = n_tp // 2
    tx, ty = col // 2, col % 2
    tiles = rows // HDIM
    barrier = pltpu.get_barrier_semaphore()

    def tp_peer(k):
        return (col + k) % n_tp

    def plane_peer(k):
        return (group + k // n_tp) % n_cfg, (col + k) % n_tp

    def seq_peer(k):
        return (me + k) % n_seq

    def hail_plane(k, carry):
        g, c = plane_peer(k)
        pl.semaphore_signal(barrier, inc=1, device_id={"cfg": g, "tp": c}, device_id_type=MESH)
        return carry

    lax.fori_loop(1, n_tp * n_cfg, hail_plane, 0)

    near_count = 4 * reach + 1

    def hail_seq(k, carry):
        peer = (2 * chip + 2 * n_seq - 2 * reach + k) % n_seq

        @pl.when(peer != me)
        def _():
            pl.semaphore_signal(barrier, inc=1, device_id={"seq": peer}, device_id_type=MESH)

        return carry

    lax.fori_loop(0, near_count + 1, hail_seq, 0)

    def remote(src, dst, send, recv, axis, peer):
        return pltpu.make_async_remote_copy(
            src_ref=src, dst_ref=dst, send_sem=send, recv_sem=recv,
            device_id={axis: peer}, device_id_type=MESH,
        )

    firsts = [
        pltpu.make_async_copy(source, target, first_sem.at[n])
        for n, (source, target) in enumerate(
            (
                (counts_ref, counts), (widths_ref, widths), (steps_ref, steps), (guidance_ref, guidance),
                (freq_ref, freq_s), (qg_ref, qg_s), (kg_ref, kg_s), (latent_ref, latent_s),
            )
        )
    ]
    for copy in firsts:
        copy.start()
    loads = [
        pltpu.make_async_copy(qkv_ref.at[1], qkv.at[1], load_sem.at[0]),
        pltpu.make_async_copy(qkv_ref.at[0], qkv.at[0], load_sem.at[1]),
        pltpu.make_async_copy(mod_ref, mod_s, load_sem.at[2]),
        pltpu.make_async_copy(proj_ref, proj_s.at[pl.ds(0, CH)], load_sem.at[3]),
        pltpu.make_async_copy(stream_ref.at[pl.ds(pl.multiple_of(col * piece, piece), piece)], res.at[col], load_sem.at[4]),
    ]
    for copy in loads:
        copy.start()
    values = [
        pltpu.make_async_copy(qkv_ref.at[2, :, pl.ds(h * HDIM, HDIM)], kv.at[h, 1], load_sem.at[5 + h]) for h in range(heads)
    ]
    for copy in values:
        copy.start()
    my_cols = pl.ds(pl.multiple_of(ty * half, half), half)
    near_cols = pl.ds(pl.multiple_of((1 - ty) * half, half), half)
    own_w = pltpu.make_async_copy(w_ref.at[:, my_cols], wall.at[col], load_sem.at[5 + heads])
    own_w.start()

    for copy in firsts:
        copy.wait()
    ends = request_ends(counts)
    starts = [jnp.int32(0)] + ends[:-1]
    ids = [jnp.int32(r) for r in range(NREQ)]
    row = me * rows + lax.broadcasted_iota(jnp.int32, (rows, HDIM), 0)
    start = pick(row, ends, starts)
    span = pick(row, ends, [widths[r].astype(F32) for r in range(NREQ)])
    pos = jnp.maximum(row - start - TXT, 0).astype(F32)
    height_id = jnp.floor((pos + 0.5) / span)
    width_id = pos - height_id * span
    lane = lax.broadcasted_iota(jnp.int32, (rows, HDIM), 1)
    angle = jnp.where(lane < 16, 0.0, jnp.where(lane < 72, height_id, width_id)) * freq_s[...]
    even = lane % 2 == 0
    cos = jnp.cos(angle)
    sin = jnp.sin(angle)
    sin = jnp.where(even, -sin, sin)

    def rotated(part, h, gain):
        x = qkv[part, :, h * HDIM : (h + 1) * HDIM].astype(F32)
        x = x * lax.rsqrt(jnp.mean(x * x, axis=-1, keepdims=True) + 1e-06) * gain
        mate = jnp.where(even, pltpu.roll(x, HDIM - 1, 1), pltpu.roll(x, 1, 1))
        return x * cos + mate * sin

    def make_key(h):
        key = rotated(1, h, kg_s[...])
        for b in range(tiles):
            at = slice(b * HDIM, (b + 1) * HDIM)
            kv[h, 0, at, :] = key[at].T.astype(BF16)

    loads[0].wait()
    make_key(0)
    for copy in values:
        copy.wait()

    def slot(dz, p, h):
        return win.at[dz + reach, p, h]

    def go_right(d, h, src):
        return remote(src, slot(-d, core, h), right_sem.at[d - 1, h], recv_sem.at[reach - d, core, h], "seq", right)

    def go_left(d, h, src):
        return remote(src, slot(d, core, h), left_sem.at[d - 1, h], recv_sem.at[reach + d, core, h], "seq", left)

    def share(dz, h, src):
        return remote(src, slot(dz, core, h), share_sem.at[dz + reach, h], recv_sem.at[dz + reach, core, h], "seq", partner)

    def landed(dz, p, h):
        remote(slot(dz, p, h), slot(dz, p, h), share_sem.at[0, 0], recv_sem.at[dz + reach, p, h], "seq", partner).wait_recv()

    cut = rows - rim
    whole, early, late = pl.ds(0, rows), pl.ds(0, rim), pl.ds(cut, rim)

    def rim_right(h, at):
        return remote(
            slot(1 - reach, core, h).at[:, at], slot(-reach, core, h).at[:, at],
            right_sem.at[reach - 1, h], recv_sem.at[0, core, h], "seq", right,
        )

    def rim_left(h, at):
        return remote(
            slot(reach - 1, core, h).at[:, at], slot(reach, core, h).at[:, at],
            left_sem.at[reach - 1, h], recv_sem.at[2 * reach, core, h], "seq", left,
        )

    def at_rim(right_op, left_op):
        @pl.when(core == 0)
        def _():
            right_op(late)
            left_op(whole)

        @pl.when(core == 1)
        def _():
            right_op(whole)
            left_op(early)

    def set_out(h):
        go_right(1, h, kv.at[h]).start()
        go_left(1, h, kv.at[h]).start()
        share(0, h, kv.at[h]).start()

    pl.semaphore_wait(barrier, n_tp * n_cfg - 1 + near_count)
    set_out(0)
    make_key(1)
    set_out(1)
    make_key(2)
    set_out(2)

    x_next = ((tx + 1) % n_x) * 2 + ty
    x_prev = ((tx + n_x - 1) % n_x) * 2 + ty
    y_peer = tx * 2 + 1 - ty
    far_x = ((tx + 2) % n_x) * 2
    core_rows = pl.ds(pl.multiple_of(core * 2 * quarter, 2 * quarter), 2 * quarter)
    low_rows = pl.ds(pl.multiple_of(core * 2 * quarter, quarter), quarter)
    high_rows = pl.ds(pl.multiple_of(core * 2 * quarter + quarter, quarter), quarter)
    mate_rows = pl.ds(pl.multiple_of(other * 2 * quarter, 2 * quarter), 2 * quarter)
    mate_low = pl.ds(pl.multiple_of(other * 2 * quarter, quarter), quarter)
    mate_high = pl.ds(pl.multiple_of(other * 2 * quarter + quarter, quarter), quarter)

    def w_at(source, part):
        return wall.at[source, part]

    prev_own, prev_near = x_prev, (x_prev // 2) * 2 + 1 - ty
    next_own, next_near = x_next, (x_next // 2) * 2 + 1 - ty
    far_own, far_near = far_x + ty, far_x + 1 - ty
    pieces = [
        (y_peer, core_rows, mate_rows),
        (prev_own, core_rows, mate_rows),
        (prev_near, core_rows, mate_rows),
        (next_own, core_rows, mate_rows),
        (next_near, core_rows, mate_rows),
        (far_own, low_rows, mate_low),
        (far_near, low_rows, mate_low),
        (far_own, high_rows, mate_high),
        (far_near, high_rows, mate_high),
    ]

    def w_sends():
        own = w_ref.at[core_rows, my_cols]
        near = w_at(y_peer, core_rows)
        return [
            remote(w_ref.at[core_rows, near_cols], w_at(col, core_rows), wsend.at[0], wrecv.at[0], "tp", y_peer),
            remote(own, w_at(col, core_rows), wsend.at[1], wrecv.at[1], "tp", x_next),
            remote(own, w_at(col, core_rows), wsend.at[3], wrecv.at[3], "tp", x_prev),
            remote(near, near, wsend.at[2], wrecv.at[2], "tp", x_next),
            remote(near, near, wsend.at[4], wrecv.at[4], "tp", x_prev),
            remote(w_at(prev_own, low_rows), w_at(prev_own, low_rows), wsend.at[5], wrecv.at[5], "tp", x_next),
            remote(w_at(next_own, high_rows), w_at(next_own, high_rows), wsend.at[7], wrecv.at[7], "tp", x_prev),
            remote(w_at(prev_near, low_rows), w_at(prev_near, low_rows), wsend.at[6], wrecv.at[6], "tp", x_next),
            remote(w_at(next_near, high_rows), w_at(next_near, high_rows), wsend.at[8], wrecv.at[8], "tp", x_prev),
        ]

    w_out = w_sends()

    def w_share(n):
        source, part, _ = pieces[n]
        return remote(w_at(source, part), w_at(source, part), wshare.at[n], wpartner.at[n], "seq", partner)

    def w_landed(n):
        source, part, _ = pieces[n]
        remote(w_at(source, part), w_at(source, part), wshare.at[n], wrecv.at[n], "tp", y_peer).wait_recv()

    def w_shared(n):
        source, _, part = pieces[n]
        remote(w_at(source, part), w_at(source, part), wshare.at[n], wpartner.at[n], "seq", partner).wait_recv()

    for n in (0, 1, 2):
        w_out[n].start()

    def res_copy(k, dest_slot):
        c = tp_peer(k)
        return remote(
            stream_ref.at[pl.ds(pl.multiple_of(c * piece, piece), piece)], res.at[dest_slot],
            res_send.at[k], res_recv.at[dest_slot], "tp", c,
        )

    def give_res(k, carry):
        res_copy(k, col).start()
        return carry

    lax.fori_loop(1, n_tp, give_res, 0)

    loads[1].wait()
    for h in range(heads):
        q_s[h] = rotated(0, h, qg_s[...]).astype(BF16)
    reqq[...] = pick(row, ends, ids)
    every = lax.broadcasted_iota(jnp.int32, (n_seq, rows), 0) * rows + lax.broadcasted_iota(jnp.int32, (n_seq, rows), 1)
    reqk[...] = pick(every, ends, ids)

    def wide(x):
        return jnp.concatenate([x] * tiles, axis=1)

    def update(h, blocks):
        q = q_s[h]
        asked = wide(reqq[...])
        scores = []
        for ref, source in blocks:
            keys = jnp.concatenate([ref[0, b * HDIM : (b + 1) * HDIM, :] for b in range(tiles)], axis=1)
            s = jnp.dot(q, keys, preferred_element_type=F32)
            scores.append(jnp.where(asked == reqk[pl.ds(source, 1), :], s, NEG))
        best = functools.reduce(jnp.maximum, scores)
        m_old = m_s[h]
        m_new = jnp.maximum(m_old, jnp.max(best, axis=1, keepdims=True))
        shrink = jnp.exp2((m_old - m_new) * EXP2_SCALE)
        m_wide = wide(m_new)
        total = None
        acc = acc_s[h] * shrink
        for (ref, source), s in zip(blocks, scores):
            p = jnp.exp2((s - m_wide) * EXP2_SCALE)
            total = p if total is None else total + p
            acc = acc + jnp.dot(p.astype(BF16), ref[1], preferred_element_type=F32)
        l_s[h] = l_s[h] * shrink + jnp.sum(total, axis=1, keepdims=True)
        acc_s[h] = acc
        m_s[h] = m_new

    def block_of(dz, p):
        return ((chip + dz + chips) % chips) * 2 + p

    def own(h, carry):
        blank = jnp.zeros((2, cut, HDIM), BF16)

        @pl.when(core == 0)
        def _():
            win[0, 0, h, :, pl.ds(0, cut), :] = blank

        @pl.when(core == 1)
        def _():
            win[2 * reach, 1, h, :, pl.ds(rim, cut), :] = blank

        m_s[h] = jnp.full((rows, HDIM), NEG, F32)
        l_s[h] = jnp.zeros((rows, HDIM), F32)
        acc_s[h] = jnp.zeros((rows, HDIM), F32)
        update(h, [(kv.at[h], me)])
        return carry

    lax.fori_loop(0, heads, own, 0)

    loads[2].wait()
    chunk = 512
    token = me * rows + col * piece + lax.broadcasted_iota(jnp.int32, (piece, chunk), 0)

    def pick_rows(j, carry):
        at = pl.ds(pl.multiple_of(j * chunk, chunk), chunk)
        for which, out in ((0, gate), (1, scale), (2, shift)):
            value = jnp.broadcast_to(mod_s[which, 0:1, at], (piece, chunk))
            for r in range(NREQ - 1):
                value = jnp.where(token >= ends[r], mod_s[which, r + 1 : r + 2, at], value)
            out[:, at] = value
        return carry

    lax.fori_loop(0, feats // chunk, pick_rows, 0)

    give = reach - 2 * reach * core
    take = -give

    def pair(d, p, h):
        return [(slot(-d, p, h), block_of(-d, p)), (slot(d, p, h), block_of(d, p))]

    def att_copy(h, k, dest_slot):
        c = tp_peer(k)
        return remote(
            att_s.at[h, pl.ds(pl.multiple_of((c // 2) * quarter, quarter), quarter)], attx.at[h, dest_slot],
            att_send.at[h, k], att_recv.at[h, dest_slot], "tp", c,
        )

    def give_att(h):
        att_s[h] = (acc_s[h] / l_s[h]).astype(BF16)

        def one(k, carry):
            att_copy(h, k, col).start()
            return carry

        lax.fori_loop(1, n_tp, one, 0)
        attx[h, col] = att_s[h, pl.ds(pl.multiple_of(tx * quarter, quarter), quarter), :]

    def take_att(h):
        def one(k, carry):
            att_copy(h, k, tp_peer(k)).wait_recv()
            return carry

        lax.fori_loop(1, n_tp, one, 0)

    def product(h, at):
        left_side = jnp.concatenate([attx[h, k] for k in range(n_tp)], axis=1)
        weights = wall[:, h * HDIM : (h + 1) * HDIM, at].reshape(n_tp * HDIM, chunk)
        return jnp.dot(left_side, weights, preferred_element_type=F32)

    def step(i, carry):
        d, h = 1 + i // heads, i % heads
        d_last, h_last = 1 + (i + heads - 1) // heads - 1, (i + heads - 1) % heads

        @pl.when(i == 3)
        def _():
            w_landed(0)
            w_out[3].start()
            w_out[4].start()
            w_landed(1)
            w_out[5].start()
            w_landed(3)
            w_out[6].start()
            for n in (0, 1, 3):
                w_share(n).start()

        @pl.when(i == 7)
        def _():
            w_landed(2)
            w_out[7].start()
            w_landed(4)
            w_out[8].start()
            for n in (2, 4):
                w_share(n).start()

        @pl.when(i == 9)
        def _():
            for n in (5, 7):
                w_landed(n)
                w_share(n).start()

        @pl.when(d < reach - 1)
        def _():
            landed(-d, core, h)
            go_right(d + 1, h, slot(-d, core, h)).start()
            landed(d, core, h)
            go_left(d + 1, h, slot(d, core, h)).start()

        @pl.when(d == reach - 1)
        def _():
            landed(-d, core, h)
            landed(d, core, h)
            at_rim(lambda at: rim_right(h, at).start(), lambda at: rim_left(h, at).start())

        @pl.when(d < reach)
        def _():
            share(-d, h, slot(-d, core, h)).start()
            share(d, h, slot(d, core, h)).start()

        @pl.when(d == reach)
        def _():
            at_rim(lambda at: rim_right(h, at).wait_recv(), lambda at: rim_left(h, at).wait_recv())
            share(give, h, slot(give, core, h)).start()

        update(h, pair(d, core, h))

        @pl.when((i > 0) & (d_last < reach))
        def _():
            landed(-d_last, other, h_last)
            landed(d_last, other, h_last)
            update(h_last, pair(d_last, other, h_last))

        @pl.when(((i > 0) & (i < 4)) | (d_last == reach))
        def _():
            near = (d_last != reach).astype(jnp.int32)
            dz = (1 - near) * take
            hh = near * (i - 1) + (1 - near) * h_last
            landed(dz, other, hh)
            update(hh, [(slot(dz, other, hh), block_of(dz, other))])

        @pl.when(i == 10)
        def _():
            for n in (6, 8):
                w_landed(n)
                w_share(n).start()

        for done in range(heads - 1):

            @pl.when(i == heads * (reach - 1) + done + 1)
            def _():
                give_att(done)

        return carry

    lax.fori_loop(0, heads * reach, step, 0)

    landed(take, other, heads - 1)
    update(heads - 1, [(slot(take, other, heads - 1), block_of(take, other))])
    give_att(heads - 1)
    own_w.wait()
    for n in range(9):
        w_shared(n)
    take_att(0)
    take_att(1)

    def early_product(j, carry):
        at = pl.ds(pl.multiple_of(j * chunk, chunk), chunk)
        made[:, at] = product(0, at) + product(1, at)
        return carry

    lax.fori_loop(0, half // chunk, early_product, 0)

    lane8 = lax.broadcasted_iota(jnp.int32, (1, HDIM), 1)
    top_row = jnp.zeros((1, HDIM), F32)
    for h in range(heads):
        top = jnp.max(jnp.max(m_s[h], axis=0, keepdims=True), axis=1, keepdims=True) * SCALE
        top_row = jnp.where(lane8 == 2 * NREQ + h, top, top_row)

    loads[3].wait()
    proj_s[pl.ds(CH, HDIM - CH), :] = jnp.zeros((HDIM - CH, feats), BF16)
    loads[4].wait()

    def take_res(k, carry):
        res_copy(k, tp_peer(k)).wait_recv()
        return carry

    lax.fori_loop(1, n_tp, take_res, 0)
    take_att(2)

    def y_copy(j):
        return remote(yout.at[j], ygot.at[j], y_send.at[j], y_recv.at[j], "tp", y_peer)

    keep = pl.ds(pl.multiple_of(ty * piece, piece), piece)
    pass_on = pl.ds(pl.multiple_of((1 - ty) * piece, piece), piece)

    def last_product(j, carry):
        at = pl.ds(pl.multiple_of(j * chunk, chunk), chunk)
        made[:, at] = made[:, at] + product(2, at)
        yout[j] = made[pass_on, at].astype(BF16)
        y_copy(j).start()
        return carry

    lax.fori_loop(0, half // chunk, last_product, 0)

    total1 = jnp.zeros((piece, 1), F32)
    for j in range(half // width):
        at = pl.ds(pl.multiple_of(ty * half + j * width, width), width)
        value = res[ty * (n_tp // 2) + j].astype(F32) + gate[:, at] * made[keep, j * width : (j + 1) * width]
        mixed[:, at] = value
        total1 = total1 + jnp.sum(value, axis=1, keepdims=True)
    for j in range(half // chunk):
        y_copy(j).wait_recv()
        at = pl.ds(pl.multiple_of((1 - ty) * half + j * chunk, chunk), chunk)
        mixed[:, at] = gate[:, at] * ygot[j].astype(F32)
    for j in range(half // width):
        at = pl.ds(pl.multiple_of((1 - ty) * half + j * width, width), width)
        value = res[(1 - ty) * (n_tp // 2) + j].astype(F32) + mixed[:, at]
        mixed[:, at] = value
        total1 = total1 + jnp.sum(value, axis=1, keepdims=True)
    mean = total1 * (1.0 / feats)
    variance = jnp.zeros((piece, 1), F32)
    for j in range(n_tp):
        at = slice(j * width, (j + 1) * width)
        centred = mixed[:, at] - mean
        mixed[:, at] = centred
        variance = variance + jnp.sum(centred * centred, axis=1, keepdims=True)
    inverse = lax.rsqrt(variance * (1.0 / feats) + 1e-06)
    flow = jnp.zeros((piece, HDIM), F32)
    for j in range(n_tp):
        at = slice(j * width, (j + 1) * width)
        normed = (mixed[:, at] * inverse * (1.0 + scale[:, at]) + shift[:, at]).astype(BF16)
        flow = flow + lax.dot_general(
            normed, proj_s[:, at], (((1,), (1,)), ((), ())), preferred_element_type=F32
        )
    flow_s[...] = flow
    even_rows = flow_s[pl.ds(0, piece // 2, stride=2), :]
    odd_rows = flow_s[pl.ds(1, piece // 2, stride=2), :]
    own_flow = even_rows + pltpu.roll(odd_rows, CH, 1)
    mine[...] = own_flow
    flows[group, col] = own_flow
    def flow_copy(k, g_slot, c_slot):
        g, c = plane_peer(k)
        return pltpu.make_async_remote_copy(
            src_ref=mine, dst_ref=flows.at[g_slot, c_slot],
            send_sem=flow_send.at[k], recv_sem=flow_recv.at[g_slot, c_slot],
            device_id={"cfg": g, "tp": c}, device_id_type=MESH,
        )

    def give_flow(k, carry):
        flow_copy(k, group, col).start()
        return carry

    lax.fori_loop(1, n_tp * n_cfg, give_flow, 0)

    pairs = rows // 2
    lane2 = lax.broadcasted_iota(jnp.int32, (pairs, HDIM), 1)
    row2 = me * rows + 2 * lax.broadcasted_iota(jnp.int32, (pairs, HDIM), 0) + (lane2 >= CH).astype(jnp.int32)
    request = pick(row2, ends, [jnp.int32(r) for r in range(NREQ)])
    image = (row2 - pick(row2, ends, [jnp.int32(0)] + ends[:-1])) >= TXT
    guide = pick(row2, ends, [guidance[r] for r in range(NREQ)])
    at_step = pick(row2, ends, [steps[r].astype(F32) for r in range(NREQ)])

    def sigma(u):
        remaining = 1.0 - u / STEPS
        return 3.0 * remaining / (1.0 + 2.0 * remaining)

    delta = sigma(at_step + 1.0) - sigma(at_step)

    def take_flow(k, carry):
        g, c = plane_peer(k)
        flow_copy(k, g, c).wait_recv()
        return carry

    lax.fori_loop(1, n_tp * n_cfg, take_flow, 0)

    cond = flows[0].reshape(pairs, HDIM)
    uncond = flows[1].reshape(pairs, HDIM)
    guided = uncond + guide * (cond - uncond)
    cond_square = jnp.where(image, cond * cond, 0.0)
    guided_square = jnp.where(image, guided * guided, 0.0)
    parts = []
    for square in (cond_square, guided_square):
        for r in range(NREQ):
            parts.append(jnp.sum(jnp.where(request == r, square, 0.0), axis=0, keepdims=True))
    stacked = jnp.sum(jnp.concatenate(parts, axis=0), axis=1, keepdims=True)
    diagonal = lax.broadcasted_iota(jnp.int32, (2 * NREQ, HDIM), 0) == lax.broadcasted_iota(jnp.int32, (2 * NREQ, HDIM), 1)
    own_sums = jnp.sum(jnp.where(diagonal, stacked, 0.0), axis=0, keepdims=True) + top_row
    row_s[...] = own_sums
    sums[me] = own_sums

    def sum_copy(k, dest_slot):
        return pltpu.make_async_remote_copy(
            src_ref=row_s, dst_ref=sums.at[dest_slot],
            send_sem=sum_send.at[k], recv_sem=sum_recv.at[dest_slot],
            device_id={"seq": seq_peer(k)}, device_id_type=MESH,
        )

    def give_sum(k, carry):
        sum_copy(k, me).start()
        return carry

    lax.fori_loop(1, n_seq, give_sum, 0)

    def take_sum(k, carry):
        sum_copy(k, seq_peer(k)).wait_recv()
        return carry

    lax.fori_loop(1, n_seq, take_sum, 0)

    total = sums[0]
    top = sums[0]
    for k in range(1, n_seq):
        total = total + sums[k]
        top = jnp.maximum(top, sums[k])
    tops_ref[...] = pltpu.roll(top, HDIM - 2 * NREQ, 1)[:, :heads]
    lane1 = lax.broadcasted_iota(jnp.int32, (1, HDIM), 1)
    entries = jnp.ones((1, HDIM), F32)
    for r in range(NREQ):
        entries = jnp.where(lane1 == r, counts[r].astype(F32) * CH, entries)
    guided_total = pltpu.roll(total, HDIM - NREQ, 1)
    factor = (PHI_MIX * jnp.sqrt(total / entries + 1e-06) + (1.0 - PHI_MIX)) / jnp.sqrt(guided_total / entries + 1e-06)
    factor_row = jnp.zeros((pairs, HDIM), F32)
    for r in range(NREQ):
        one = jnp.sum(jnp.where(lane1 == r, factor, 0.0), axis=1, keepdims=True)
        factor_row = jnp.where(request == r, one, factor_row)
    velocity = guided * jnp.where(image, factor_row, 0.0)
    stepped = latent_s[...] + delta * velocity
    for value, out in ((velocity, vel_ref), (stepped, next_ref)):
        value = jnp.where(group == 0, value, pltpu.roll(value, CH, 1))
        out[:, :HDIM] = value[:HDIM].T[:CH]
        out[:, HDIM:] = jnp.concatenate([value[HDIM:], value[HDIM:]], axis=0).T[:CH, : pairs - HDIM]

    def drain_tp(k, carry):
        res_copy(k, col).wait_send()
        for h in range(heads):
            att_copy(h, k, col).wait_send()
        return carry

    lax.fori_loop(1, n_tp, drain_tp, 0)

    def drain_flow(k, carry):
        flow_copy(k, group, col).wait_send()
        return carry

    lax.fori_loop(1, n_tp * n_cfg, drain_flow, 0)

    def drain_sum(k, carry):
        sum_copy(k, me).wait_send()
        return carry

    lax.fori_loop(1, n_seq, drain_sum, 0)

    def drain(h, carry):
        for d in range(1, reach):
            go_right(d, h, kv.at[h]).wait_send()
            go_left(d, h, kv.at[h]).wait_send()
        at_rim(lambda at: rim_right(h, at).wait_send(), lambda at: rim_left(h, at).wait_send())
        for dz in range(1 - reach, reach):
            share(dz, h, kv.at[h]).wait_send()
        share(give, h, kv.at[h]).wait_send()
        return carry

    lax.fori_loop(0, heads, drain, 0)
    for copy in w_out:
        copy.wait_send()
    for n in range(9):
        w_share(n).wait_send()
    for j in range(half // chunk):
        y_copy(j).wait_send()


def local(stream, qkv, q_gain, k_gain, w_out, mod, w_proj, latent, guidance, img_counts, img_widths, step_index):
    rows, width = stream.shape[1], stream.shape[2]
    feats = w_out.shape[1]
    heads = width // HDIM
    n_seq, n_tp, n_cfg = lax.axis_size("seq"), lax.axis_size("tp"), lax.axis_size("cfg")
    piece = rows // n_tp
    img_most = (rows * n_seq - NREQ * TXT) // 4
    longest = TXT + img_most
    reach = ((longest + rows - 2) // rows + 1) // 2
    rim = min(rows, -(-(longest - (2 * reach - 1) * rows - 1) // HDIM) * HDIM)
    vmem = pl.BlockSpec(memory_space=pltpu.VMEM)
    hbm = pl.BlockSpec(memory_space=pltpu.HBM)
    dma = pltpu.SemaphoreType.DMA
    pairs = rows // 2
    half = feats // 2
    chunk = 512
    vel, nxt, tops = pl.pallas_call(
        functools.partial(kernel, rim),
        out_shape=(
            jax.ShapeDtypeStruct((CH, pairs), F32),
            jax.ShapeDtypeStruct((CH, pairs), F32),
            jax.ShapeDtypeStruct((1, heads), F32),
        ),
        in_specs=[hbm] * 13,
        out_specs=(vmem,) * 3,
        scratch_shapes=[
            pltpu.SMEM((NREQ,), jnp.int32),
            pltpu.SMEM((NREQ,), jnp.int32),
            pltpu.SMEM((NREQ,), jnp.int32),
            pltpu.SMEM((NREQ,), F32),
            pltpu.VMEM((pairs, HDIM), F32),
            pltpu.VMEM((1, HDIM), F32),
            pltpu.VMEM((1, HDIM), F32),
            pltpu.VMEM((1, HDIM), F32),
            pltpu.VMEM((2, rows, width), BF16),
            pltpu.VMEM((heads, rows, HDIM), BF16),
            pltpu.VMEM((heads, 2, rows, HDIM), BF16),
            pltpu.VMEM((rows, HDIM), jnp.int32),
            pltpu.VMEM((n_seq, rows), jnp.int32),
            pltpu.VMEM((2 * reach + 1, 2, heads, 2, rows, HDIM), BF16),
            pltpu.VMEM((heads, rows, HDIM), F32),
            pltpu.VMEM((heads, rows, HDIM), F32),
            pltpu.VMEM((heads, rows, HDIM), F32),
            pltpu.VMEM((n_tp, rows, half), BF16),
            pltpu.VMEM((heads, rows, HDIM), BF16),
            pltpu.VMEM((heads, n_tp, 2 * piece, HDIM), BF16),
            pltpu.VMEM((2 * piece, half), F32),
            pltpu.VMEM((half // chunk, piece, chunk), BF16),
            pltpu.VMEM((half // chunk, piece, chunk), BF16),
            pltpu.VMEM((n_tp, piece, width), BF16),
            pltpu.VMEM((3, NREQ, feats), F32),
            pltpu.VMEM((HDIM, feats), BF16),
            pltpu.VMEM((piece, feats), F32),
            pltpu.VMEM((piece, feats), F32),
            pltpu.VMEM((piece, feats), F32),
            pltpu.VMEM((piece, feats), F32),
            pltpu.VMEM((piece, HDIM), F32),
            pltpu.VMEM((piece // 2, HDIM), F32),
            pltpu.VMEM((n_cfg, n_tp, piece // 2, HDIM), F32),
            pltpu.VMEM((1, HDIM), F32),
            pltpu.VMEM((n_seq, 1, HDIM), F32),
            dma((8,)),
            dma((6 + heads,)),
            dma((reach, heads)),
            dma((reach, heads)),
            dma((2 * reach + 1, heads)),
            dma((2 * reach + 1, 2, heads)),
            dma((9,)),
            dma((9,)),
            dma((9,)),
            dma((9,)),
            dma((heads, n_tp)),
            dma((heads, n_tp)),
            dma((half // chunk,)),
            dma((half // chunk,)),
            dma((n_tp,)),
            dma((n_tp,)),
            dma((n_tp * n_cfg,)),
            dma((n_cfg, n_tp)),
            dma((n_seq,)),
            dma((n_seq,)),
        ],
        compiler_params=pltpu.CompilerParams(collective_id=0, has_side_effects=True, vmem_limit_bytes=38 << 20),
        name="flow_step",
    )(*(pltpu.with_memory_space_constraint(x, pltpu.HBM) for x in (
        img_counts, img_widths, step_index, guidance, jnp.transpose(qkv[0], (1, 0, 2)), w_out, stream[0],
        jnp.transpose(mod[0], (1, 0, 2)), w_proj, latent, jnp.asarray(frequency_row()),
        q_gain.reshape(1, HDIM), k_gain.reshape(1, HDIM),
    )))
    return (vel.T, nxt.T, tops)


def solution(mesh):
    placed = (
        P("cfg", "seq", "tp"),
        P("cfg", "seq", None, "tp"),
        P(),
        P(),
        P("tp", None),
        P("cfg", None, None, None),
        P(),
        P("seq", None),
        P(),
        P(),
        P(),
        P(),
    )
    return jax.shard_map(
        local,
        mesh=mesh,
        in_specs=placed,
        out_specs=(P("seq", "cfg"), P("seq", "cfg"), P("cfg", "tp")),
        check_vma=False,
    )
```

```python
import functools
import math

import jax
import jax.numpy as jnp
import numpy as np
from jax import lax
from jax.experimental import pallas as pl
from jax.experimental.pallas import tpu as pltpu
from jax.sharding import PartitionSpec as P

MESH = pl.DeviceIdType.MESH
HDIM = 128
CH = 64
TXT = 128
STEPS = 8
NREQ = 8
PHI_MIX = 0.7
NEG = -1e30
SCALE = 1.0 / math.sqrt(float(HDIM))
EXP2_SCALE = SCALE * math.log2(math.e)
F32 = jnp.float32
BF16 = jnp.bfloat16


def frequency_row():
    pair_index = np.arange(64)
    axis_of = np.where(pair_index < 8, 0, np.where(pair_index < 36, 1, 2))
    axis_start = np.array([0, 8, 36])[axis_of]
    axis_width = np.array([16.0, 56.0, 56.0])[axis_of]
    frequency = 10000.0 ** (-2.0 * (pair_index - axis_start) / axis_width)
    return np.repeat(frequency, 2).astype(np.float32)[None, :]


def request_ends(counts):
    ends = []
    end = jnp.int32(0)
    for r in range(NREQ):
        end = end + (TXT + counts[r])
        ends.append(end)
    return ends


def pick(rows, ends, values):
    out = jnp.full(rows.shape, values[0])
    for r in range(NREQ - 1):
        out = jnp.where(rows >= ends[r], values[r + 1], out)
    return out


def kernel(
    rim,
    counts_ref, widths_ref, steps_ref, guidance_ref, qkv_ref, w_ref, stream_ref, mod_ref, proj_ref, latent_ref,
    freq_ref, qg_ref, kg_ref,
    vel_ref, next_ref, tops_ref,
    counts, widths, steps, guidance, latent_s, freq_s, qg_s, kg_s, qkv, q_s, kv, reqq, reqk, win, m_s, l_s, acc_s,
    wall, att_s, attx, made, yout, ygot,
    res, mod_s, proj_s, mixed, gate, scale, shift, flow_s, mine, flows, row_s, sums,
    first_sem, load_sem, right_sem, left_sem, share_sem, recv_sem, wsend, wrecv, wshare, wpartner,
    att_send, att_recv, y_send, y_recv, res_send, res_recv, flow_send, flow_recv, sum_send, sum_recv,
):
    n_tp, n_seq, n_cfg = lax.axis_size("tp"), lax.axis_size("seq"), lax.axis_size("cfg")
    group, me, col = lax.axis_index("cfg"), lax.axis_index("seq"), lax.axis_index("tp")
    heads, rows = q_s.shape[0], q_s.shape[1]
    width = heads * HDIM
    feats = w_ref.shape[1]
    half = feats // 2
    piece = rows // n_tp
    quarter = 2 * piece
    reach = win.shape[0] // 2
    chips = n_seq // 2
    chip, core = me // 2, me % 2
    other = 1 - core
    right = ((chip + 1) % chips) * 2 + core
    left = ((chip + chips - 1) % chips) * 2 + core
    partner = chip * 2 + other
    n_x = n_tp // 2
    tx, ty = col // 2, col % 2
    tiles = rows // HDIM
    barrier = pltpu.get_barrier_semaphore()

    def tp_peer(k):
        return (col + k) % n_tp

    def plane_peer(k):
        return (group + k // n_tp) % n_cfg, (col + k) % n_tp

    def seq_peer(k):
        return (me + k) % n_seq

    def hail_plane(k, carry):
        g, c = plane_peer(k)
        pl.semaphore_signal(barrier, inc=1, device_id={"cfg": g, "tp": c}, device_id_type=MESH)
        return carry

    lax.fori_loop(1, n_tp * n_cfg, hail_plane, 0)

    near_count = 4 * reach + 1

    def hail_seq(k, carry):
        peer = (2 * chip + 2 * n_seq - 2 * reach + k) % n_seq

        @pl.when(peer != me)
        def _():
            pl.semaphore_signal(barrier, inc=1, device_id={"seq": peer}, device_id_type=MESH)

        return carry

    lax.fori_loop(0, near_count + 1, hail_seq, 0)

    def remote(src, dst, send, recv, axis, peer):
        return pltpu.make_async_remote_copy(
            src_ref=src, dst_ref=dst, send_sem=send, recv_sem=recv,
            device_id={axis: peer}, device_id_type=MESH,
        )

    firsts = [
        pltpu.make_async_copy(source, target, first_sem.at[n])
        for n, (source, target) in enumerate(
            (
                (counts_ref, counts), (widths_ref, widths), (steps_ref, steps), (guidance_ref, guidance),
                (freq_ref, freq_s), (qg_ref, qg_s), (kg_ref, kg_s), (latent_ref, latent_s),
            )
        )
    ]
    for copy in firsts:
        copy.start()
    loads = [
        pltpu.make_async_copy(qkv_ref.at[1], qkv.at[1], load_sem.at[0]),
        pltpu.make_async_copy(qkv_ref.at[0], qkv.at[0], load_sem.at[1]),
        pltpu.make_async_copy(mod_ref, mod_s, load_sem.at[2]),
        pltpu.make_async_copy(proj_ref, proj_s.at[pl.ds(0, CH)], load_sem.at[3]),
        pltpu.make_async_copy(stream_ref.at[pl.ds(pl.multiple_of(col * piece, piece), piece)], res.at[col], load_sem.at[4]),
    ]
    for copy in loads:
        copy.start()
    values = [
        pltpu.make_async_copy(qkv_ref.at[2, :, pl.ds(h * HDIM, HDIM)], kv.at[h, 1], load_sem.at[5 + h]) for h in range(heads)
    ]
    for copy in values:
        copy.start()
    my_cols = pl.ds(pl.multiple_of(ty * half, half), half)
    near_cols = pl.ds(pl.multiple_of((1 - ty) * half, half), half)
    own_w = pltpu.make_async_copy(w_ref.at[:, my_cols], wall.at[col], load_sem.at[5 + heads])
    own_w.start()

    for copy in firsts:
        copy.wait()
    ends = request_ends(counts)
    starts = [jnp.int32(0)] + ends[:-1]
    ids = [jnp.int32(r) for r in range(NREQ)]
    row = me * rows + lax.broadcasted_iota(jnp.int32, (rows, HDIM), 0)
    start = pick(row, ends, starts)
    span = pick(row, ends, [widths[r].astype(F32) for r in range(NREQ)])
    pos = jnp.maximum(row - start - TXT, 0).astype(F32)
    height_id = jnp.floor((pos + 0.5) / span)
    width_id = pos - height_id * span
    lane = lax.broadcasted_iota(jnp.int32, (rows, HDIM), 1)
    angle = jnp.where(lane < 16, 0.0, jnp.where(lane < 72, height_id, width_id)) * freq_s[...]
    even = lane % 2 == 0
    cos = jnp.cos(angle)
    sin = jnp.sin(angle)
    sin = jnp.where(even, -sin, sin)

    def rotated(part, h, gain):
        x = qkv[part, :, h * HDIM : (h + 1) * HDIM].astype(F32)
        x = x * lax.rsqrt(jnp.mean(x * x, axis=-1, keepdims=True) + 1e-06) * gain
        mate = jnp.where(even, pltpu.roll(x, HDIM - 1, 1), pltpu.roll(x, 1, 1))
        return x * cos + mate * sin

    def make_key(h):
        key = rotated(1, h, kg_s[...])
        for b in range(tiles):
            at = slice(b * HDIM, (b + 1) * HDIM)
            kv[h, 0, at, :] = key[at].T.astype(BF16)

    loads[0].wait()
    make_key(0)
    for copy in values:
        copy.wait()

    def slot(dz, p, h):
        return win.at[dz + reach, p, h]

    def go_right(d, h, src):
        return remote(src, slot(-d, core, h), right_sem.at[d - 1, h], recv_sem.at[reach - d, core, h], "seq", right)

    def go_left(d, h, src):
        return remote(src, slot(d, core, h), left_sem.at[d - 1, h], recv_sem.at[reach + d, core, h], "seq", left)

    def share(dz, h, src):
        return remote(src, slot(dz, core, h), share_sem.at[dz + reach, h], recv_sem.at[dz + reach, core, h], "seq", partner)

    def landed(dz, p, h):
        remote(slot(dz, p, h), slot(dz, p, h), share_sem.at[0, 0], recv_sem.at[dz + reach, p, h], "seq", partner).wait_recv()

    cut = rows - rim
    whole, early, late = pl.ds(0, rows), pl.ds(0, rim), pl.ds(cut, rim)

    def rim_right(h, at):
        return remote(
            slot(1 - reach, core, h).at[:, at], slot(-reach, core, h).at[:, at],
            right_sem.at[reach - 1, h], recv_sem.at[0, core, h], "seq", right,
        )

    def rim_left(h, at):
        return remote(
            slot(reach - 1, core, h).at[:, at], slot(reach, core, h).at[:, at],
            left_sem.at[reach - 1, h], recv_sem.at[2 * reach, core, h], "seq", left,
        )

    def at_rim(right_op, left_op):
        @pl.when(core == 0)
        def _():
            right_op(late)
            left_op(whole)

        @pl.when(core == 1)
        def _():
            right_op(whole)
            left_op(early)

    def set_out(h):
        go_right(1, h, kv.at[h]).start()
        go_left(1, h, kv.at[h]).start()
        share(0, h, kv.at[h]).start()

    pl.semaphore_wait(barrier, n_tp * n_cfg - 1 + near_count)
    set_out(0)
    make_key(1)
    set_out(1)
    make_key(2)
    set_out(2)

    x_next = ((tx + 1) % n_x) * 2 + ty
    x_prev = ((tx + n_x - 1) % n_x) * 2 + ty
    y_peer = tx * 2 + 1 - ty
    far_x = ((tx + 2) % n_x) * 2
    core_rows = pl.ds(pl.multiple_of(core * 2 * quarter, 2 * quarter), 2 * quarter)
    low_rows = pl.ds(pl.multiple_of(core * 2 * quarter, quarter), quarter)
    high_rows = pl.ds(pl.multiple_of(core * 2 * quarter + quarter, quarter), quarter)
    mate_rows = pl.ds(pl.multiple_of(other * 2 * quarter, 2 * quarter), 2 * quarter)
    mate_low = pl.ds(pl.multiple_of(other * 2 * quarter, quarter), quarter)
    mate_high = pl.ds(pl.multiple_of(other * 2 * quarter + quarter, quarter), quarter)

    def w_at(source, part):
        return wall.at[source, part]

    prev_own, prev_near = x_prev, (x_prev // 2) * 2 + 1 - ty
    next_own, next_near = x_next, (x_next // 2) * 2 + 1 - ty
    far_own, far_near = far_x + ty, far_x + 1 - ty
    pieces = [
        (y_peer, core_rows, mate_rows),
        (prev_own, core_rows, mate_rows),
        (prev_near, core_rows, mate_rows),
        (next_own, core_rows, mate_rows),
        (next_near, core_rows, mate_rows),
        (far_own, low_rows, mate_low),
        (far_near, low_rows, mate_low),
        (far_own, high_rows, mate_high),
        (far_near, high_rows, mate_high),
    ]

    def w_sends():
        own = w_ref.at[core_rows, my_cols]
        near = w_at(y_peer, core_rows)
        return [
            remote(w_ref.at[core_rows, near_cols], w_at(col, core_rows), wsend.at[0], wrecv.at[0], "tp", y_peer),
            remote(own, w_at(col, core_rows), wsend.at[1], wrecv.at[1], "tp", x_next),
            remote(own, w_at(col, core_rows), wsend.at[3], wrecv.at[3], "tp", x_prev),
            remote(near, near, wsend.at[2], wrecv.at[2], "tp", x_next),
            remote(near, near, wsend.at[4], wrecv.at[4], "tp", x_prev),
            remote(w_at(prev_own, low_rows), w_at(prev_own, low_rows), wsend.at[5], wrecv.at[5], "tp", x_next),
            remote(w_at(next_own, high_rows), w_at(next_own, high_rows), wsend.at[7], wrecv.at[7], "tp", x_prev),
            remote(w_at(prev_near, low_rows), w_at(prev_near, low_rows), wsend.at[6], wrecv.at[6], "tp", x_next),
            remote(w_at(next_near, high_rows), w_at(next_near, high_rows), wsend.at[8], wrecv.at[8], "tp", x_prev),
        ]

    w_out = w_sends()

    def w_share(n):
        source, part, _ = pieces[n]
        return remote(w_at(source, part), w_at(source, part), wshare.at[n], wpartner.at[n], "seq", partner)

    def w_landed(n):
        source, part, _ = pieces[n]
        remote(w_at(source, part), w_at(source, part), wshare.at[n], wrecv.at[n], "tp", y_peer).wait_recv()

    def w_shared(n):
        source, _, part = pieces[n]
        remote(w_at(source, part), w_at(source, part), wshare.at[n], wpartner.at[n], "seq", partner).wait_recv()

    for n in (0, 1, 2):
        w_out[n].start()

    def res_copy(k, dest_slot):
        c = tp_peer(k)
        return remote(
            stream_ref.at[pl.ds(pl.multiple_of(c * piece, piece), piece)], res.at[dest_slot],
            res_send.at[k], res_recv.at[dest_slot], "tp", c,
        )

    def give_res(k, carry):
        res_copy(k, col).start()
        return carry

    lax.fori_loop(1, n_tp, give_res, 0)

    loads[1].wait()
    for h in range(heads):
        q_s[h] = rotated(0, h, qg_s[...]).astype(BF16)
    reqq[...] = pick(row, ends, ids)
    every = lax.broadcasted_iota(jnp.int32, (n_seq, rows), 0) * rows + lax.broadcasted_iota(jnp.int32, (n_seq, rows), 1)
    reqk[...] = pick(every, ends, ids)

    def wide(x):
        return jnp.concatenate([x] * tiles, axis=1)

    def update(h, blocks):
        q = q_s[h]
        asked = wide(reqq[...])
        scores = []
        for ref, source in blocks:
            keys = jnp.concatenate([ref[0, b * HDIM : (b + 1) * HDIM, :] for b in range(tiles)], axis=1)
            s = jnp.dot(q, keys, preferred_element_type=F32)
            scores.append(jnp.where(asked == reqk[pl.ds(source, 1), :], s, NEG))
        best = functools.reduce(jnp.maximum, scores)
        m_old = m_s[h]
        m_new = jnp.maximum(m_old, jnp.max(best, axis=1, keepdims=True))
        shrink = jnp.exp2((m_old - m_new) * EXP2_SCALE)
        m_wide = wide(m_new)
        total = None
        acc = acc_s[h] * shrink
        for (ref, source), s in zip(blocks, scores):
            p = jnp.exp2((s - m_wide) * EXP2_SCALE)
            total = p if total is None else total + p
            acc = acc + jnp.dot(p.astype(BF16), ref[1], preferred_element_type=F32)
        l_s[h] = l_s[h] * shrink + jnp.sum(total, axis=1, keepdims=True)
        acc_s[h] = acc
        m_s[h] = m_new

    def block_of(dz, p):
        return ((chip + dz + chips) % chips) * 2 + p

    def own(h, carry):
        blank = jnp.zeros((2, cut, HDIM), BF16)

        @pl.when(core == 0)
        def _():
            win[0, 0, h, :, pl.ds(0, cut), :] = blank

        @pl.when(core == 1)
        def _():
            win[2 * reach, 1, h, :, pl.ds(rim, cut), :] = blank

        m_s[h] = jnp.full((rows, HDIM), NEG, F32)
        l_s[h] = jnp.zeros((rows, HDIM), F32)
        acc_s[h] = jnp.zeros((rows, HDIM), F32)
        update(h, [(kv.at[h], me)])
        return carry

    lax.fori_loop(0, heads, own, 0)

    loads[2].wait()
    chunk = 512
    token = me * rows + col * piece + lax.broadcasted_iota(jnp.int32, (piece, chunk), 0)

    def pick_rows(j, carry):
        at = pl.ds(pl.multiple_of(j * chunk, chunk), chunk)
        for which, out in ((0, gate), (1, scale), (2, shift)):
            value = jnp.broadcast_to(mod_s[which, 0:1, at], (piece, chunk))
            for r in range(NREQ - 1):
                value = jnp.where(token >= ends[r], mod_s[which, r + 1 : r + 2, at], value)
            out[:, at] = value
        return carry

    lax.fori_loop(0, feats // chunk, pick_rows, 0)

    give = reach - 2 * reach * core
    take = -give

    def pair(d, p, h):
        return [(slot(-d, p, h), block_of(-d, p)), (slot(d, p, h), block_of(d, p))]

    def att_copy(h, k, dest_slot):
        c = tp_peer(k)
        return remote(
            att_s.at[h, pl.ds(pl.multiple_of((c // 2) * quarter, quarter), quarter)], attx.at[h, dest_slot],
            att_send.at[h, k], att_recv.at[h, dest_slot], "tp", c,
        )

    def give_att(h):
        att_s[h] = (acc_s[h] / l_s[h]).astype(BF16)

        def one(k, carry):
            att_copy(h, k, col).start()
            return carry

        lax.fori_loop(1, n_tp, one, 0)
        attx[h, col] = att_s[h, pl.ds(pl.multiple_of(tx * quarter, quarter), quarter), :]

    def take_att(h):
        def one(k, carry):
            att_copy(h, k, tp_peer(k)).wait_recv()
            return carry

        lax.fori_loop(1, n_tp, one, 0)

    def product(h, at):
        left_side = jnp.concatenate([attx[h, k] for k in range(n_tp)], axis=1)
        weights = wall[:, h * HDIM : (h + 1) * HDIM, at].reshape(n_tp * HDIM, chunk)
        return jnp.dot(left_side, weights, preferred_element_type=F32)

    def multiply(h):
        def one(j, carry):
            at = pl.ds(pl.multiple_of(j * chunk, chunk), chunk)
            made[:, at] = product(h, at) if h == 0 else made[:, at] + product(h, at)
            return carry

        lax.fori_loop(0, half // chunk, one, 0)

    def from_partner(d, h):
        landed(-d, other, h)
        landed(d, other, h)
        update(h, pair(d, other, h))

    def one_from_partner(dz, h):
        landed(dz, other, h)
        update(h, [(slot(dz, other, h), block_of(dz, other))])

    def step(i, carry):
        d, h = 1 + i // heads, i % heads
        d_last, h_last = 1 + (i + heads - 1) // heads - 1, (i + heads - 1) % heads

        @pl.when(i == 3)
        def _():
            w_landed(0)
            w_out[3].start()
            w_out[4].start()
            w_landed(1)
            w_out[5].start()
            w_landed(3)
            w_out[6].start()
            for n in (0, 1, 3):
                w_share(n).start()

        @pl.when(i == 7)
        def _():
            w_landed(2)
            w_out[7].start()
            w_landed(4)
            w_out[8].start()
            for n in (2, 4):
                w_share(n).start()

        @pl.when(i == 9)
        def _():
            for n in (5, 7):
                w_landed(n)
                w_share(n).start()

        @pl.when(i == heads * (reach - 1))
        def _():
            from_partner(d_last, h_last)

        for done in range(heads - 1):

            @pl.when(i == heads * (reach - 1) + done + 1)
            def _():
                one_from_partner(take, done)
                give_att(done)
                if done == 0:
                    for n in (6, 8):
                        w_landed(n)
                        w_share(n).start()
                else:
                    own_w.wait()
                    for n in range(9):
                        w_shared(n)
                    take_att(0)
                    multiply(0)

        @pl.when(d < reach - 1)
        def _():
            landed(-d, core, h)
            go_right(d + 1, h, slot(-d, core, h)).start()
            landed(d, core, h)
            go_left(d + 1, h, slot(d, core, h)).start()

        @pl.when(d == reach - 1)
        def _():
            landed(-d, core, h)
            landed(d, core, h)
            at_rim(lambda at: rim_right(h, at).start(), lambda at: rim_left(h, at).start())

        @pl.when(d < reach)
        def _():
            share(-d, h, slot(-d, core, h)).start()
            share(d, h, slot(d, core, h)).start()

        @pl.when(d == reach)
        def _():
            at_rim(lambda at: rim_right(h, at).wait_recv(), lambda at: rim_left(h, at).wait_recv())
            share(give, h, slot(give, core, h)).start()

        update(h, pair(d, core, h))

        @pl.when((i > 0) & (d < reach))
        def _():
            from_partner(d_last, h_last)

        @pl.when((i > 0) & (i < 4))
        def _():
            one_from_partner(0, i - 1)

        return carry

    lax.fori_loop(0, heads * reach, step, 0)

    one_from_partner(take, heads - 1)
    give_att(heads - 1)
    take_att(1)
    multiply(1)

    lane8 = lax.broadcasted_iota(jnp.int32, (1, HDIM), 1)
    top_row = jnp.zeros((1, HDIM), F32)
    for h in range(heads):
        top = jnp.max(jnp.max(m_s[h], axis=0, keepdims=True), axis=1, keepdims=True) * SCALE
        top_row = jnp.where(lane8 == 2 * NREQ + h, top, top_row)

    loads[3].wait()
    proj_s[pl.ds(CH, HDIM - CH), :] = jnp.zeros((HDIM - CH, feats), BF16)
    loads[4].wait()

    def take_res(k, carry):
        res_copy(k, tp_peer(k)).wait_recv()
        return carry

    lax.fori_loop(1, n_tp, take_res, 0)
    take_att(2)

    def y_copy(j):
        return remote(yout.at[j], ygot.at[j], y_send.at[j], y_recv.at[j], "tp", y_peer)

    keep = pl.ds(pl.multiple_of(ty * piece, piece), piece)
    pass_on = pl.ds(pl.multiple_of((1 - ty) * piece, piece), piece)

    def last_product(j, carry):
        at = pl.ds(pl.multiple_of(j * chunk, chunk), chunk)
        made[:, at] = made[:, at] + product(2, at)
        yout[j] = made[pass_on, at].astype(BF16)
        y_copy(j).start()
        return carry

    lax.fori_loop(0, half // chunk, last_product, 0)

    total1 = jnp.zeros((piece, 1), F32)
    for j in range(half // width):
        at = pl.ds(pl.multiple_of(ty * half + j * width, width), width)
        value = res[ty * (n_tp // 2) + j].astype(F32) + gate[:, at] * made[keep, j * width : (j + 1) * width]
        mixed[:, at] = value
        total1 = total1 + jnp.sum(value, axis=1, keepdims=True)
    for j in range(half // chunk):
        y_copy(j).wait_recv()
        at = pl.ds(pl.multiple_of((1 - ty) * half + j * chunk, chunk), chunk)
        mixed[:, at] = gate[:, at] * ygot[j].astype(F32)
    for j in range(half // width):
        at = pl.ds(pl.multiple_of((1 - ty) * half + j * width, width), width)
        value = res[(1 - ty) * (n_tp // 2) + j].astype(F32) + mixed[:, at]
        mixed[:, at] = value
        total1 = total1 + jnp.sum(value, axis=1, keepdims=True)
    mean = total1 * (1.0 / feats)
    variance = jnp.zeros((piece, 1), F32)
    for j in range(n_tp):
        at = slice(j * width, (j + 1) * width)
        centred = mixed[:, at] - mean
        mixed[:, at] = centred
        variance = variance + jnp.sum(centred * centred, axis=1, keepdims=True)
    inverse = lax.rsqrt(variance * (1.0 / feats) + 1e-06)
    flow = jnp.zeros((piece, HDIM), F32)
    for j in range(n_tp):
        at = slice(j * width, (j + 1) * width)
        normed = (mixed[:, at] * inverse * (1.0 + scale[:, at]) + shift[:, at]).astype(BF16)
        flow = flow + lax.dot_general(
            normed, proj_s[:, at], (((1,), (1,)), ((), ())), preferred_element_type=F32
        )
    flow_s[...] = flow
    even_rows = flow_s[pl.ds(0, piece // 2, stride=2), :]
    odd_rows = flow_s[pl.ds(1, piece // 2, stride=2), :]
    own_flow = even_rows + pltpu.roll(odd_rows, CH, 1)
    mine[...] = own_flow
    flows[group, col] = own_flow
    def flow_copy(k, g_slot, c_slot):
        g, c = plane_peer(k)
        return pltpu.make_async_remote_copy(
            src_ref=mine, dst_ref=flows.at[g_slot, c_slot],
            send_sem=flow_send.at[k], recv_sem=flow_recv.at[g_slot, c_slot],
            device_id={"cfg": g, "tp": c}, device_id_type=MESH,
        )

    def give_flow(k, carry):
        flow_copy(k, group, col).start()
        return carry

    lax.fori_loop(1, n_tp * n_cfg, give_flow, 0)

    pairs = rows // 2
    lane2 = lax.broadcasted_iota(jnp.int32, (pairs, HDIM), 1)
    row2 = me * rows + 2 * lax.broadcasted_iota(jnp.int32, (pairs, HDIM), 0) + (lane2 >= CH).astype(jnp.int32)
    request = pick(row2, ends, [jnp.int32(r) for r in range(NREQ)])
    image = (row2 - pick(row2, ends, [jnp.int32(0)] + ends[:-1])) >= TXT
    guide = pick(row2, ends, [guidance[r] for r in range(NREQ)])
    at_step = pick(row2, ends, [steps[r].astype(F32) for r in range(NREQ)])

    def sigma(u):
        remaining = 1.0 - u / STEPS
        return 3.0 * remaining / (1.0 + 2.0 * remaining)

    delta = sigma(at_step + 1.0) - sigma(at_step)

    def take_flow(k, carry):
        g, c = plane_peer(k)
        flow_copy(k, g, c).wait_recv()
        return carry

    lax.fori_loop(1, n_tp * n_cfg, take_flow, 0)

    cond = flows[0].reshape(pairs, HDIM)
    uncond = flows[1].reshape(pairs, HDIM)
    guided = uncond + guide * (cond - uncond)
    cond_square = jnp.where(image, cond * cond, 0.0)
    guided_square = jnp.where(image, guided * guided, 0.0)
    parts = []
    for square in (cond_square, guided_square):
        for r in range(NREQ):
            parts.append(jnp.sum(jnp.where(request == r, square, 0.0), axis=0, keepdims=True))
    stacked = jnp.sum(jnp.concatenate(parts, axis=0), axis=1, keepdims=True)
    diagonal = lax.broadcasted_iota(jnp.int32, (2 * NREQ, HDIM), 0) == lax.broadcasted_iota(jnp.int32, (2 * NREQ, HDIM), 1)
    own_sums = jnp.sum(jnp.where(diagonal, stacked, 0.0), axis=0, keepdims=True) + top_row
    row_s[...] = own_sums
    sums[me] = own_sums

    def sum_copy(k, dest_slot):
        return pltpu.make_async_remote_copy(
            src_ref=row_s, dst_ref=sums.at[dest_slot],
            send_sem=sum_send.at[k], recv_sem=sum_recv.at[dest_slot],
            device_id={"seq": seq_peer(k)}, device_id_type=MESH,
        )

    def give_sum(k, carry):
        sum_copy(k, me).start()
        return carry

    lax.fori_loop(1, n_seq, give_sum, 0)

    def take_sum(k, carry):
        sum_copy(k, seq_peer(k)).wait_recv()
        return carry

    lax.fori_loop(1, n_seq, take_sum, 0)

    total = sums[0]
    top = sums[0]
    for k in range(1, n_seq):
        total = total + sums[k]
        top = jnp.maximum(top, sums[k])
    tops_ref[...] = pltpu.roll(top, HDIM - 2 * NREQ, 1)[:, :heads]
    lane1 = lax.broadcasted_iota(jnp.int32, (1, HDIM), 1)
    entries = jnp.ones((1, HDIM), F32)
    for r in range(NREQ):
        entries = jnp.where(lane1 == r, counts[r].astype(F32) * CH, entries)
    guided_total = pltpu.roll(total, HDIM - NREQ, 1)
    factor = (PHI_MIX * jnp.sqrt(total / entries + 1e-06) + (1.0 - PHI_MIX)) / jnp.sqrt(guided_total / entries + 1e-06)
    factor_row = jnp.zeros((pairs, HDIM), F32)
    for r in range(NREQ):
        one = jnp.sum(jnp.where(lane1 == r, factor, 0.0), axis=1, keepdims=True)
        factor_row = jnp.where(request == r, one, factor_row)
    velocity = guided * jnp.where(image, factor_row, 0.0)
    stepped = latent_s[...] + delta * velocity
    for value, out in ((velocity, vel_ref), (stepped, next_ref)):
        value = jnp.where(group == 0, value, pltpu.roll(value, CH, 1))
        out[:, :HDIM] = value[:HDIM].T[:CH]
        out[:, HDIM:] = jnp.concatenate([value[HDIM:], value[HDIM:]], axis=0).T[:CH, : pairs - HDIM]

    def drain_tp(k, carry):
        res_copy(k, col).wait_send()
        for h in range(heads):
            att_copy(h, k, col).wait_send()
        return carry

    lax.fori_loop(1, n_tp, drain_tp, 0)

    def drain_flow(k, carry):
        flow_copy(k, group, col).wait_send()
        return carry

    lax.fori_loop(1, n_tp * n_cfg, drain_flow, 0)

    def drain_sum(k, carry):
        sum_copy(k, me).wait_send()
        return carry

    lax.fori_loop(1, n_seq, drain_sum, 0)

    def drain(h, carry):
        for d in range(1, reach):
            go_right(d, h, kv.at[h]).wait_send()
            go_left(d, h, kv.at[h]).wait_send()
        at_rim(lambda at: rim_right(h, at).wait_send(), lambda at: rim_left(h, at).wait_send())
        for dz in range(1 - reach, reach):
            share(dz, h, kv.at[h]).wait_send()
        share(give, h, kv.at[h]).wait_send()
        return carry

    lax.fori_loop(0, heads, drain, 0)
    for copy in w_out:
        copy.wait_send()
    for n in range(9):
        w_share(n).wait_send()
    for j in range(half // chunk):
        y_copy(j).wait_send()


def local(stream, qkv, q_gain, k_gain, w_out, mod, w_proj, latent, guidance, img_counts, img_widths, step_index):
    rows, width = stream.shape[1], stream.shape[2]
    feats = w_out.shape[1]
    heads = width // HDIM
    n_seq, n_tp, n_cfg = lax.axis_size("seq"), lax.axis_size("tp"), lax.axis_size("cfg")
    piece = rows // n_tp
    img_most = (rows * n_seq - NREQ * TXT) // 4
    longest = TXT + img_most
    reach = ((longest + rows - 2) // rows + 1) // 2
    rim = min(rows, -(-(longest - (2 * reach - 1) * rows - 1) // HDIM) * HDIM)
    vmem = pl.BlockSpec(memory_space=pltpu.VMEM)
    hbm = pl.BlockSpec(memory_space=pltpu.HBM)
    dma = pltpu.SemaphoreType.DMA
    pairs = rows // 2
    half = feats // 2
    chunk = 512
    vel, nxt, tops = pl.pallas_call(
        functools.partial(kernel, rim),
        out_shape=(
            jax.ShapeDtypeStruct((CH, pairs), F32),
            jax.ShapeDtypeStruct((CH, pairs), F32),
            jax.ShapeDtypeStruct((1, heads), F32),
        ),
        in_specs=[hbm] * 13,
        out_specs=(vmem,) * 3,
        scratch_shapes=[
            pltpu.SMEM((NREQ,), jnp.int32),
            pltpu.SMEM((NREQ,), jnp.int32),
            pltpu.SMEM((NREQ,), jnp.int32),
            pltpu.SMEM((NREQ,), F32),
            pltpu.VMEM((pairs, HDIM), F32),
            pltpu.VMEM((1, HDIM), F32),
            pltpu.VMEM((1, HDIM), F32),
            pltpu.VMEM((1, HDIM), F32),
            pltpu.VMEM((2, rows, width), BF16),
            pltpu.VMEM((heads, rows, HDIM), BF16),
            pltpu.VMEM((heads, 2, rows, HDIM), BF16),
            pltpu.VMEM((rows, HDIM), jnp.int32),
            pltpu.VMEM((n_seq, rows), jnp.int32),
            pltpu.VMEM((2 * reach + 1, 2, heads, 2, rows, HDIM), BF16),
            pltpu.VMEM((heads, rows, HDIM), F32),
            pltpu.VMEM((heads, rows, HDIM), F32),
            pltpu.VMEM((heads, rows, HDIM), F32),
            pltpu.VMEM((n_tp, rows, half), BF16),
            pltpu.VMEM((heads, rows, HDIM), BF16),
            pltpu.VMEM((heads, n_tp, 2 * piece, HDIM), BF16),
            pltpu.VMEM((2 * piece, half), F32),
            pltpu.VMEM((half // chunk, piece, chunk), BF16),
            pltpu.VMEM((half // chunk, piece, chunk), BF16),
            pltpu.VMEM((n_tp, piece, width), BF16),
            pltpu.VMEM((3, NREQ, feats), F32),
            pltpu.VMEM((HDIM, feats), BF16),
            pltpu.VMEM((piece, feats), F32),
            pltpu.VMEM((piece, feats), F32),
            pltpu.VMEM((piece, feats), F32),
            pltpu.VMEM((piece, feats), F32),
            pltpu.VMEM((piece, HDIM), F32),
            pltpu.VMEM((piece // 2, HDIM), F32),
            pltpu.VMEM((n_cfg, n_tp, piece // 2, HDIM), F32),
            pltpu.VMEM((1, HDIM), F32),
            pltpu.VMEM((n_seq, 1, HDIM), F32),
            dma((8,)),
            dma((6 + heads,)),
            dma((reach, heads)),
            dma((reach, heads)),
            dma((2 * reach + 1, heads)),
            dma((2 * reach + 1, 2, heads)),
            dma((9,)),
            dma((9,)),
            dma((9,)),
            dma((9,)),
            dma((heads, n_tp)),
            dma((heads, n_tp)),
            dma((half // chunk,)),
            dma((half // chunk,)),
            dma((n_tp,)),
            dma((n_tp,)),
            dma((n_tp * n_cfg,)),
            dma((n_cfg, n_tp)),
            dma((n_seq,)),
            dma((n_seq,)),
        ],
        compiler_params=pltpu.CompilerParams(collective_id=0, has_side_effects=True, vmem_limit_bytes=38 << 20),
        name="flow_step",
    )(*(pltpu.with_memory_space_constraint(x, pltpu.HBM) for x in (
        img_counts, img_widths, step_index, guidance, jnp.transpose(qkv[0], (1, 0, 2)), w_out, stream[0],
        jnp.transpose(mod[0], (1, 0, 2)), w_proj, latent, jnp.asarray(frequency_row()),
        q_gain.reshape(1, HDIM), k_gain.reshape(1, HDIM),
    )))
    return (vel.T, nxt.T, tops)


def solution(mesh):
    placed = (
        P("cfg", "seq", "tp"),
        P("cfg", "seq", None, "tp"),
        P(),
        P(),
        P("tp", None),
        P("cfg", None, None, None),
        P(),
        P("seq", None),
        P(),
        P(),
        P(),
        P(),
    )
    return jax.shard_map(
        local,
        mesh=mesh,
        in_specs=placed,
        out_specs=(P("seq", "cfg"), P("seq", "cfg"), P("cfg", "tp")),
        check_vma=False,
    )
```

```python
import functools
import math

import jax
import jax.numpy as jnp
import numpy as np
from jax import lax
from jax.experimental import pallas as pl
from jax.experimental.pallas import tpu as pltpu
from jax.sharding import PartitionSpec as P

MESH = pl.DeviceIdType.MESH
HDIM = 128
CH = 64
TXT = 128
STEPS = 8
NREQ = 8
PHI_MIX = 0.7
NEG = -1e30
SCALE = 1.0 / math.sqrt(float(HDIM))
EXP2_SCALE = SCALE * math.log2(math.e)
F32 = jnp.float32
BF16 = jnp.bfloat16


def frequency_row():
    pair_index = np.arange(64)
    axis_of = np.where(pair_index < 8, 0, np.where(pair_index < 36, 1, 2))
    axis_start = np.array([0, 8, 36])[axis_of]
    axis_width = np.array([16.0, 56.0, 56.0])[axis_of]
    frequency = 10000.0 ** (-2.0 * (pair_index - axis_start) / axis_width)
    return np.repeat(frequency, 2).astype(np.float32)[None, :]


def request_ends(counts):
    ends = []
    end = jnp.int32(0)
    for r in range(NREQ):
        end = end + (TXT + counts[r])
        ends.append(end)
    return ends


def pick(rows, ends, values):
    out = jnp.full(rows.shape, values[0])
    for r in range(NREQ - 1):
        out = jnp.where(rows >= ends[r], values[r + 1], out)
    return out


def kernel(
    rim,
    counts_ref, widths_ref, steps_ref, guidance_ref, qkv_ref, w_ref, stream_ref, mod_ref, proj_ref, latent_ref,
    freq_ref, qg_ref, kg_ref,
    vel_ref, next_ref, tops_ref,
    counts, widths, steps, guidance, latent_s, freq_s, qg_s, kg_s, qkv, q_s, kv, reqq, reqk, win, m_s, l_s, acc_s,
    wall, att_s, attx, made, yout, ygot,
    res, mod_s, proj_s, mixed, gate, scale, shift, flow_s, mine, flows, row_s, sums,
    first_sem, load_sem, right_sem, left_sem, share_sem, recv_sem, wsend, wrecv, wshare, wpartner,
    att_send, att_recv, y_send, y_recv, res_send, res_recv, flow_send, flow_recv, sum_send, sum_recv,
):
    n_tp, n_seq, n_cfg = lax.axis_size("tp"), lax.axis_size("seq"), lax.axis_size("cfg")
    group, me, col = lax.axis_index("cfg"), lax.axis_index("seq"), lax.axis_index("tp")
    heads, rows = q_s.shape[0], q_s.shape[1]
    width = heads * HDIM
    feats = w_ref.shape[1]
    half = feats // 2
    piece = rows // n_tp
    quarter = 2 * piece
    reach = win.shape[0] // 2
    chips = n_seq // 2
    chip, core = me // 2, me % 2
    other = 1 - core
    right = ((chip + 1) % chips) * 2 + core
    left = ((chip + chips - 1) % chips) * 2 + core
    partner = chip * 2 + other
    n_x = n_tp // 2
    tx, ty = col // 2, col % 2
    tiles = rows // HDIM
    barrier = pltpu.get_barrier_semaphore()

    def tp_peer(k):
        return (col + k) % n_tp

    def plane_peer(k):
        return (group + k // n_tp) % n_cfg, (col + k) % n_tp

    def seq_peer(k):
        return (me + k) % n_seq

    def hail_plane(k, carry):
        g, c = plane_peer(k)
        pl.semaphore_signal(barrier, inc=1, device_id={"cfg": g, "tp": c}, device_id_type=MESH)
        return carry

    lax.fori_loop(1, n_tp * n_cfg, hail_plane, 0)

    near_count = 4 * reach + 1

    def hail_seq(k, carry):
        peer = (2 * chip + 2 * n_seq - 2 * reach + k) % n_seq

        @pl.when(peer != me)
        def _():
            pl.semaphore_signal(barrier, inc=1, device_id={"seq": peer}, device_id_type=MESH)

        return carry

    lax.fori_loop(0, near_count + 1, hail_seq, 0)

    def remote(src, dst, send, recv, axis, peer):
        return pltpu.make_async_remote_copy(
            src_ref=src, dst_ref=dst, send_sem=send, recv_sem=recv,
            device_id={axis: peer}, device_id_type=MESH,
        )

    firsts = [
        pltpu.make_async_copy(source, target, first_sem.at[n])
        for n, (source, target) in enumerate(
            (
                (counts_ref, counts), (widths_ref, widths), (steps_ref, steps), (guidance_ref, guidance),
                (freq_ref, freq_s), (qg_ref, qg_s), (kg_ref, kg_s), (latent_ref, latent_s),
            )
        )
    ]
    for copy in firsts:
        copy.start()
    loads = [
        pltpu.make_async_copy(qkv_ref.at[1], qkv.at[1], load_sem.at[0]),
        pltpu.make_async_copy(qkv_ref.at[0], qkv.at[0], load_sem.at[1]),
        pltpu.make_async_copy(mod_ref, mod_s, load_sem.at[2]),
        pltpu.make_async_copy(proj_ref, proj_s.at[pl.ds(0, CH)], load_sem.at[3]),
        pltpu.make_async_copy(stream_ref.at[pl.ds(pl.multiple_of(col * piece, piece), piece)], res.at[col], load_sem.at[4]),
    ]
    for copy in loads:
        copy.start()
    values = [
        pltpu.make_async_copy(qkv_ref.at[2, :, pl.ds(h * HDIM, HDIM)], kv.at[h, 1], load_sem.at[5 + h]) for h in range(heads)
    ]
    for copy in values:
        copy.start()
    my_cols = pl.ds(pl.multiple_of(ty * half, half), half)
    near_cols = pl.ds(pl.multiple_of((1 - ty) * half, half), half)
    own_w = pltpu.make_async_copy(w_ref.at[:, my_cols], wall.at[col], load_sem.at[5 + heads])
    own_w.start()

    for copy in firsts:
        copy.wait()
    ends = request_ends(counts)
    starts = [jnp.int32(0)] + ends[:-1]
    ids = [jnp.int32(r) for r in range(NREQ)]
    row = me * rows + lax.broadcasted_iota(jnp.int32, (rows, HDIM), 0)
    start = pick(row, ends, starts)
    span = pick(row, ends, [widths[r].astype(F32) for r in range(NREQ)])
    pos = jnp.maximum(row - start - TXT, 0).astype(F32)
    height_id = jnp.floor((pos + 0.5) / span)
    width_id = pos - height_id * span
    lane = lax.broadcasted_iota(jnp.int32, (rows, HDIM), 1)
    angle = jnp.where(lane < 16, 0.0, jnp.where(lane < 72, height_id, width_id)) * freq_s[...]
    even = lane % 2 == 0
    cos = jnp.cos(angle)
    sin = jnp.sin(angle)
    sin = jnp.where(even, -sin, sin)

    def rotated(part, h, gain):
        x = qkv[part, :, h * HDIM : (h + 1) * HDIM].astype(F32)
        x = x * lax.rsqrt(jnp.mean(x * x, axis=-1, keepdims=True) + 1e-06) * gain
        mate = jnp.where(even, pltpu.roll(x, HDIM - 1, 1), pltpu.roll(x, 1, 1))
        return x * cos + mate * sin

    def make_key(h):
        key = rotated(1, h, kg_s[...])
        for b in range(tiles):
            at = slice(b * HDIM, (b + 1) * HDIM)
            kv[h, 0, at, :] = key[at].T.astype(BF16)

    loads[0].wait()
    make_key(0)
    for copy in values:
        copy.wait()

    def slot(dz, p, h):
        return win.at[dz + reach, p, h]

    def go_right(d, h, src):
        return remote(src, slot(-d, core, h), right_sem.at[d - 1, h], recv_sem.at[reach - d, core, h], "seq", right)

    def go_left(d, h, src):
        return remote(src, slot(d, core, h), left_sem.at[d - 1, h], recv_sem.at[reach + d, core, h], "seq", left)

    def share(dz, h, src):
        return remote(src, slot(dz, core, h), share_sem.at[dz + reach, h], recv_sem.at[dz + reach, core, h], "seq", partner)

    def landed(dz, p, h):
        remote(slot(dz, p, h), slot(dz, p, h), share_sem.at[0, 0], recv_sem.at[dz + reach, p, h], "seq", partner).wait_recv()

    cut = rows - rim
    whole, early, late = pl.ds(0, rows), pl.ds(0, rim), pl.ds(cut, rim)

    def rim_right(h, at):
        return remote(
            slot(1 - reach, core, h).at[:, at], slot(-reach, core, h).at[:, at],
            right_sem.at[reach - 1, h], recv_sem.at[0, core, h], "seq", right,
        )

    def rim_left(h, at):
        return remote(
            slot(reach - 1, core, h).at[:, at], slot(reach, core, h).at[:, at],
            left_sem.at[reach - 1, h], recv_sem.at[2 * reach, core, h], "seq", left,
        )

    def at_rim(right_op, left_op):
        @pl.when(core == 0)
        def _():
            right_op(late)
            left_op(whole)

        @pl.when(core == 1)
        def _():
            right_op(whole)
            left_op(early)

    def set_out(h):
        go_right(1, h, kv.at[h]).start()
        go_left(1, h, kv.at[h]).start()
        share(0, h, kv.at[h]).start()

    pl.semaphore_wait(barrier, n_tp * n_cfg - 1 + near_count)
    set_out(0)
    make_key(1)
    set_out(1)
    make_key(2)
    set_out(2)

    x_next = ((tx + 1) % n_x) * 2 + ty
    x_prev = ((tx + n_x - 1) % n_x) * 2 + ty
    y_peer = tx * 2 + 1 - ty
    far_x = ((tx + 2) % n_x) * 2
    core_rows = pl.ds(pl.multiple_of(core * 2 * quarter, 2 * quarter), 2 * quarter)
    low_rows = pl.ds(pl.multiple_of(core * 2 * quarter, quarter), quarter)
    high_rows = pl.ds(pl.multiple_of(core * 2 * quarter + quarter, quarter), quarter)
    mate_rows = pl.ds(pl.multiple_of(other * 2 * quarter, 2 * quarter), 2 * quarter)
    mate_low = pl.ds(pl.multiple_of(other * 2 * quarter, quarter), quarter)
    mate_high = pl.ds(pl.multiple_of(other * 2 * quarter + quarter, quarter), quarter)

    def w_at(source, part):
        return wall.at[source, part]

    prev_own, prev_near = x_prev, (x_prev // 2) * 2 + 1 - ty
    next_own, next_near = x_next, (x_next // 2) * 2 + 1 - ty
    far_own, far_near = far_x + ty, far_x + 1 - ty
    pieces = [
        (y_peer, core_rows, mate_rows),
        (prev_own, core_rows, mate_rows),
        (prev_near, core_rows, mate_rows),
        (next_own, core_rows, mate_rows),
        (next_near, core_rows, mate_rows),
        (far_own, low_rows, mate_low),
        (far_near, low_rows, mate_low),
        (far_own, high_rows, mate_high),
        (far_near, high_rows, mate_high),
    ]

    def w_sends():
        own = w_ref.at[core_rows, my_cols]
        near = w_at(y_peer, core_rows)
        return [
            remote(w_ref.at[core_rows, near_cols], w_at(col, core_rows), wsend.at[0], wrecv.at[0], "tp", y_peer),
            remote(own, w_at(col, core_rows), wsend.at[1], wrecv.at[1], "tp", x_next),
            remote(own, w_at(col, core_rows), wsend.at[3], wrecv.at[3], "tp", x_prev),
            remote(near, near, wsend.at[2], wrecv.at[2], "tp", x_next),
            remote(near, near, wsend.at[4], wrecv.at[4], "tp", x_prev),
            remote(w_at(prev_own, low_rows), w_at(prev_own, low_rows), wsend.at[5], wrecv.at[5], "tp", x_next),
            remote(w_at(next_own, high_rows), w_at(next_own, high_rows), wsend.at[7], wrecv.at[7], "tp", x_prev),
            remote(w_at(prev_near, low_rows), w_at(prev_near, low_rows), wsend.at[6], wrecv.at[6], "tp", x_next),
            remote(w_at(next_near, high_rows), w_at(next_near, high_rows), wsend.at[8], wrecv.at[8], "tp", x_prev),
        ]

    w_out = w_sends()

    def w_share(n):
        source, part, _ = pieces[n]
        return remote(w_at(source, part), w_at(source, part), wshare.at[n], wpartner.at[n], "seq", partner)

    def w_landed(n):
        source, part, _ = pieces[n]
        remote(w_at(source, part), w_at(source, part), wshare.at[n], wrecv.at[n], "tp", y_peer).wait_recv()

    def w_shared(n):
        source, _, part = pieces[n]
        remote(w_at(source, part), w_at(source, part), wshare.at[n], wpartner.at[n], "seq", partner).wait_recv()

    for n in (0, 1, 2):
        w_out[n].start()

    def res_copy(k, dest_slot):
        c = tp_peer(k)
        return remote(
            stream_ref.at[pl.ds(pl.multiple_of(c * piece, piece), piece)], res.at[dest_slot],
            res_send.at[k], res_recv.at[dest_slot], "tp", c,
        )

    def give_res(k, carry):
        res_copy(k, col).start()
        return carry

    lax.fori_loop(1, n_tp, give_res, 0)

    loads[1].wait()
    for h in range(heads):
        q_s[h] = rotated(0, h, qg_s[...]).astype(BF16)
    reqq[...] = pick(row, ends, ids)
    every = lax.broadcasted_iota(jnp.int32, (n_seq, rows), 0) * rows + lax.broadcasted_iota(jnp.int32, (n_seq, rows), 1)
    reqk[...] = pick(every, ends, ids)

    def wide(x):
        return jnp.concatenate([x] * tiles, axis=1)

    def update(h, blocks):
        q = q_s[h]
        asked = wide(reqq[...])
        scores = []
        for ref, source in blocks:
            keys = jnp.concatenate([ref[0, b * HDIM : (b + 1) * HDIM, :] for b in range(tiles)], axis=1)
            s = jnp.dot(q, keys, preferred_element_type=F32)
            scores.append(jnp.where(asked == reqk[pl.ds(source, 1), :], s, NEG))
        best = functools.reduce(jnp.maximum, scores)
        m_old = m_s[h]
        m_new = jnp.maximum(m_old, jnp.max(best, axis=1, keepdims=True))
        shrink = jnp.exp2((m_old - m_new) * EXP2_SCALE)
        m_wide = wide(m_new)
        total = None
        acc = acc_s[h] * shrink
        for (ref, source), s in zip(blocks, scores):
            p = jnp.exp2((s - m_wide) * EXP2_SCALE)
            total = p if total is None else total + p
            acc = acc + jnp.dot(p.astype(BF16), ref[1], preferred_element_type=F32)
        l_s[h] = l_s[h] * shrink + jnp.sum(total, axis=1, keepdims=True)
        acc_s[h] = acc
        m_s[h] = m_new

    def block_of(dz, p):
        return ((chip + dz + chips) % chips) * 2 + p

    def own(h, carry):
        blank = jnp.zeros((2, cut, HDIM), BF16)

        @pl.when(core == 0)
        def _():
            win[0, 0, h, :, pl.ds(0, cut), :] = blank

        @pl.when(core == 1)
        def _():
            win[2 * reach, 1, h, :, pl.ds(rim, cut), :] = blank

        m_s[h] = jnp.full((rows, HDIM), NEG, F32)
        l_s[h] = jnp.zeros((rows, HDIM), F32)
        acc_s[h] = jnp.zeros((rows, HDIM), F32)
        update(h, [(kv.at[h], me)])
        return carry

    lax.fori_loop(0, heads, own, 0)

    loads[2].wait()
    chunk = 512
    token = me * rows + col * piece + lax.broadcasted_iota(jnp.int32, (piece, chunk), 0)

    def pick_rows(j, carry):
        at = pl.ds(pl.multiple_of(j * chunk, chunk), chunk)
        for which, out in ((0, gate), (1, scale), (2, shift)):
            value = jnp.broadcast_to(mod_s[which, 0:1, at], (piece, chunk))
            for r in range(NREQ - 1):
                value = jnp.where(token >= ends[r], mod_s[which, r + 1 : r + 2, at], value)
            out[:, at] = value
        return carry

    lax.fori_loop(0, feats // chunk, pick_rows, 0)

    give = reach - 2 * reach * core
    take = -give

    def pair(d, p, h):
        return [(slot(-d, p, h), block_of(-d, p)), (slot(d, p, h), block_of(d, p))]

    def att_copy(h, k, dest_slot):
        c = tp_peer(k)
        return remote(
            att_s.at[h, pl.ds(pl.multiple_of((c // 2) * quarter, quarter), quarter)], attx.at[h, dest_slot],
            att_send.at[h, k], att_recv.at[h, dest_slot], "tp", c,
        )

    def give_att(h):
        att_s[h] = (acc_s[h] / l_s[h]).astype(BF16)

        def one(k, carry):
            att_copy(h, k, col).start()
            return carry

        lax.fori_loop(1, n_tp, one, 0)
        attx[h, col] = att_s[h, pl.ds(pl.multiple_of(tx * quarter, quarter), quarter), :]

    def take_att(h):
        def one(k, carry):
            att_copy(h, k, tp_peer(k)).wait_recv()
            return carry

        lax.fori_loop(1, n_tp, one, 0)

    def product(h, at):
        left_side = jnp.concatenate([attx[h, k] for k in range(n_tp)], axis=1)
        weights = wall[:, h * HDIM : (h + 1) * HDIM, at].reshape(n_tp * HDIM, chunk)
        return jnp.dot(left_side, weights, preferred_element_type=F32)

    def from_partner(d, h):
        landed(-d, other, h)
        landed(d, other, h)
        update(h, pair(d, other, h))

    def one_from_partner(dz, h):
        landed(dz, other, h)
        update(h, [(slot(dz, other, h), block_of(dz, other))])

    def step(i, carry):
        d, h = 1 + i // heads, i % heads
        d_last, h_last = 1 + (i + heads - 1) // heads - 1, (i + heads - 1) % heads

        @pl.when(i == 3)
        def _():
            w_landed(0)
            w_out[3].start()
            w_out[4].start()
            w_landed(1)
            w_out[5].start()
            w_landed(3)
            w_out[6].start()
            for n in (0, 1, 3):
                w_share(n).start()

        @pl.when(i == 7)
        def _():
            w_landed(2)
            w_out[7].start()
            w_landed(4)
            w_out[8].start()
            for n in (2, 4):
                w_share(n).start()

        @pl.when(i == 9)
        def _():
            for n in (5, 7):
                w_landed(n)
                w_share(n).start()

        @pl.when(i == heads * (reach - 1))
        def _():
            from_partner(d_last, h_last)

        for done in range(heads - 1):

            @pl.when(i == heads * (reach - 1) + done + 1)
            def _():
                one_from_partner(take, done)
                give_att(done)
                if done == 0:
                    for n in (6, 8):
                        w_landed(n)
                        w_share(n).start()

        @pl.when(d < reach - 1)
        def _():
            landed(-d, core, h)
            go_right(d + 1, h, slot(-d, core, h)).start()
            landed(d, core, h)
            go_left(d + 1, h, slot(d, core, h)).start()

        @pl.when(d == reach - 1)
        def _():
            landed(-d, core, h)
            landed(d, core, h)
            at_rim(lambda at: rim_right(h, at).start(), lambda at: rim_left(h, at).start())

        @pl.when(d < reach)
        def _():
            share(-d, h, slot(-d, core, h)).start()
            share(d, h, slot(d, core, h)).start()

        @pl.when(d == reach)
        def _():
            at_rim(lambda at: rim_right(h, at).wait_recv(), lambda at: rim_left(h, at).wait_recv())
            share(give, h, slot(give, core, h)).start()

        update(h, pair(d, core, h))

        @pl.when((i > 0) & (d < reach))
        def _():
            from_partner(d_last, h_last)

        @pl.when((i > 0) & (i < 4))
        def _():
            one_from_partner(0, i - 1)

        return carry

    lax.fori_loop(0, heads * reach, step, 0)

    one_from_partner(take, heads - 1)
    give_att(heads - 1)
    own_w.wait()
    for n in range(9):
        w_shared(n)
    take_att(0)
    take_att(1)

    def early_product(j, carry):
        at = pl.ds(pl.multiple_of(j * chunk, chunk), chunk)
        made[:, at] = product(0, at) + product(1, at)
        return carry

    lax.fori_loop(0, half // chunk, early_product, 0)

    lane8 = lax.broadcasted_iota(jnp.int32, (1, HDIM), 1)
    top_row = jnp.zeros((1, HDIM), F32)
    for h in range(heads):
        top = jnp.max(jnp.max(m_s[h], axis=0, keepdims=True), axis=1, keepdims=True) * SCALE
        top_row = jnp.where(lane8 == 2 * NREQ + h, top, top_row)

    loads[3].wait()
    proj_s[pl.ds(CH, HDIM - CH), :] = jnp.zeros((HDIM - CH, feats), BF16)
    loads[4].wait()

    def take_res(k, carry):
        res_copy(k, tp_peer(k)).wait_recv()
        return carry

    lax.fori_loop(1, n_tp, take_res, 0)
    take_att(2)

    def y_copy(j):
        return remote(yout.at[j], ygot.at[j], y_send.at[j], y_recv.at[j], "tp", y_peer)

    keep = pl.ds(pl.multiple_of(ty * piece, piece), piece)
    pass_on = pl.ds(pl.multiple_of((1 - ty) * piece, piece), piece)

    def last_product(j, carry):
        at = pl.ds(pl.multiple_of(j * chunk, chunk), chunk)
        made[:, at] = made[:, at] + product(2, at)
        yout[j] = made[pass_on, at].astype(BF16)
        y_copy(j).start()
        return carry

    lax.fori_loop(0, half // chunk, last_product, 0)

    total1 = jnp.zeros((piece, 1), F32)
    for j in range(half // width):
        at = pl.ds(pl.multiple_of(ty * half + j * width, width), width)
        value = res[ty * (n_tp // 2) + j].astype(F32) + gate[:, at] * made[keep, j * width : (j + 1) * width]
        mixed[:, at] = value
        total1 = total1 + jnp.sum(value, axis=1, keepdims=True)
    for j in range(half // chunk):
        y_copy(j).wait_recv()
        at = pl.ds(pl.multiple_of((1 - ty) * half + j * chunk, chunk), chunk)
        mixed[:, at] = gate[:, at] * ygot[j].astype(F32)
    for j in range(half // width):
        at = pl.ds(pl.multiple_of((1 - ty) * half + j * width, width), width)
        value = res[(1 - ty) * (n_tp // 2) + j].astype(F32) + mixed[:, at]
        mixed[:, at] = value
        total1 = total1 + jnp.sum(value, axis=1, keepdims=True)
    mean = total1 * (1.0 / feats)
    variance = jnp.zeros((piece, 1), F32)
    for j in range(n_tp):
        at = slice(j * width, (j + 1) * width)
        centred = mixed[:, at] - mean
        mixed[:, at] = centred
        variance = variance + jnp.sum(centred * centred, axis=1, keepdims=True)
    inverse = lax.rsqrt(variance * (1.0 / feats) + 1e-06)
    flow = jnp.zeros((piece, HDIM), F32)
    for j in range(n_tp):
        at = slice(j * width, (j + 1) * width)
        normed = (mixed[:, at] * inverse * (1.0 + scale[:, at]) + shift[:, at]).astype(BF16)
        flow = flow + lax.dot_general(
            normed, proj_s[:, at], (((1,), (1,)), ((), ())), preferred_element_type=F32
        )
    flow_s[...] = flow
    even_rows = flow_s[pl.ds(0, piece // 2, stride=2), :]
    odd_rows = flow_s[pl.ds(1, piece // 2, stride=2), :]
    own_flow = even_rows + pltpu.roll(odd_rows, CH, 1)
    mine[...] = own_flow
    flows[group, col] = own_flow
    def flow_copy(k, g_slot, c_slot):
        g, c = plane_peer(k)
        return pltpu.make_async_remote_copy(
            src_ref=mine, dst_ref=flows.at[g_slot, c_slot],
            send_sem=flow_send.at[k], recv_sem=flow_recv.at[g_slot, c_slot],
            device_id={"cfg": g, "tp": c}, device_id_type=MESH,
        )

    def give_flow(k, carry):
        flow_copy(k, group, col).start()
        return carry

    lax.fori_loop(1, n_tp * n_cfg, give_flow, 0)

    pairs = rows // 2
    lane2 = lax.broadcasted_iota(jnp.int32, (pairs, HDIM), 1)
    row2 = me * rows + 2 * lax.broadcasted_iota(jnp.int32, (pairs, HDIM), 0) + (lane2 >= CH).astype(jnp.int32)
    request = pick(row2, ends, [jnp.int32(r) for r in range(NREQ)])
    image = (row2 - pick(row2, ends, [jnp.int32(0)] + ends[:-1])) >= TXT
    guide = pick(row2, ends, [guidance[r] for r in range(NREQ)])
    at_step = pick(row2, ends, [steps[r].astype(F32) for r in range(NREQ)])

    def sigma(u):
        remaining = 1.0 - u / STEPS
        return 3.0 * remaining / (1.0 + 2.0 * remaining)

    delta = sigma(at_step + 1.0) - sigma(at_step)

    def take_flow(k, carry):
        g, c = plane_peer(k)
        flow_copy(k, g, c).wait_recv()
        return carry

    lax.fori_loop(1, n_tp * n_cfg, take_flow, 0)

    cond = flows[0].reshape(pairs, HDIM)
    uncond = flows[1].reshape(pairs, HDIM)
    guided = uncond + guide * (cond - uncond)
    cond_square = jnp.where(image, cond * cond, 0.0)
    guided_square = jnp.where(image, guided * guided, 0.0)
    parts = []
    for square in (cond_square, guided_square):
        for r in range(NREQ):
            parts.append(jnp.sum(jnp.where(request == r, square, 0.0), axis=0, keepdims=True))
    stacked = jnp.sum(jnp.concatenate(parts, axis=0), axis=1, keepdims=True)
    diagonal = lax.broadcasted_iota(jnp.int32, (2 * NREQ, HDIM), 0) == lax.broadcasted_iota(jnp.int32, (2 * NREQ, HDIM), 1)
    own_sums = jnp.sum(jnp.where(diagonal, stacked, 0.0), axis=0, keepdims=True) + top_row
    row_s[...] = own_sums
    sums[me] = own_sums

    def sum_copy(k, dest_slot):
        return pltpu.make_async_remote_copy(
            src_ref=row_s, dst_ref=sums.at[dest_slot],
            send_sem=sum_send.at[k], recv_sem=sum_recv.at[dest_slot],
            device_id={"seq": seq_peer(k)}, device_id_type=MESH,
        )

    def give_sum(k, carry):
        sum_copy(k, me).start()
        return carry

    lax.fori_loop(1, n_seq, give_sum, 0)

    def take_sum(k, carry):
        sum_copy(k, seq_peer(k)).wait_recv()
        return carry

    lax.fori_loop(1, n_seq, take_sum, 0)

    total = sums[0]
    top = sums[0]
    for k in range(1, n_seq):
        total = total + sums[k]
        top = jnp.maximum(top, sums[k])
    tops_ref[...] = pltpu.roll(top, HDIM - 2 * NREQ, 1)[:, :heads]
    lane1 = lax.broadcasted_iota(jnp.int32, (1, HDIM), 1)
    entries = jnp.ones((1, HDIM), F32)
    for r in range(NREQ):
        entries = jnp.where(lane1 == r, counts[r].astype(F32) * CH, entries)
    guided_total = pltpu.roll(total, HDIM - NREQ, 1)
    factor = (PHI_MIX * jnp.sqrt(total / entries + 1e-06) + (1.0 - PHI_MIX)) / jnp.sqrt(guided_total / entries + 1e-06)
    factor_row = jnp.zeros((pairs, HDIM), F32)
    for r in range(NREQ):
        one = jnp.sum(jnp.where(lane1 == r, factor, 0.0), axis=1, keepdims=True)
        factor_row = jnp.where(request == r, one, factor_row)
    velocity = guided * jnp.where(image, factor_row, 0.0)
    stepped = latent_s[...] + delta * velocity
    for value, out in ((velocity, vel_ref), (stepped, next_ref)):
        value = jnp.where(group == 0, value, pltpu.roll(value, CH, 1))
        out[:, :HDIM] = value[:HDIM].T[:CH]
        out[:, HDIM:] = jnp.concatenate([value[HDIM:], value[HDIM:]], axis=0).T[:CH, : pairs - HDIM]

    def drain_tp(k, carry):
        res_copy(k, col).wait_send()
        for h in range(heads):
            att_copy(h, k, col).wait_send()
        return carry

    lax.fori_loop(1, n_tp, drain_tp, 0)

    def drain_flow(k, carry):
        flow_copy(k, group, col).wait_send()
        return carry

    lax.fori_loop(1, n_tp * n_cfg, drain_flow, 0)

    def drain_sum(k, carry):
        sum_copy(k, me).wait_send()
        return carry

    lax.fori_loop(1, n_seq, drain_sum, 0)

    def drain(h, carry):
        for d in range(1, reach):
            go_right(d, h, kv.at[h]).wait_send()
            go_left(d, h, kv.at[h]).wait_send()
        at_rim(lambda at: rim_right(h, at).wait_send(), lambda at: rim_left(h, at).wait_send())
        for dz in range(1 - reach, reach):
            share(dz, h, kv.at[h]).wait_send()
        share(give, h, kv.at[h]).wait_send()
        return carry

    lax.fori_loop(0, heads, drain, 0)
    for copy in w_out:
        copy.wait_send()
    for n in range(9):
        w_share(n).wait_send()
    for j in range(half // chunk):
        y_copy(j).wait_send()


def local(stream, qkv, q_gain, k_gain, w_out, mod, w_proj, latent, guidance, img_counts, img_widths, step_index):
    rows, width = stream.shape[1], stream.shape[2]
    feats = w_out.shape[1]
    heads = width // HDIM
    n_seq, n_tp, n_cfg = lax.axis_size("seq"), lax.axis_size("tp"), lax.axis_size("cfg")
    piece = rows // n_tp
    img_most = (rows * n_seq - NREQ * TXT) // 4
    longest = TXT + img_most
    reach = ((longest + rows - 2) // rows + 1) // 2
    rim = min(rows, -(-(longest - (2 * reach - 1) * rows - 1) // HDIM) * HDIM)
    vmem = pl.BlockSpec(memory_space=pltpu.VMEM)
    hbm = pl.BlockSpec(memory_space=pltpu.HBM)
    dma = pltpu.SemaphoreType.DMA
    pairs = rows // 2
    half = feats // 2
    chunk = 512
    vel, nxt, tops = pl.pallas_call(
        functools.partial(kernel, rim),
        out_shape=(
            jax.ShapeDtypeStruct((CH, pairs), F32),
            jax.ShapeDtypeStruct((CH, pairs), F32),
            jax.ShapeDtypeStruct((1, heads), F32),
        ),
        in_specs=[hbm] * 13,
        out_specs=(vmem,) * 3,
        scratch_shapes=[
            pltpu.SMEM((NREQ,), jnp.int32),
            pltpu.SMEM((NREQ,), jnp.int32),
            pltpu.SMEM((NREQ,), jnp.int32),
            pltpu.SMEM((NREQ,), F32),
            pltpu.VMEM((pairs, HDIM), F32),
            pltpu.VMEM((1, HDIM), F32),
            pltpu.VMEM((1, HDIM), F32),
            pltpu.VMEM((1, HDIM), F32),
            pltpu.VMEM((2, rows, width), BF16),
            pltpu.VMEM((heads, rows, HDIM), BF16),
            pltpu.VMEM((heads, 2, rows, HDIM), BF16),
            pltpu.VMEM((rows, HDIM), jnp.int32),
            pltpu.VMEM((n_seq, rows), jnp.int32),
            pltpu.VMEM((2 * reach + 1, 2, heads, 2, rows, HDIM), BF16),
            pltpu.VMEM((heads, rows, HDIM), F32),
            pltpu.VMEM((heads, rows, HDIM), F32),
            pltpu.VMEM((heads, rows, HDIM), F32),
            pltpu.VMEM((n_tp, rows, half), BF16),
            pltpu.VMEM((heads, rows, HDIM), BF16),
            pltpu.VMEM((heads, n_tp, 2 * piece, HDIM), BF16),
            pltpu.VMEM((2 * piece, half), F32),
            pltpu.VMEM((half // chunk, piece, chunk), BF16),
            pltpu.VMEM((half // chunk, piece, chunk), BF16),
            pltpu.VMEM((n_tp, piece, width), BF16),
            pltpu.VMEM((3, NREQ, feats), F32),
            pltpu.VMEM((HDIM, feats), BF16),
            pltpu.VMEM((piece, feats), F32),
            pltpu.VMEM((piece, feats), F32),
            pltpu.VMEM((piece, feats), F32),
            pltpu.VMEM((piece, feats), F32),
            pltpu.VMEM((piece, HDIM), F32),
            pltpu.VMEM((piece // 2, HDIM), F32),
            pltpu.VMEM((n_cfg, n_tp, piece // 2, HDIM), F32),
            pltpu.VMEM((1, HDIM), F32),
            pltpu.VMEM((n_seq, 1, HDIM), F32),
            dma((8,)),
            dma((6 + heads,)),
            dma((reach, heads)),
            dma((reach, heads)),
            dma((2 * reach + 1, heads)),
            dma((2 * reach + 1, 2, heads)),
            dma((9,)),
            dma((9,)),
            dma((9,)),
            dma((9,)),
            dma((heads, n_tp)),
            dma((heads, n_tp)),
            dma((half // chunk,)),
            dma((half // chunk,)),
            dma((n_tp,)),
            dma((n_tp,)),
            dma((n_tp * n_cfg,)),
            dma((n_cfg, n_tp)),
            dma((n_seq,)),
            dma((n_seq,)),
        ],
        compiler_params=pltpu.CompilerParams(collective_id=0, has_side_effects=True, vmem_limit_bytes=38 << 20),
        name="flow_step",
    )(*(pltpu.with_memory_space_constraint(x, pltpu.HBM) for x in (
        img_counts, img_widths, step_index, guidance, jnp.transpose(qkv[0], (1, 0, 2)), w_out, stream[0],
        jnp.transpose(mod[0], (1, 0, 2)), w_proj, latent, jnp.asarray(frequency_row()),
        q_gain.reshape(1, HDIM), k_gain.reshape(1, HDIM),
    )))
    return (vel.T, nxt.T, tops)


def solution(mesh):
    placed = (
        P("cfg", "seq", "tp"),
        P("cfg", "seq", None, "tp"),
        P(),
        P(),
        P("tp", None),
        P("cfg", None, None, None),
        P(),
        P("seq", None),
        P(),
        P(),
        P(),
        P(),
    )
    return jax.shard_map(
        local,
        mesh=mesh,
        in_specs=placed,
        out_specs=(P("seq", "cfg"), P("seq", "cfg"), P("cfg", "tp")),
        check_vma=False,
    )
```

```python
import functools
import math

import jax
import jax.numpy as jnp
import numpy as np
from jax import lax
from jax.experimental import pallas as pl
from jax.experimental.pallas import tpu as pltpu
from jax.sharding import PartitionSpec as P

MESH = pl.DeviceIdType.MESH
HDIM = 128
CH = 64
TXT = 128
STEPS = 8
NREQ = 8
PHI_MIX = 0.7
NEG = -1e30
SCALE = 1.0 / math.sqrt(float(HDIM))
EXP2_SCALE = SCALE * math.log2(math.e)
F32 = jnp.float32
BF16 = jnp.bfloat16


def frequency_row():
    pair_index = np.arange(64)
    axis_of = np.where(pair_index < 8, 0, np.where(pair_index < 36, 1, 2))
    axis_start = np.array([0, 8, 36])[axis_of]
    axis_width = np.array([16.0, 56.0, 56.0])[axis_of]
    frequency = 10000.0 ** (-2.0 * (pair_index - axis_start) / axis_width)
    return np.repeat(frequency, 2).astype(np.float32)[None, :]


def request_ends(counts):
    ends = []
    end = jnp.int32(0)
    for r in range(NREQ):
        end = end + (TXT + counts[r])
        ends.append(end)
    return ends


def pick(rows, ends, values):
    out = jnp.full(rows.shape, values[0])
    for r in range(NREQ - 1):
        out = jnp.where(rows >= ends[r], values[r + 1], out)
    return out


def kernel(
    rim,
    counts_ref, widths_ref, steps_ref, guidance_ref, qkv_ref, w_ref, stream_ref, mod_ref, proj_ref, latent_ref,
    freq_ref, qg_ref, kg_ref,
    vel_ref, next_ref, tops_ref,
    counts, widths, steps, guidance, latent_s, freq_s, qg_s, kg_s, qkv, q_s, kv, reqq, reqk, win, m_s, l_s, acc_s,
    wall, att_s, attx, made, yout, ygot,
    res, mod_s, proj_s, mixed, gate, scale, shift, flow_s, mine, flows, row_s, sums,
    first_sem, load_sem, right_sem, left_sem, share_sem, recv_sem, wsend, wrecv, wshare, wpartner,
    att_send, att_recv, y_send, y_recv, res_send, res_recv, flow_send, flow_recv, sum_send, sum_recv,
):
    n_tp, n_seq, n_cfg = lax.axis_size("tp"), lax.axis_size("seq"), lax.axis_size("cfg")
    group, me, col = lax.axis_index("cfg"), lax.axis_index("seq"), lax.axis_index("tp")
    heads, rows = q_s.shape[0], q_s.shape[1]
    width = heads * HDIM
    feats = w_ref.shape[1]
    half = feats // 2
    piece = rows // n_tp
    quarter = 2 * piece
    reach = win.shape[0] // 2
    chips = n_seq // 2
    chip, core = me // 2, me % 2
    other = 1 - core
    right = ((chip + 1) % chips) * 2 + core
    left = ((chip + chips - 1) % chips) * 2 + core
    partner = chip * 2 + other
    n_x = n_tp // 2
    tx, ty = col // 2, col % 2
    tiles = rows // HDIM
    barrier = pltpu.get_barrier_semaphore()

    def tp_peer(k):
        return (col + k) % n_tp

    def far_first(t, count):
        return count // 2 + (t + 1) // 2 * (1 - 2 * (t % 2))

    def plane_peer(k):
        return (group + k // n_tp) % n_cfg, (col + k) % n_tp

    def seq_peer(k):
        return (me + k) % n_seq

    def hail_plane(k, carry):
        g, c = plane_peer(k)
        pl.semaphore_signal(barrier, inc=1, device_id={"cfg": g, "tp": c}, device_id_type=MESH)
        return carry

    near_count = 4 * reach + 1

    def hail_seq(k, carry):
        peer = (2 * chip + 2 * n_seq - 2 * reach + k) % n_seq

        @pl.when(peer != me)
        def _():
            pl.semaphore_signal(barrier, inc=1, device_id={"seq": peer}, device_id_type=MESH)

        return carry

    lax.fori_loop(0, near_count + 1, hail_seq, 0)
    lax.fori_loop(1, n_tp * n_cfg, hail_plane, 0)

    def remote(src, dst, send, recv, axis, peer):
        return pltpu.make_async_remote_copy(
            src_ref=src, dst_ref=dst, send_sem=send, recv_sem=recv,
            device_id={axis: peer}, device_id_type=MESH,
        )

    firsts = [
        pltpu.make_async_copy(source, target, first_sem.at[n])
        for n, (source, target) in enumerate(
            (
                (counts_ref, counts), (widths_ref, widths), (steps_ref, steps), (guidance_ref, guidance),
                (freq_ref, freq_s), (qg_ref, qg_s), (kg_ref, kg_s), (latent_ref, latent_s),
            )
        )
    ]
    for copy in firsts:
        copy.start()
    loads = [
        pltpu.make_async_copy(qkv_ref.at[1], qkv.at[1], load_sem.at[0]),
        pltpu.make_async_copy(qkv_ref.at[0], qkv.at[0], load_sem.at[1]),
        pltpu.make_async_copy(mod_ref, mod_s, load_sem.at[2]),
        pltpu.make_async_copy(proj_ref, proj_s.at[pl.ds(0, CH)], load_sem.at[3]),
        pltpu.make_async_copy(stream_ref.at[pl.ds(pl.multiple_of(col * piece, piece), piece)], res.at[col], load_sem.at[4]),
    ]
    for copy in loads:
        copy.start()
    values = [
        pltpu.make_async_copy(qkv_ref.at[2, :, pl.ds(h * HDIM, HDIM)], kv.at[h, 1], load_sem.at[5 + h]) for h in range(heads)
    ]
    for copy in values:
        copy.start()
    my_cols = pl.ds(pl.multiple_of(ty * half, half), half)
    near_cols = pl.ds(pl.multiple_of((1 - ty) * half, half), half)
    own_w = pltpu.make_async_copy(w_ref.at[:, my_cols], wall.at[col], load_sem.at[5 + heads])
    own_w.start()

    for copy in firsts:
        copy.wait()
    ends = request_ends(counts)
    starts = [jnp.int32(0)] + ends[:-1]
    ids = [jnp.int32(r) for r in range(NREQ)]
    row = me * rows + lax.broadcasted_iota(jnp.int32, (rows, HDIM), 0)
    start = pick(row, ends, starts)
    span = pick(row, ends, [widths[r].astype(F32) for r in range(NREQ)])
    pos = jnp.maximum(row - start - TXT, 0).astype(F32)
    height_id = jnp.floor((pos + 0.5) / span)
    width_id = pos - height_id * span
    lane = lax.broadcasted_iota(jnp.int32, (rows, HDIM), 1)
    angle = jnp.where(lane < 16, 0.0, jnp.where(lane < 72, height_id, width_id)) * freq_s[...]
    even = lane % 2 == 0
    cos = jnp.cos(angle)
    sin = jnp.sin(angle)
    sin = jnp.where(even, -sin, sin)

    def rotated(part, h, gain):
        x = qkv[part, :, h * HDIM : (h + 1) * HDIM].astype(F32)
        x = x * lax.rsqrt(jnp.mean(x * x, axis=-1, keepdims=True) + 1e-06) * gain
        mate = jnp.where(even, pltpu.roll(x, HDIM - 1, 1), pltpu.roll(x, 1, 1))
        return x * cos + mate * sin

    def make_key(h):
        key = rotated(1, h, kg_s[...])
        for b in range(tiles):
            at = slice(b * HDIM, (b + 1) * HDIM)
            kv[h, 0, at, :] = key[at].T.astype(BF16)

    loads[0].wait()
    make_key(0)
    for copy in values:
        copy.wait()

    def slot(dz, p, h):
        return win.at[dz + reach, p, h]

    def go_right(d, h, src):
        return remote(src, slot(-d, core, h), right_sem.at[d - 1, h], recv_sem.at[reach - d, core, h], "seq", right)

    def go_left(d, h, src):
        return remote(src, slot(d, core, h), left_sem.at[d - 1, h], recv_sem.at[reach + d, core, h], "seq", left)

    def share(dz, h, src):
        return remote(src, slot(dz, core, h), share_sem.at[dz + reach, h], recv_sem.at[dz + reach, core, h], "seq", partner)

    def landed(dz, p, h):
        remote(slot(dz, p, h), slot(dz, p, h), share_sem.at[0, 0], recv_sem.at[dz + reach, p, h], "seq", partner).wait_recv()

    cut = rows - rim
    whole, early, late = pl.ds(0, rows), pl.ds(0, rim), pl.ds(cut, rim)

    def rim_right(h, at):
        return remote(
            slot(1 - reach, core, h).at[:, at], slot(-reach, core, h).at[:, at],
            right_sem.at[reach - 1, h], recv_sem.at[0, core, h], "seq", right,
        )

    def rim_left(h, at):
        return remote(
            slot(reach - 1, core, h).at[:, at], slot(reach, core, h).at[:, at],
            left_sem.at[reach - 1, h], recv_sem.at[2 * reach, core, h], "seq", left,
        )

    def at_rim(right_op, left_op):
        @pl.when(core == 0)
        def _():
            right_op(late)
            left_op(whole)

        @pl.when(core == 1)
        def _():
            right_op(whole)
            left_op(early)

    def set_out(h):
        go_right(1, h, kv.at[h]).start()
        go_left(1, h, kv.at[h]).start()
        share(0, h, kv.at[h]).start()

    pl.semaphore_wait(barrier, n_tp * n_cfg - 1 + near_count)
    set_out(0)
    make_key(1)
    set_out(1)
    make_key(2)
    set_out(2)

    x_next = ((tx + 1) % n_x) * 2 + ty
    x_prev = ((tx + n_x - 1) % n_x) * 2 + ty
    y_peer = tx * 2 + 1 - ty
    far_x = ((tx + 2) % n_x) * 2
    core_rows = pl.ds(pl.multiple_of(core * 2 * quarter, 2 * quarter), 2 * quarter)
    low_rows = pl.ds(pl.multiple_of(core * 2 * quarter, quarter), quarter)
    high_rows = pl.ds(pl.multiple_of(core * 2 * quarter + quarter, quarter), quarter)
    mate_rows = pl.ds(pl.multiple_of(other * 2 * quarter, 2 * quarter), 2 * quarter)
    mate_low = pl.ds(pl.multiple_of(other * 2 * quarter, quarter), quarter)
    mate_high = pl.ds(pl.multiple_of(other * 2 * quarter + quarter, quarter), quarter)

    def w_at(source, part):
        return wall.at[source, part]

    prev_own, prev_near = x_prev, (x_prev // 2) * 2 + 1 - ty
    next_own, next_near = x_next, (x_next // 2) * 2 + 1 - ty
    far_own, far_near = far_x + ty, far_x + 1 - ty
    pieces = [
        (y_peer, core_rows, mate_rows),
        (prev_own, core_rows, mate_rows),
        (prev_near, core_rows, mate_rows),
        (next_own, core_rows, mate_rows),
        (next_near, core_rows, mate_rows),
        (far_own, low_rows, mate_low),
        (far_near, low_rows, mate_low),
        (far_own, high_rows, mate_high),
        (far_near, high_rows, mate_high),
    ]

    def w_sends():
        own = w_ref.at[core_rows, my_cols]
        near = w_at(y_peer, core_rows)
        return [
            remote(w_ref.at[core_rows, near_cols], w_at(col, core_rows), wsend.at[0], wrecv.at[0], "tp", y_peer),
            remote(own, w_at(col, core_rows), wsend.at[1], wrecv.at[1], "tp", x_next),
            remote(own, w_at(col, core_rows), wsend.at[3], wrecv.at[3], "tp", x_prev),
            remote(near, near, wsend.at[2], wrecv.at[2], "tp", x_next),
            remote(near, near, wsend.at[4], wrecv.at[4], "tp", x_prev),
            remote(w_at(prev_own, low_rows), w_at(prev_own, low_rows), wsend.at[5], wrecv.at[5], "tp", x_next),
            remote(w_at(next_own, high_rows), w_at(next_own, high_rows), wsend.at[7], wrecv.at[7], "tp", x_prev),
            remote(w_at(prev_near, low_rows), w_at(prev_near, low_rows), wsend.at[6], wrecv.at[6], "tp", x_next),
            remote(w_at(next_near, high_rows), w_at(next_near, high_rows), wsend.at[8], wrecv.at[8], "tp", x_prev),
        ]

    w_out = w_sends()

    def w_share(n):
        source, part, _ = pieces[n]
        return remote(w_at(source, part), w_at(source, part), wshare.at[n], wpartner.at[n], "seq", partner)

    def w_landed(n):
        source, part, _ = pieces[n]
        remote(w_at(source, part), w_at(source, part), wshare.at[n], wrecv.at[n], "tp", y_peer).wait_recv()

    def w_shared(n):
        source, _, part = pieces[n]
        remote(w_at(source, part), w_at(source, part), wshare.at[n], wpartner.at[n], "seq", partner).wait_recv()

    for n in (0, 1, 2):
        w_out[n].start()

    def res_copy(k, dest_slot):
        c = tp_peer(k)
        return remote(
            stream_ref.at[pl.ds(pl.multiple_of(c * piece, piece), piece)], res.at[dest_slot],
            res_send.at[k], res_recv.at[dest_slot], "tp", c,
        )

    def give_res(k, carry):
        res_copy(k, col).start()
        return carry

    lax.fori_loop(1, n_tp, give_res, 0)

    loads[1].wait()
    for h in range(heads):
        q_s[h] = rotated(0, h, qg_s[...]).astype(BF16)
    reqq[...] = pick(row, ends, ids)
    every = lax.broadcasted_iota(jnp.int32, (n_seq, rows), 0) * rows + lax.broadcasted_iota(jnp.int32, (n_seq, rows), 1)
    reqk[...] = pick(every, ends, ids)

    def wide(x):
        return jnp.concatenate([x] * tiles, axis=1)

    def update(h, blocks):
        q = q_s[h]
        asked = wide(reqq[...])
        scores = []
        for ref, source in blocks:
            keys = jnp.concatenate([ref[0, b * HDIM : (b + 1) * HDIM, :] for b in range(tiles)], axis=1)
            s = jnp.dot(q, keys, preferred_element_type=F32)
            scores.append(jnp.where(asked == reqk[pl.ds(source, 1), :], s, NEG))
        best = functools.reduce(jnp.maximum, scores)
        m_old = m_s[h]
        m_new = jnp.maximum(m_old, jnp.max(best, axis=1, keepdims=True))
        shrink = jnp.exp2((m_old - m_new) * EXP2_SCALE)
        m_wide = wide(m_new)
        total = None
        acc = acc_s[h] * shrink
        for (ref, source), s in zip(blocks, scores):
            p = jnp.exp2((s - m_wide) * EXP2_SCALE)
            total = p if total is None else total + p
            acc = acc + jnp.dot(p.astype(BF16), ref[1], preferred_element_type=F32)
        l_s[h] = l_s[h] * shrink + jnp.sum(total, axis=1, keepdims=True)
        acc_s[h] = acc
        m_s[h] = m_new

    def block_of(dz, p):
        return ((chip + dz + chips) % chips) * 2 + p

    def own(h, carry):
        blank = jnp.zeros((2, cut, HDIM), BF16)

        @pl.when(core == 0)
        def _():
            win[0, 0, h, :, pl.ds(0, cut), :] = blank

        @pl.when(core == 1)
        def _():
            win[2 * reach, 1, h, :, pl.ds(rim, cut), :] = blank

        m_s[h] = jnp.full((rows, HDIM), NEG, F32)
        l_s[h] = jnp.zeros((rows, HDIM), F32)
        acc_s[h] = jnp.zeros((rows, HDIM), F32)
        update(h, [(kv.at[h], me)])
        return carry

    lax.fori_loop(0, heads, own, 0)

    loads[2].wait()
    chunk = 512
    token = me * rows + col * piece + lax.broadcasted_iota(jnp.int32, (piece, chunk), 0)

    def pick_rows(j, carry):
        at = pl.ds(pl.multiple_of(j * chunk, chunk), chunk)
        for which, out in ((0, gate), (1, scale), (2, shift)):
            value = jnp.broadcast_to(mod_s[which, 0:1, at], (piece, chunk))
            for r in range(NREQ - 1):
                value = jnp.where(token >= ends[r], mod_s[which, r + 1 : r + 2, at], value)
            out[:, at] = value
        return carry

    lax.fori_loop(0, feats // chunk, pick_rows, 0)

    give = reach - 2 * reach * core
    take = -give

    def pair(d, p, h):
        return [(slot(-d, p, h), block_of(-d, p)), (slot(d, p, h), block_of(d, p))]

    def att_copy(h, k, dest_slot):
        c = tp_peer(k)
        return remote(
            att_s.at[h, pl.ds(pl.multiple_of((c // 2) * quarter, quarter), quarter)], attx.at[h, dest_slot],
            att_send.at[h, k], att_recv.at[h, dest_slot], "tp", c,
        )

    def give_att(h):
        att_s[h] = (acc_s[h] / l_s[h]).astype(BF16)

        def one(t, carry):
            att_copy(h, far_first(t, n_tp), col).start()
            return carry

        lax.fori_loop(0, n_tp - 1, one, 0)
        attx[h, col] = att_s[h, pl.ds(pl.multiple_of(tx * quarter, quarter), quarter), :]

    def take_att(h):
        def one(k, carry):
            att_copy(h, k, tp_peer(k)).wait_recv()
            return carry

        lax.fori_loop(1, n_tp, one, 0)

    def product(h, at):
        left_side = jnp.concatenate([attx[h, k] for k in range(n_tp)], axis=1)
        weights = wall[:, h * HDIM : (h + 1) * HDIM, at].reshape(n_tp * HDIM, chunk)
        return jnp.dot(left_side, weights, preferred_element_type=F32)

    def from_partner(d, h):
        landed(-d, other, h)
        landed(d, other, h)
        update(h, pair(d, other, h))

    def one_from_partner(dz, h):
        landed(dz, other, h)
        update(h, [(slot(dz, other, h), block_of(dz, other))])

    def step(i, carry):
        d, h = 1 + i // heads, i % heads
        d_last, h_last = 1 + (i + heads - 1) // heads - 1, (i + heads - 1) % heads

        @pl.when(i == 3)
        def _():
            w_landed(0)
            w_out[3].start()
            w_out[4].start()
            w_landed(1)
            w_out[5].start()
            w_landed(3)
            w_out[6].start()
            for n in (0, 1, 3):
                w_share(n).start()

        @pl.when(i == 7)
        def _():
            w_landed(2)
            w_out[7].start()
            w_landed(4)
            w_out[8].start()
            for n in (2, 4):
                w_share(n).start()

        @pl.when(i == 9)
        def _():
            for n in (5, 7):
                w_landed(n)
                w_share(n).start()

        @pl.when(i == heads * (reach - 1))
        def _():
            from_partner(d_last, h_last)

        for done in range(heads - 1):

            @pl.when(i == heads * (reach - 1) + done + 1)
            def _():
                one_from_partner(take, done)
                give_att(done)
                if done == 0:
                    for n in (6, 8):
                        w_landed(n)
                        w_share(n).start()

        @pl.when(d < reach - 1)
        def _():
            landed(-d, core, h)
            go_right(d + 1, h, slot(-d, core, h)).start()
            landed(d, core, h)
            go_left(d + 1, h, slot(d, core, h)).start()

        @pl.when(d == reach - 1)
        def _():
            landed(-d, core, h)
            landed(d, core, h)
            at_rim(lambda at: rim_right(h, at).start(), lambda at: rim_left(h, at).start())

        @pl.when(d < reach)
        def _():
            share(-d, h, slot(-d, core, h)).start()
            share(d, h, slot(d, core, h)).start()

        @pl.when(d == reach)
        def _():
            at_rim(lambda at: rim_right(h, at).wait_recv(), lambda at: rim_left(h, at).wait_recv())
            share(give, h, slot(give, core, h)).start()

        update(h, pair(d, core, h))

        @pl.when((i > 0) & (d < reach))
        def _():
            from_partner(d_last, h_last)

        @pl.when((i > 0) & (i < 4))
        def _():
            one_from_partner(0, i - 1)

        return carry

    lax.fori_loop(0, heads * reach, step, 0)

    one_from_partner(take, heads - 1)
    give_att(heads - 1)
    own_w.wait()
    for n in range(9):
        w_shared(n)
    take_att(0)
    take_att(1)

    def early_product(j, carry):
        at = pl.ds(pl.multiple_of(j * chunk, chunk), chunk)
        made[:, at] = product(0, at) + product(1, at)
        return carry

    lax.fori_loop(0, half // chunk, early_product, 0)

    lane8 = lax.broadcasted_iota(jnp.int32, (1, HDIM), 1)
    top_row = jnp.zeros((1, HDIM), F32)
    for h in range(heads):
        top = jnp.max(jnp.max(m_s[h], axis=0, keepdims=True), axis=1, keepdims=True) * SCALE
        top_row = jnp.where(lane8 == 2 * NREQ + h, top, top_row)

    loads[3].wait()
    proj_s[pl.ds(CH, HDIM - CH), :] = jnp.zeros((HDIM - CH, feats), BF16)
    loads[4].wait()

    def take_res(k, carry):
        res_copy(k, tp_peer(k)).wait_recv()
        return carry

    lax.fori_loop(1, n_tp, take_res, 0)
    take_att(2)

    def y_copy(j):
        return remote(yout.at[j], ygot.at[j], y_send.at[j], y_recv.at[j], "tp", y_peer)

    keep = pl.ds(pl.multiple_of(ty * piece, piece), piece)
    pass_on = pl.ds(pl.multiple_of((1 - ty) * piece, piece), piece)

    def last_product(j, carry):
        at = pl.ds(pl.multiple_of(j * chunk, chunk), chunk)
        made[:, at] = made[:, at] + product(2, at)
        yout[j] = made[pass_on, at].astype(BF16)
        y_copy(j).start()
        return carry

    lax.fori_loop(0, half // chunk, last_product, 0)

    total1 = jnp.zeros((piece, 1), F32)
    for j in range(half // width):
        at = pl.ds(pl.multiple_of(ty * half + j * width, width), width)
        value = res[ty * (n_tp // 2) + j].astype(F32) + gate[:, at] * made[keep, j * width : (j + 1) * width]
        mixed[:, at] = value
        total1 = total1 + jnp.sum(value, axis=1, keepdims=True)
    for j in range(half // chunk):
        y_copy(j).wait_recv()
        at = pl.ds(pl.multiple_of((1 - ty) * half + j * chunk, chunk), chunk)
        mixed[:, at] = gate[:, at] * ygot[j].astype(F32)
    for j in range(half // width):
        at = pl.ds(pl.multiple_of((1 - ty) * half + j * width, width), width)
        value = res[(1 - ty) * (n_tp // 2) + j].astype(F32) + mixed[:, at]
        mixed[:, at] = value
        total1 = total1 + jnp.sum(value, axis=1, keepdims=True)
    mean = total1 * (1.0 / feats)
    variance = jnp.zeros((piece, 1), F32)
    for j in range(n_tp):
        at = slice(j * width, (j + 1) * width)
        centred = mixed[:, at] - mean
        mixed[:, at] = centred
        variance = variance + jnp.sum(centred * centred, axis=1, keepdims=True)
    inverse = lax.rsqrt(variance * (1.0 / feats) + 1e-06)
    flow = jnp.zeros((piece, HDIM), F32)
    for j in range(n_tp):
        at = slice(j * width, (j + 1) * width)
        normed = (mixed[:, at] * inverse * (1.0 + scale[:, at]) + shift[:, at]).astype(BF16)
        flow = flow + lax.dot_general(
            normed, proj_s[:, at], (((1,), (1,)), ((), ())), preferred_element_type=F32
        )
    flow_s[...] = flow
    even_rows = flow_s[pl.ds(0, piece // 2, stride=2), :]
    odd_rows = flow_s[pl.ds(1, piece // 2, stride=2), :]
    own_flow = even_rows + pltpu.roll(odd_rows, CH, 1)
    mine[...] = own_flow
    flows[group, col] = own_flow
    def flow_copy(k, g_slot, c_slot):
        g, c = plane_peer(k)
        return pltpu.make_async_remote_copy(
            src_ref=mine, dst_ref=flows.at[g_slot, c_slot],
            send_sem=flow_send.at[k], recv_sem=flow_recv.at[g_slot, c_slot],
            device_id={"cfg": g, "tp": c}, device_id_type=MESH,
        )

    def give_flow(t, carry):
        k = (1 - t % 2) * n_tp + far_first(t // 2, n_tp)
        flow_copy(k, group, col).start()
        return carry

    lax.fori_loop(0, n_tp * n_cfg - 1, give_flow, 0)

    pairs = rows // 2
    lane2 = lax.broadcasted_iota(jnp.int32, (pairs, HDIM), 1)
    row2 = me * rows + 2 * lax.broadcasted_iota(jnp.int32, (pairs, HDIM), 0) + (lane2 >= CH).astype(jnp.int32)
    request = pick(row2, ends, [jnp.int32(r) for r in range(NREQ)])
    image = (row2 - pick(row2, ends, [jnp.int32(0)] + ends[:-1])) >= TXT
    guide = pick(row2, ends, [guidance[r] for r in range(NREQ)])
    at_step = pick(row2, ends, [steps[r].astype(F32) for r in range(NREQ)])

    def sigma(u):
        remaining = 1.0 - u / STEPS
        return 3.0 * remaining / (1.0 + 2.0 * remaining)

    delta = sigma(at_step + 1.0) - sigma(at_step)

    def take_flow(k, carry):
        g, c = plane_peer(k)
        flow_copy(k, g, c).wait_recv()
        return carry

    lax.fori_loop(1, n_tp * n_cfg, take_flow, 0)

    cond = flows[0].reshape(pairs, HDIM)
    uncond = flows[1].reshape(pairs, HDIM)
    guided = uncond + guide * (cond - uncond)
    cond_square = jnp.where(image, cond * cond, 0.0)
    guided_square = jnp.where(image, guided * guided, 0.0)
    parts = []
    for square in (cond_square, guided_square):
        for r in range(NREQ):
            parts.append(jnp.sum(jnp.where(request == r, square, 0.0), axis=0, keepdims=True))
    stacked = jnp.sum(jnp.concatenate(parts, axis=0), axis=1, keepdims=True)
    diagonal = lax.broadcasted_iota(jnp.int32, (2 * NREQ, HDIM), 0) == lax.broadcasted_iota(jnp.int32, (2 * NREQ, HDIM), 1)
    own_sums = jnp.sum(jnp.where(diagonal, stacked, 0.0), axis=0, keepdims=True) + top_row
    row_s[...] = own_sums
    sums[me] = own_sums

    def sum_copy(k, dest_slot):
        return pltpu.make_async_remote_copy(
            src_ref=row_s, dst_ref=sums.at[dest_slot],
            send_sem=sum_send.at[k], recv_sem=sum_recv.at[dest_slot],
            device_id={"seq": seq_peer(k)}, device_id_type=MESH,
        )

    def give_sum(t, carry):
        sum_copy(far_first(t, n_seq), me).start()
        return carry

    lax.fori_loop(0, n_seq - 1, give_sum, 0)

    def take_sum(k, carry):
        sum_copy(k, seq_peer(k)).wait_recv()
        return carry

    lax.fori_loop(1, n_seq, take_sum, 0)

    total = sums[0]
    top = sums[0]
    for k in range(1, n_seq):
        total = total + sums[k]
        top = jnp.maximum(top, sums[k])
    tops_ref[...] = pltpu.roll(top, HDIM - 2 * NREQ, 1)[:, :heads]
    lane1 = lax.broadcasted_iota(jnp.int32, (1, HDIM), 1)
    entries = jnp.ones((1, HDIM), F32)
    for r in range(NREQ):
        entries = jnp.where(lane1 == r, counts[r].astype(F32) * CH, entries)
    guided_total = pltpu.roll(total, HDIM - NREQ, 1)
    factor = (PHI_MIX * jnp.sqrt(total / entries + 1e-06) + (1.0 - PHI_MIX)) / jnp.sqrt(guided_total / entries + 1e-06)
    factor_row = jnp.zeros((pairs, HDIM), F32)
    for r in range(NREQ):
        one = jnp.sum(jnp.where(lane1 == r, factor, 0.0), axis=1, keepdims=True)
        factor_row = jnp.where(request == r, one, factor_row)
    velocity = guided * jnp.where(image, factor_row, 0.0)
    stepped = latent_s[...] + delta * velocity
    for value, out in ((velocity, vel_ref), (stepped, next_ref)):
        value = jnp.where(group == 0, value, pltpu.roll(value, CH, 1))
        out[:, :HDIM] = value[:HDIM].T[:CH]
        out[:, HDIM:] = jnp.concatenate([value[HDIM:], value[HDIM:]], axis=0).T[:CH, : pairs - HDIM]

    def drain_tp(k, carry):
        res_copy(k, col).wait_send()
        for h in range(heads):
            att_copy(h, k, col).wait_send()
        return carry

    lax.fori_loop(1, n_tp, drain_tp, 0)

    def drain_flow(k, carry):
        flow_copy(k, group, col).wait_send()
        return carry

    lax.fori_loop(1, n_tp * n_cfg, drain_flow, 0)

    def drain_sum(k, carry):
        sum_copy(k, me).wait_send()
        return carry

    lax.fori_loop(1, n_seq, drain_sum, 0)

    def drain(h, carry):
        for d in range(1, reach):
            go_right(d, h, kv.at[h]).wait_send()
            go_left(d, h, kv.at[h]).wait_send()
        at_rim(lambda at: rim_right(h, at).wait_send(), lambda at: rim_left(h, at).wait_send())
        for dz in range(1 - reach, reach):
            share(dz, h, kv.at[h]).wait_send()
        share(give, h, kv.at[h]).wait_send()
        return carry

    lax.fori_loop(0, heads, drain, 0)
    for copy in w_out:
        copy.wait_send()
    for n in range(9):
        w_share(n).wait_send()
    for j in range(half // chunk):
        y_copy(j).wait_send()


def local(stream, qkv, q_gain, k_gain, w_out, mod, w_proj, latent, guidance, img_counts, img_widths, step_index):
    rows, width = stream.shape[1], stream.shape[2]
    feats = w_out.shape[1]
    heads = width // HDIM
    n_seq, n_tp, n_cfg = lax.axis_size("seq"), lax.axis_size("tp"), lax.axis_size("cfg")
    piece = rows // n_tp
    img_most = (rows * n_seq - NREQ * TXT) // 4
    longest = TXT + img_most
    reach = ((longest + rows - 2) // rows + 1) // 2
    rim = min(rows, -(-(longest - (2 * reach - 1) * rows - 1) // HDIM) * HDIM)
    vmem = pl.BlockSpec(memory_space=pltpu.VMEM)
    hbm = pl.BlockSpec(memory_space=pltpu.HBM)
    dma = pltpu.SemaphoreType.DMA
    pairs = rows // 2
    half = feats // 2
    chunk = 512
    vel, nxt, tops = pl.pallas_call(
        functools.partial(kernel, rim),
        out_shape=(
            jax.ShapeDtypeStruct((CH, pairs), F32),
            jax.ShapeDtypeStruct((CH, pairs), F32),
            jax.ShapeDtypeStruct((1, heads), F32),
        ),
        in_specs=[hbm] * 13,
        out_specs=(vmem,) * 3,
        scratch_shapes=[
            pltpu.SMEM((NREQ,), jnp.int32),
            pltpu.SMEM((NREQ,), jnp.int32),
            pltpu.SMEM((NREQ,), jnp.int32),
            pltpu.SMEM((NREQ,), F32),
            pltpu.VMEM((pairs, HDIM), F32),
            pltpu.VMEM((1, HDIM), F32),
            pltpu.VMEM((1, HDIM), F32),
            pltpu.VMEM((1, HDIM), F32),
            pltpu.VMEM((2, rows, width), BF16),
            pltpu.VMEM((heads, rows, HDIM), BF16),
            pltpu.VMEM((heads, 2, rows, HDIM), BF16),
            pltpu.VMEM((rows, HDIM), jnp.int32),
            pltpu.VMEM((n_seq, rows), jnp.int32),
            pltpu.VMEM((2 * reach + 1, 2, heads, 2, rows, HDIM), BF16),
            pltpu.VMEM((heads, rows, HDIM), F32),
            pltpu.VMEM((heads, rows, HDIM), F32),
            pltpu.VMEM((heads, rows, HDIM), F32),
            pltpu.VMEM((n_tp, rows, half), BF16),
            pltpu.VMEM((heads, rows, HDIM), BF16),
            pltpu.VMEM((heads, n_tp, 2 * piece, HDIM), BF16),
            pltpu.VMEM((2 * piece, half), F32),
            pltpu.VMEM((half // chunk, piece, chunk), BF16),
            pltpu.VMEM((half // chunk, piece, chunk), BF16),
            pltpu.VMEM((n_tp, piece, width), BF16),
            pltpu.VMEM((3, NREQ, feats), F32),
            pltpu.VMEM((HDIM, feats), BF16),
            pltpu.VMEM((piece, feats), F32),
            pltpu.VMEM((piece, feats), F32),
            pltpu.VMEM((piece, feats), F32),
            pltpu.VMEM((piece, feats), F32),
            pltpu.VMEM((piece, HDIM), F32),
            pltpu.VMEM((piece // 2, HDIM), F32),
            pltpu.VMEM((n_cfg, n_tp, piece // 2, HDIM), F32),
            pltpu.VMEM((1, HDIM), F32),
            pltpu.VMEM((n_seq, 1, HDIM), F32),
            dma((8,)),
            dma((6 + heads,)),
            dma((reach, heads)),
            dma((reach, heads)),
            dma((2 * reach + 1, heads)),
            dma((2 * reach + 1, 2, heads)),
            dma((9,)),
            dma((9,)),
            dma((9,)),
            dma((9,)),
            dma((heads, n_tp)),
            dma((heads, n_tp)),
            dma((half // chunk,)),
            dma((half // chunk,)),
            dma((n_tp,)),
            dma((n_tp,)),
            dma((n_tp * n_cfg,)),
            dma((n_cfg, n_tp)),
            dma((n_seq,)),
            dma((n_seq,)),
        ],
        compiler_params=pltpu.CompilerParams(collective_id=0, has_side_effects=True, vmem_limit_bytes=38 << 20),
        name="flow_step",
    )(*(pltpu.with_memory_space_constraint(x, pltpu.HBM) for x in (
        img_counts, img_widths, step_index, guidance, jnp.transpose(qkv[0], (1, 0, 2)), w_out, stream[0],
        jnp.transpose(mod[0], (1, 0, 2)), w_proj, latent, jnp.asarray(frequency_row()),
        q_gain.reshape(1, HDIM), k_gain.reshape(1, HDIM),
    )))
    return (vel.T, nxt.T, tops)


def solution(mesh):
    placed = (
        P("cfg", "seq", "tp"),
        P("cfg", "seq", None, "tp"),
        P(),
        P(),
        P("tp", None),
        P("cfg", None, None, None),
        P(),
        P("seq", None),
        P(),
        P(),
        P(),
        P(),
    )
    return jax.shard_map(
        local,
        mesh=mesh,
        in_specs=placed,
        out_specs=(P("seq", "cfg"), P("seq", "cfg"), P("cfg", "tp")),
        check_vma=False,
    )
```
